32 devices in a mesh: dp: 8 (over z, y), seq: 4 (over x, core).
Axes of the slice: x: 2, y: 2, z: 4, core: 2. Of those that a mesh axis runs over, the one named last changes fastest.
Arguments:
- tokens: bfloat16 [16384, 1024], P(('dp', 'seq')), may hold values from -6 to 6
- attn_gain: bfloat16 [1024], replicated, may hold values from 0.25 to 1.75
- w_query: bfloat16 [1024, 256], replicated, may hold values from -0.1875 to 0.1875
- w_key: bfloat16 [1024, 256], replicated, may hold values from -0.1875 to 0.1875
- w_value: bfloat16 [1024, 1024], replicated, may hold values from -0.1875 to 0.1875
- w_output: bfloat16 [1024, 1024], replicated, may hold values from -0.75 to 0.75
- mlp_gain: bfloat16 [1024], replicated, may hold values from 0.25 to 1.75
- w_gate: bfloat16 [1024, 2752], P(('dp', 'seq')), may hold values from -0.1875 to 0.1875
- w_up: bfloat16 [1024, 2752], P(('dp', 'seq')), may hold values from -0.1875 to 0.1875
- w_down: bfloat16 [1024, 2752], P(('dp', 'seq')), may hold values from -0.109375 to 0.109375
- out_grad: bfloat16 [16384, 1024], P(('dp', 'seq')), may hold values from -6 to 6
Outputs:
- layer_out: bfloat16 [16384, 1024], P(('dp', 'seq'))
- tokens_grad: float32 [16384, 1024], P(('dp', 'seq'))
- attn_gain_grad: float32 [1024], P(('dp', 'seq'))
- w_query_grad: float32 [1024, 256], P(('dp', 'seq'))
- w_key_grad: float32 [1024, 256], P(('dp', 'seq'))
- w_value_grad: float32 [1024, 1024], P(('dp', 'seq'))
- w_output_grad: float32 [1024, 1024], P(('dp', 'seq'))
- mlp_gain_grad: float32 [1024], P(('dp', 'seq'))
- w_gate_grad: float32 [1024, 2752], P(('dp', 'seq'))
- w_up_grad: float32 [1024, 2752], P(('dp', 'seq'))
- w_down_grad: float32 [1024, 2752], P(('dp', 'seq'))
The draws below stay inside these ranges and needn't reach their ends.
All inputs are finite; a program needn't handle non-finite values.
Results may differ from the reference program's by a relative error of at most 0.012.
Values may be sent and summed in bfloat16 or wider, within the bound.
A program may use at most 192 MiB of HBM per device.

```python
import math
import jax
import jax.numpy as jnp
from jax import lax

D = 1024
H = 16
KD = 16
VD = 64
FF = 2752
GROUP = 512
FEAT = 273
HK = 256
HV = 1024
SEQ_LEN = 2048
SEQS = 8
TOKENS = 16384


def steps_of(key, shape, pieces, least, high):
    level = 1.0
    for position, blocks in pieces:
        heights = jax.random.uniform(jax.random.fold_in(jax.random.fold_in(key, 6), position), (blocks,), jnp.float32, least / len(pieces), high / len(pieces))
        level = level * jnp.repeat(jnp.exp(heights), shape[position] // blocks).reshape((-1,) + (1,) * (len(shape) - 1 - position))
    return level


def noise(rng, shape, scale, most, pieces=(), dtype=jnp.bfloat16):
    entries = jax.random.normal(rng, shape, jnp.float32) * scale
    if len(pieces) > 0:
        entries = steps_of(rng, shape, pieces, -0.22, 0.18) * entries
    return jnp.clip(entries, min=-most, max=most).astype(dtype)


def setup_inputs(seed: int = 0) -> dict:
    splits = jax.random.split(jax.random.key(seed), 12)
    return {
        "tokens": noise(splits[0], (TOKENS, D), 1.0, 6.0, ((0, 32),)),
        "attn_gain": jnp.clip(1.0 + 0.15 * jax.random.normal(splits[1], (D,), jnp.float32), 0.25, 1.75).astype(jnp.bfloat16),
        "w_query": noise(splits[2], (D, HK), D ** -0.5, 0.1875),
        "w_key": noise(splits[3], (D, HK), D ** -0.5, 0.1875),
        "w_value": noise(splits[4], (D, HV), D ** -0.5, 0.1875),
        "w_output": noise(splits[5], (HV, D), VD ** -0.5, 0.75),
        "mlp_gain": jnp.clip(1.0 + 0.15 * jax.random.normal(splits[6], (D,), jnp.float32), 0.25, 1.75).astype(jnp.bfloat16),
        "w_gate": noise(splits[7], (D, FF), D ** -0.5, 0.1875, ((0, 32),)),
        "w_up": noise(splits[8], (D, FF), D ** -0.5, 0.1875, ((0, 32),)),
        "w_down": noise(splits[9], (D, FF), FF ** -0.5, 0.109375, ((0, 32),)),
        "out_grad": noise(splits[10], (TOKENS, D), 1.0, 6.0, ((0, 32),)),
    }


epsilon = 1e-05
quad_scale = 1.0 / (4.0 * math.sqrt(2.0))

@jax.custom_vjp
def low(v):
    return lax.optimization_barrier(v.astype(jnp.bfloat16)).astype(jnp.float32)

@jax.custom_vjp
def low_back(v):
    return v

def low_keep(v):
    return (low(v), None)

def low_pass(kept, grad):
    return (grad,)

def back_keep(v):
    return (v, None)

def back_low(kept, grad):
    return (low(grad),)
low.defvjp(low_keep, low_pass)
low_back.defvjp(back_keep, back_low)

def product(left, right):
    return jnp.dot(left, right, precision=lax.Precision.HIGHEST, preferred_element_type=jnp.float32)

def rms_norm(inputs, gain):
    return inputs * lax.rsqrt(lax.optimization_barrier(jnp.mean(inputs * inputs, axis=-1, keepdims=True)) + epsilon) * gain

def features(vectors):
    count = vectors.shape[0]
    square = (vectors[:, :, None] * vectors[:, None, :]).reshape(count, -1) * quad_scale
    return jnp.concatenate([jnp.ones((count, 1), jnp.float32), vectors * 0.5, square], axis=1)

def block_step(carry, block):
    state, total = carry
    queries, keys, values = block
    width = queries.shape[0]
    score = product(queries, keys.T) * 0.25
    weight = 1.0 + score + 0.5 * score * score
    later = lax.broadcasted_iota(jnp.int32, (width, width), 0) >= lax.broadcasted_iota(jnp.int32, (width, width), 1)
    weight = jnp.where(later, weight, 0.0)
    query_feat = low(features(queries))
    key_feat = low(features(keys))
    numer = product(low(weight), values) + product(query_feat, low(state))
    denom = lax.optimization_barrier(jnp.sum(weight, axis=1)) + product(query_feat, total)
    state = state + product(key_feat.T, values)
    total = total + lax.optimization_barrier(jnp.sum(key_feat, axis=0))
    return ((state, total), numer / denom[:, None])

def head_attention(queries, keys, values):
    length = queries.shape[0]
    blocks = length // GROUP
    split = (queries.reshape(blocks, GROUP, -1), keys.reshape(blocks, GROUP, -1), values.reshape(blocks, GROUP, -1))
    start = (jnp.zeros((FEAT, values.shape[1]), jnp.float32), jnp.zeros((FEAT,), jnp.float32))
    final_carry, mixed = lax.scan(jax.checkpoint(block_step), start, split)
    return mixed.reshape(length, -1)
all_heads = jax.vmap(head_attention, in_axes=1, out_axes=1)

def forward(inputs, attn_gain, w_query, w_key, w_value, w_output, mlp_gain, w_gate, w_up, w_down):
    length = inputs.shape[0]
    normed = low(rms_norm(inputs, attn_gain))
    queries = low_back(low(product(normed, w_query))).reshape(length, H, KD)
    keys = low_back(low(product(normed, w_key))).reshape(length, H, KD)
    values = low_back(low(product(normed, w_value))).reshape(length, H, VD)
    mixed = all_heads(queries, keys, values)
    mixed = low_back(low(mixed.reshape(length, HV)))
    middle = inputs + low_back(product(mixed, w_output))
    normed_mlp = low(rms_norm(middle, mlp_gain))
    gate = low_back(product(normed_mlp, w_gate))
    upward = low_back(product(normed_mlp, w_up))
    hidden = low(jax.nn.silu(gate) * upward)
    return middle + low_back(product(hidden, w_down.T))

def reference(tokens, attn_gain, w_query, w_key, w_value, w_output, mlp_gain, w_gate, w_up, w_down, out_grad):
    params = tuple((param.astype(jnp.float32) for param in (attn_gain, w_query, w_key, w_value, w_output, mlp_gain, w_gate, w_up, w_down)))
    inputs = tokens.astype(jnp.float32).reshape(SEQS, SEQ_LEN, D)
    cotangent = out_grad.astype(jnp.float32).reshape(SEQS, SEQ_LEN, D)

    def one_sequence(sums, pair):
        result, backward = jax.vjp(forward, pair[0], *params)
        grads = backward(pair[1])
        sums = tuple((total_in + grad_in for total_in, grad_in in zip(sums, grads[1:])))
        return (sums, (result.astype(jnp.bfloat16), grads[0]))
    zeros = tuple((jnp.zeros_like(param) for param in params))
    sums, (results, input_grads) = lax.scan(one_sequence, zeros, (inputs, cotangent))
    return (results.reshape(TOKENS, D), input_grads.reshape(TOKENS, D), sums[0], sums[1], sums[2], sums[3], sums[4], sums[5], sums[6], sums[7], sums[8])
```

```python
import math

import jax
import jax.numpy as jnp
import numpy as np
from jax import lax
from jax.experimental import pallas as pl
from jax.experimental.pallas import tpu as pltpu
from jax.sharding import PartitionSpec as P

KD = 16
VD = 64
LANES = 128
FEATS = 256
EPS = 1e-05
QUAD = 1.0 / (4.0 * math.sqrt(2.0))
F32 = jnp.float32
BF16 = jnp.bfloat16
VMEM_LIMIT = 58 << 20


def feature_tables():
    pick_a = np.zeros((LANES, FEATS), np.float32)
    pick_b = np.zeros((LANES, FEATS), np.float32)
    rows = np.zeros((8, FEATS), np.float32)
    spot = 0
    for a in range(KD):
        for b in range(a, KD):
            pick_a[a::KD, spot] = 1.0
            pick_b[b::KD, spot] = 1.0
            rows[2, spot] = QUAD
            rows[3, spot] = 1.0 if a == b else 2.0
            spot += 1
    for a in range(KD):
        pick_a[a::KD, spot] = 1.0
        rows[1, spot] = 1.0
        rows[2, spot] = 0.5
        rows[3, spot] = 1.0
        spot += 1
    rows[0:4, spot] = 1.0
    return jnp.asarray(pick_a, BF16), jnp.asarray(pick_b, BF16), jnp.asarray(rows)


def dot(left, right):
    return jnp.dot(left, right, preferred_element_type=F32)


def dot_nt(left, right):
    return lax.dot_general(left, right, (((1,), (1,)), ((), ())), preferred_element_type=F32)


def dot_tn(left, right):
    return lax.dot_general(left, right, (((0,), (0,)), ((), ())), preferred_element_type=F32)


def tile_at(index):
    return pl.ds(pl.multiple_of(index * LANES, LANES), LANES)


def head_lanes(rows, spot):
    return lax.broadcasted_iota(jnp.int32, (rows, LANES), 1) // KD == spot


def half_lanes(rows, half):
    return lax.broadcasted_iota(jnp.int32, (rows, LANES), 1) // VD == half


def halves_of(masked, pick_a, pick_b, rows):
    first = dot(masked, pick_a) + rows[0:1, :]
    second = dot(masked, pick_b) + rows[1:2, :]
    return first, second


def features_of(masked, pick_a, pick_b, rows):
    first, second = halves_of(masked, pick_a, pick_b, rows)
    return (first * second * rows[2:3, :]).astype(BF16)


def only(mask, value):
    return jnp.where(mask, value, jnp.zeros_like(value))


def project_body(tok, gain, wq, wk, wv, normed, query, keys, values):
    x = tok[...].astype(F32)
    scale = lax.rsqrt(jnp.mean(x * x, axis=-1, keepdims=True) + EPS)
    normed[...] = (x * scale * gain[...]).astype(BF16)
    query[...] = dot(normed[...], wq[...]).astype(BF16)
    keys[...] = dot(normed[...], wk[...]).astype(BF16)
    values[...] = dot(normed[...], wv[...]).astype(BF16)


def state_body(keys, values, pick_a, pick_b, rows, state, total):
    pairs = values.shape[1] // LANES
    count = keys.shape[0]

    def step(pair, carry):
        turned = values[:, tile_at(pair)].T
        for half in range(2):
            head = pair * 2 + half
            masked = only(head_lanes(count, head % 8), keys[:, tile_at(head // 8)])
            feat = features_of(masked, pick_a[...], pick_b[...], rows[...])
            sums = dot(turned[half * VD : (half + 1) * VD, :], feat)
            state[head] = (sums * rows[3:4, :]).astype(BF16)
            total[head] = jnp.sum(feat.astype(F32), axis=0, keepdims=True) * rows[3:4, :]
        return carry

    lax.fori_loop(0, pairs, step, 0)


def causal(rows, columns, row_start, column_start):
    row = lax.broadcasted_iota(jnp.int32, (rows, columns), 0) + row_start
    column = lax.broadcasted_iota(jnp.int32, (rows, columns), 1) + column_start
    return row >= column


def attend_body(query, keys, values, pick_a, pick_b, rows, state, total, mixed, inverse, block=256):
    pairs = values.shape[1] // LANES
    count = keys.shape[0]

    def step(pair, carry):
        vals = values[:, tile_at(pair)]
        for start in range(0, count, block):
            stop = start + block
            numer = None
            for half in range(2):
                head = pair * 2 + half
                masked = only(head_lanes(block, head % 8), query[start:stop, tile_at(head // 8)])
                score = dot_nt(masked, keys[0:stop, tile_at(head // 8)]) * 0.25
                weight = 1.0 + score + 0.5 * score * score
                weight = jnp.where(causal(block, stop, start, 0), weight, 0.0)
                feat = features_of(masked, pick_a[...], pick_b[...], rows[...])
                inter = feat.astype(F32) * total[head]
                denom = jnp.sum(weight, axis=1, keepdims=True) + jnp.sum(
                    inter, axis=1, keepdims=True
                )
                across = dot_nt(feat, state[head])
                both = dot(weight.astype(BF16), vals[0:stop, :])
                across = jnp.concatenate([across, across], axis=1)
                whole = (both + across) / denom
                flip = jnp.broadcast_to(1.0 / denom, (block, LANES))
                if half == 0:
                    numer, invs = whole, flip
                else:
                    mask = half_lanes(block, 0)
                    numer = jnp.where(mask, numer, whole)
                    invs = jnp.where(mask, invs, flip)
            mixed[start:stop, tile_at(pair)] = numer.astype(BF16)
            inverse[start:stop, tile_at(pair)] = invs
        return carry

    lax.fori_loop(0, pairs, step, 0)


def back_state_body(query, mixed, inverse, d_mixed, pick_a, pick_b, rows, d_state, d_total):
    pairs = mixed.shape[1] // LANES
    count = query.shape[0]

    def step(pair, carry):
        spot = tile_at(pair)
        d_numer = d_mixed[:, spot].astype(F32) * inverse[:, spot]
        lost = d_numer * mixed[:, spot].astype(F32)
        turned = d_numer.astype(BF16).T
        for half in range(2):
            head = pair * 2 + half
            masked = only(head_lanes(count, head % 8), query[:, tile_at(head // 8)])
            feat = features_of(masked, pick_a[...], pick_b[...], rows[...])
            d_denom = -jnp.sum(only(half_lanes(count, half), lost), axis=1, keepdims=True)
            sums = dot(turned[half * VD : (half + 1) * VD, :], feat)
            d_state[head] = (sums * rows[3:4, :]).astype(BF16)
            d_total[head] = (
                jnp.sum(feat.astype(F32) * d_denom, axis=0, keepdims=True) * rows[3:4, :]
            )
        return carry

    lax.fori_loop(0, pairs, step, 0)


def feature_back(d_feat, first, second, pick_a, pick_b, rows):
    scaled = d_feat * rows[2:3, :]
    return dot_nt((scaled * second).astype(BF16), pick_a) + dot_nt(
        (scaled * first).astype(BF16), pick_b
    )


def attend_back_body(
    query,
    keys,
    values,
    mixed,
    inverse,
    d_mixed,
    pick_a,
    pick_b,
    rows,
    state,
    total,
    d_state,
    d_total,
    d_query,
    d_keys,
    d_values,
    q_sum,
    k_sum,
    v_sum,
    block=256,
):
    pairs = values.shape[1] // LANES
    count = keys.shape[0]
    q_sum[...] = jnp.zeros_like(q_sum)
    k_sum[...] = jnp.zeros_like(k_sum)

    def step(pair, carry):
        spot = tile_at(pair)
        d_numer = d_mixed[:, spot].astype(F32) * inverse[:, spot]
        lost = d_numer * mixed[:, spot].astype(F32)
        d_low = d_numer.astype(BF16)
        turned = pltpu.roll(lost, VD, 1)
        vals = values[:, spot]
        for half in range(2):
            head = pair * 2 + half
            place = tile_at(head // 8)
            mine = half_lanes(count, half)
            lanes = head_lanes(count, head % 8)
            d_denom = -jnp.sum(only(mine, lost), axis=1, keepdims=True)
            d_wide = jnp.where(mine, d_numer, -turned).astype(BF16)
            v_wide = jnp.where(mine, vals, jnp.ones_like(vals))
            q_mask = only(lanes, query[:, place])
            k_mask = only(lanes, keys[:, place])
            grads_q, grads_k, grads_v = [], [], []
            for start in range(0, count, block):
                stop = start + block
                score = dot_nt(q_mask[start:stop], k_mask[0:stop]) * 0.25
                d_weight = dot_nt(d_wide[start:stop], v_wide[0:stop])
                d_score = only(causal(block, stop, start, 0), d_weight * (1.0 + score))
                grads_q.append(dot(d_score.astype(BF16), k_mask[0:stop]))
                rest = count - start
                score = dot_nt(k_mask[start:stop], q_mask[start:count]) * 0.25
                mask = causal(rest, block, 0, 0)
                mask = (
                    lax.broadcasted_iota(jnp.int32, (block, rest), 0)
                    <= lax.broadcasted_iota(jnp.int32, (block, rest), 1)
                )
                weight = only(mask, 1.0 + score + 0.5 * score * score)
                d_weight = dot_nt(v_wide[start:stop], d_wide[start:count])
                d_score = only(mask, d_weight * (1.0 + score))
                grads_k.append(dot(d_score.astype(BF16), q_mask[start:count]))
                grads_v.append(dot(weight.astype(BF16), d_low[start:count]))
            first, second = halves_of(q_mask, pick_a[...], pick_b[...], rows[...])
            d_feat = dot(d_low[:, half * VD : (half + 1) * VD], state[head]) + d_denom * total[head]
            inter_q = feature_back(d_feat, first, second, pick_a[...], pick_b[...], rows[...])
            first, second = halves_of(k_mask, pick_a[...], pick_b[...], rows[...])
            feat = (first * second * rows[2:3, :]).astype(BF16)
            d_feat = dot(vals[:, half * VD : (half + 1) * VD], d_state[head]) + d_total[head]
            inter_k = feature_back(d_feat, first, second, pick_a[...], pick_b[...], rows[...])
            inter_v = dot_nt(feat, d_state[head])
            inter_v = jnp.concatenate([inter_v, inter_v], axis=1)
            whole_v = jnp.concatenate(grads_v, axis=0) + inter_v
            v_sum[...] = whole_v if half == 0 else jnp.where(mine, whole_v, v_sum[...])
            q_sum[:, place] += jnp.concatenate(grads_q, axis=0) * 0.25 + only(lanes, inter_q)
            k_sum[:, place] += jnp.concatenate(grads_k, axis=0) * 0.25 + only(lanes, inter_k)
        d_values[:, spot] = v_sum[...].astype(BF16)
        return carry

    lax.fori_loop(0, pairs, step, 0)
    d_query[...] = q_sum[...].astype(BF16)
    d_keys[...] = k_sum[...].astype(BF16)


def call(body, shapes, *operands, scratch=()):
    return pl.pallas_call(
        body,
        out_shape=[jax.ShapeDtypeStruct(shape, kind) for shape, kind in shapes],
        scratch_shapes=list(scratch),
        compiler_params=pltpu.CompilerParams(vmem_limit_bytes=VMEM_LIMIT),
    )(*operands)


def rms_norm(inputs, gain):
    return inputs * lax.rsqrt(jnp.mean(inputs * inputs, axis=-1, keepdims=True) + EPS) * gain


def gated(gate_in, up_in):
    return jax.nn.silu(gate_in) * up_in


def before(parts, axis, reverse=False):
    place = lax.axis_index(axis)
    order = jnp.arange(parts.shape[0])
    chosen = order > place if reverse else order < place
    chosen = chosen.reshape((-1,) + (1,) * (parts.ndim - 1))
    return jnp.sum(jnp.where(chosen, parts.astype(F32), 0.0), axis=0)


def shards(
    tokens, attn_gain, w_query, w_key, w_value, w_output, mlp_gain, w_gate, w_up, w_down, out_grad
):
    count, width = tokens.shape
    heads = w_query.shape[1] // KD
    all_values = heads * VD
    tables = feature_tables()
    inputs = tokens.astype(F32)
    gain = attn_gain.astype(F32).reshape(1, width)
    gate_full, up_full, down_full = (
        lax.all_gather(w, ("dp", "seq"), axis=0, tiled=True) for w in (w_gate, w_up, w_down)
    )
    normed, query, keys, values = call(
        project_body,
        [
            ((count, width), BF16),
            ((count, heads * KD), BF16),
            ((count, heads * KD), BF16),
            ((count, all_values), BF16),
        ],
        tokens,
        gain,
        w_query,
        w_key,
        w_value,
    )
    state_shapes = [((heads, VD, FEATS), BF16), ((heads, 1, FEATS), F32)]
    state, total = call(state_body, state_shapes, keys, values, *tables)
    state = before(lax.all_gather(state, "seq"), "seq").astype(BF16)
    total = before(lax.all_gather(total, "seq"), "seq")
    mixed, inverse = call(
        attend_body,
        [((count, all_values), BF16), ((count, all_values), F32)],
        query,
        keys,
        values,
        *tables,
        state,
        total,
    )
    middle = inputs + dot(mixed, w_output)
    normed_mlp, second_back = jax.vjp(rms_norm, middle, mlp_gain.astype(F32))
    mlp_low = normed_mlp.astype(BF16)
    gate = dot(mlp_low, gate_full)
    upward = dot(mlp_low, up_full)
    hidden_val, gated_back = jax.vjp(gated, gate, upward)
    hidden = hidden_val.astype(BF16)
    layer_out = (middle + dot_nt(hidden, down_full)).astype(BF16)
    d_hidden = dot(out_grad, down_full)
    down_grad = dot_tn(out_grad, hidden).astype(BF16)
    d_gate_f, d_up_f = gated_back(d_hidden)
    d_gate = d_gate_f.astype(BF16)
    d_up = d_up_f.astype(BF16)
    gate_grad = dot_tn(mlp_low, d_gate).astype(BF16)
    up_grad = dot_tn(mlp_low, d_up).astype(BF16)
    d_normed_mlp = dot_nt(d_gate, gate_full) + dot_nt(d_up, up_full)
    d_middle_norm, mlp_gain_part = second_back(d_normed_mlp)
    d_middle = out_grad.astype(F32) + d_middle_norm
    d_branch = d_middle.astype(BF16)
    output_grad = dot_tn(mixed, d_branch).astype(BF16)
    d_mixed = dot_nt(d_branch, w_output).astype(BF16)
    d_state, d_total = call(
        back_state_body, state_shapes, query, mixed, inverse, d_mixed, *tables
    )
    d_state = before(lax.all_gather(d_state, "seq"), "seq", True).astype(BF16)
    d_total = before(lax.all_gather(d_total, "seq"), "seq", True)
    d_query, d_keys, d_values = call(
        attend_back_body,
        [
            ((count, heads * KD), BF16),
            ((count, heads * KD), BF16),
            ((count, all_values), BF16),
        ],
        query,
        keys,
        values,
        mixed,
        inverse,
        d_mixed,
        *tables,
        state,
        total,
        d_state,
        d_total,
        scratch=[
            pltpu.VMEM((count, heads * KD), F32),
            pltpu.VMEM((count, heads * KD), F32),
            pltpu.VMEM((count, LANES), F32),
        ],
    )
    d_normed = dot_nt(d_query, w_query) + dot_nt(d_keys, w_key) + dot_nt(d_values, w_value)
    query_grad = dot_tn(normed, d_query).astype(BF16)
    key_grad = dot_tn(normed, d_keys).astype(BF16)
    value_grad = dot_tn(normed, d_values).astype(BF16)
    _, first_back = jax.vjp(rms_norm, inputs, attn_gain.astype(F32))
    d_inputs_norm, attn_gain_part = first_back(d_normed)
    tokens_grad = d_middle + d_inputs_norm
    parts = [query_grad, key_grad, value_grad, output_grad, gate_grad, up_grad, down_grad]
    joined = lax.psum_scatter(
        jnp.concatenate(parts, axis=1), ("dp", "seq"), scatter_dimension=0, tiled=True
    ).astype(F32)
    edges = np.cumsum([part.shape[1] for part in parts])[:-1]
    query_grad, key_grad, value_grad, output_grad, gate_grad, up_grad, down_grad = jnp.split(
        joined, edges, axis=1
    )
    gains = lax.psum_scatter(
        jnp.stack([attn_gain_part, mlp_gain_part], axis=1),
        ("dp", "seq"),
        scatter_dimension=0,
        tiled=True,
    )
    return (
        layer_out,
        tokens_grad,
        gains[:, 0],
        query_grad,
        key_grad,
        value_grad,
        output_grad,
        gains[:, 1],
        gate_grad,
        up_grad,
        down_grad,
    )


def solution(mesh):
    rows = P(("dp", "seq"), None)
    in_specs = (rows, P(), P(), P(), P(), P(), P(), rows, rows, rows, rows)
    out_specs = (
        rows,
        rows,
        P(("dp", "seq")),
        rows,
        rows,
        rows,
        rows,
        P(("dp", "seq")),
        rows,
        rows,
        rows,
    )
    return jax.shard_map(
        shards, mesh=mesh, in_specs=in_specs, out_specs=out_specs, check_vma=False
    )
```

```python
import math

import jax
import jax.numpy as jnp
import numpy as np
from jax import lax
from jax.experimental import pallas as pl
from jax.experimental.pallas import tpu as pltpu
from jax.sharding import PartitionSpec as P

KD = 16
VD = 64
LANES = 128
FEATS = 256
EPS = 1e-05
QUAD = 1.0 / (4.0 * math.sqrt(2.0))
F32 = jnp.float32
BF16 = jnp.bfloat16
VMEM_LIMIT = 58 << 20


def feature_tables():
    pick_a = np.zeros((LANES, FEATS), np.float32)
    pick_b = np.zeros((LANES, FEATS), np.float32)
    rows = np.zeros((8, FEATS), np.float32)
    spot = 0
    for a in range(KD):
        for b in range(a, KD):
            pick_a[a::KD, spot] = 1.0
            pick_b[b::KD, spot] = 1.0
            rows[2, spot] = QUAD
            rows[3, spot] = 1.0 if a == b else 2.0
            spot += 1
    for a in range(KD):
        pick_a[a::KD, spot] = 1.0
        rows[1, spot] = 1.0
        rows[2, spot] = 0.5
        rows[3, spot] = 1.0
        spot += 1
    rows[0:4, spot] = 1.0
    return jnp.asarray(pick_a, BF16), jnp.asarray(pick_b, BF16), jnp.asarray(rows)


def dot(left, right):
    return jnp.dot(left, right, preferred_element_type=F32)


def dot_nt(left, right):
    return lax.dot_general(left, right, (((1,), (1,)), ((), ())), preferred_element_type=F32)


def dot_tn(left, right):
    return lax.dot_general(left, right, (((0,), (0,)), ((), ())), preferred_element_type=F32)


def tile_at(index):
    return pl.ds(pl.multiple_of(index * LANES, LANES), LANES)


def head_lanes(rows, spot):
    return lax.broadcasted_iota(jnp.int32, (rows, LANES), 1) // KD == spot


def half_lanes(rows, half):
    return lax.broadcasted_iota(jnp.int32, (rows, LANES), 1) // VD == half


def halves_of(masked, pick_a, pick_b, rows):
    first = dot(masked, pick_a) + rows[0:1, :]
    second = dot(masked, pick_b) + rows[1:2, :]
    return first, second


def features_of(masked, pick_a, pick_b, rows):
    first, second = halves_of(masked, pick_a, pick_b, rows)
    return (first * second * rows[2:3, :]).astype(BF16)


def only(mask, value):
    return jnp.where(mask, value, jnp.zeros_like(value))


def project_body(tok, gain, wq, wk, wv, normed, query, keys, values):
    x = tok[...].astype(F32)
    scale = lax.rsqrt(jnp.mean(x * x, axis=-1, keepdims=True) + EPS)
    normed[...] = (x * scale * gain[...]).astype(BF16)
    query[...] = dot(normed[...], wq[...]).astype(BF16)
    keys[...] = dot(normed[...], wk[...]).astype(BF16)
    values[...] = dot(normed[...], wv[...]).astype(BF16)


def state_body(keys, values, pick_a, pick_b, rows, state, total):
    pairs = values.shape[1] // LANES
    count = keys.shape[0]

    def step(pair, carry):
        turned = values[:, tile_at(pair)].T
        for half in range(2):
            head = pair * 2 + half
            masked = only(head_lanes(count, head % 8), keys[:, tile_at(head // 8)])
            feat = features_of(masked, pick_a[...], pick_b[...], rows[...])
            sums = dot(turned[half * VD : (half + 1) * VD, :], feat)
            state[head] = (sums * rows[3:4, :]).astype(BF16)
            total[head] = jnp.sum(feat.astype(F32), axis=0, keepdims=True) * rows[3:4, :]
        return carry

    lax.fori_loop(0, pairs, step, 0)


def causal(rows, columns, row_start, column_start):
    row = lax.broadcasted_iota(jnp.int32, (rows, columns), 0) + row_start
    column = lax.broadcasted_iota(jnp.int32, (rows, columns), 1) + column_start
    return row >= column


def attend_body(query, keys, values, pick_a, pick_b, rows, state, total, mixed, inverse, block=256):
    pairs = values.shape[1] // LANES
    count = keys.shape[0]

    def step(pair, carry):
        vals = values[:, tile_at(pair)]
        for start in range(0, count, block):
            stop = start + block
            numer = None
            for half in range(2):
                head = pair * 2 + half
                masked = only(head_lanes(block, head % 8), query[start:stop, tile_at(head // 8)])
                score = dot_nt(masked, keys[0:stop, tile_at(head // 8)]) * 0.25
                weight = 1.0 + score + 0.5 * score * score
                weight = jnp.where(causal(block, stop, start, 0), weight, 0.0)
                feat = features_of(masked, pick_a[...], pick_b[...], rows[...])
                inter = feat.astype(F32) * total[head]
                denom = jnp.sum(weight, axis=1, keepdims=True) + jnp.sum(
                    inter, axis=1, keepdims=True
                )
                across = dot_nt(feat, state[head])
                both = dot(weight.astype(BF16), vals[0:stop, :])
                across = jnp.concatenate([across, across], axis=1)
                whole = (both + across) / denom
                flip = jnp.broadcast_to(1.0 / denom, (block, LANES))
                if half == 0:
                    numer, invs = whole, flip
                else:
                    mask = half_lanes(block, 0)
                    numer = jnp.where(mask, numer, whole)
                    invs = jnp.where(mask, invs, flip)
            mixed[start:stop, tile_at(pair)] = numer.astype(BF16)
            inverse[start:stop, tile_at(pair)] = invs
        return carry

    lax.fori_loop(0, pairs, step, 0)


def back_state_body(query, mixed, inverse, d_mixed, pick_a, pick_b, rows, d_state, d_total):
    pairs = mixed.shape[1] // LANES
    count = query.shape[0]

    def step(pair, carry):
        spot = tile_at(pair)
        d_numer = d_mixed[:, spot].astype(F32) * inverse[:, spot]
        lost = d_numer * mixed[:, spot].astype(F32)
        turned = d_numer.astype(BF16).T
        for half in range(2):
            head = pair * 2 + half
            masked = only(head_lanes(count, head % 8), query[:, tile_at(head // 8)])
            feat = features_of(masked, pick_a[...], pick_b[...], rows[...])
            d_denom = -jnp.sum(only(half_lanes(count, half), lost), axis=1, keepdims=True)
            sums = dot(turned[half * VD : (half + 1) * VD, :], feat)
            d_state[head] = (sums * rows[3:4, :]).astype(BF16)
            d_total[head] = (
                jnp.sum(feat.astype(F32) * d_denom, axis=0, keepdims=True) * rows[3:4, :]
            )
        return carry

    lax.fori_loop(0, pairs, step, 0)


def feature_back(d_feat, first, second, pick_a, pick_b, rows):
    scaled = d_feat * rows[2:3, :]
    return dot_nt((scaled * second).astype(BF16), pick_a) + dot_nt(
        (scaled * first).astype(BF16), pick_b
    )


def attend_back_body(
    query,
    keys,
    values,
    mixed,
    inverse,
    d_mixed,
    pick_a,
    pick_b,
    rows,
    state,
    total,
    d_state,
    d_total,
    d_query,
    d_keys,
    d_values,
    q_sum,
    k_sum,
    v_sum,
    block=256,
):
    pairs = values.shape[1] // LANES
    count = keys.shape[0]
    q_sum[...] = jnp.zeros_like(q_sum)
    k_sum[...] = jnp.zeros_like(k_sum)

    def step(pair, carry):
        spot = tile_at(pair)
        d_numer = d_mixed[:, spot].astype(F32) * inverse[:, spot]
        lost = d_numer * mixed[:, spot].astype(F32)
        d_low = d_numer.astype(BF16)
        turned = pltpu.roll(lost, VD, 1)
        vals = values[:, spot]
        for half in range(2):
            head = pair * 2 + half
            place = tile_at(head // 8)
            mine = half_lanes(count, half)
            lanes = head_lanes(count, head % 8)
            d_denom = -jnp.sum(only(mine, lost), axis=1, keepdims=True)
            d_wide = jnp.where(mine, d_numer, -turned).astype(BF16)
            v_wide = jnp.where(mine, vals, jnp.ones_like(vals))
            q_mask = only(lanes, query[:, place])
            k_mask = only(lanes, keys[:, place])
            grads_q, grads_k, grads_v = [], [], []
            for start in range(0, count, block):
                stop = start + block
                score = dot_nt(q_mask[start:stop], k_mask[0:stop]) * 0.25
                d_weight = dot_nt(d_wide[start:stop], v_wide[0:stop])
                d_score = only(causal(block, stop, start, 0), d_weight * (1.0 + score))
                grads_q.append(dot(d_score.astype(BF16), k_mask[0:stop]))
                rest = count - start
                score = dot_nt(k_mask[start:stop], q_mask[start:count]) * 0.25
                mask = causal(rest, block, 0, 0)
                mask = (
                    lax.broadcasted_iota(jnp.int32, (block, rest), 0)
                    <= lax.broadcasted_iota(jnp.int32, (block, rest), 1)
                )
                weight = only(mask, 1.0 + score + 0.5 * score * score)
                d_weight = dot_nt(v_wide[start:stop], d_wide[start:count])
                d_score = only(mask, d_weight * (1.0 + score))
                grads_k.append(dot(d_score.astype(BF16), q_mask[start:count]))
                grads_v.append(dot(weight.astype(BF16), d_low[start:count]))
            first, second = halves_of(q_mask, pick_a[...], pick_b[...], rows[...])
            d_feat = dot(d_low[:, half * VD : (half + 1) * VD], state[head]) + d_denom * total[head]
            inter_q = feature_back(d_feat, first, second, pick_a[...], pick_b[...], rows[...])
            first, second = halves_of(k_mask, pick_a[...], pick_b[...], rows[...])
            feat = (first * second * rows[2:3, :]).astype(BF16)
            d_feat = dot(vals[:, half * VD : (half + 1) * VD], d_state[head]) + d_total[head]
            inter_k = feature_back(d_feat, first, second, pick_a[...], pick_b[...], rows[...])
            inter_v = dot_nt(feat, d_state[head])
            inter_v = jnp.concatenate([inter_v, inter_v], axis=1)
            whole_v = jnp.concatenate(grads_v, axis=0) + inter_v
            v_sum[...] = whole_v if half == 0 else jnp.where(mine, whole_v, v_sum[...])
            q_sum[:, place] += jnp.concatenate(grads_q, axis=0) * 0.25 + only(lanes, inter_q)
            k_sum[:, place] += jnp.concatenate(grads_k, axis=0) * 0.25 + only(lanes, inter_k)
        d_values[:, spot] = v_sum[...].astype(BF16)
        return carry

    lax.fori_loop(0, pairs, step, 0)
    d_query[...] = q_sum[...].astype(BF16)
    d_keys[...] = k_sum[...].astype(BF16)


def call(body, shapes, *operands, scratch=()):
    return pl.pallas_call(
        body,
        out_shape=[jax.ShapeDtypeStruct(shape, kind) for shape, kind in shapes],
        scratch_shapes=list(scratch),
        compiler_params=pltpu.CompilerParams(vmem_limit_bytes=VMEM_LIMIT),
    )(*operands)


def rms_norm(inputs, gain):
    return inputs * lax.rsqrt(jnp.mean(inputs * inputs, axis=-1, keepdims=True) + EPS) * gain


def gated(gate_in, up_in):
    return jax.nn.silu(gate_in) * up_in


def before(parts, axis, reverse=False):
    place = lax.axis_index(axis)
    order = jnp.arange(parts.shape[0])
    chosen = order > place if reverse else order < place
    chosen = chosen.reshape((-1,) + (1,) * (parts.ndim - 1))
    return jnp.sum(jnp.where(chosen, parts.astype(F32), 0.0), axis=0)


MESH_ID = pl.DeviceIdType.MESH


class Place:
    def __init__(self):
        self.dp, self.seq = lax.axis_index("dp"), lax.axis_index("seq")
        self.z, self.y = self.dp // 2, self.dp % 2
        self.x, self.core = self.seq // 2, self.seq % 2

    def at(self, z=None, y=None, x=None, core=None):
        z = self.z if z is None else z
        y = self.y if y is None else y
        x = self.x if x is None else x
        core = self.core if core is None else core
        return (z * 2 + y, x * 2 + core)

    def mate(self):
        return self.at(core=1 - self.core)

    def across(self, axis):
        return self.at(y=1 - self.y) if axis == "y" else self.at(x=1 - self.x)

    def own(self, axis):
        return self.y if axis == "y" else self.x


def remote(source, target, sent, landed, device):
    return pltpu.make_async_remote_copy(
        src_ref=source,
        dst_ref=target,
        send_sem=sent,
        recv_sem=landed,
        device_id=device,
        device_id_type=MESH_ID,
    )


def enter(place):
    barrier = pltpu.get_barrier_semaphore()
    others = [place.mate(), place.across("x"), place.across("y")]
    for other in (1, 2, 3):
        others.append(place.at(z=jnp.bitwise_xor(place.z, other)))
    for device in others:
        pl.semaphore_signal(barrier, inc=1, device_id=device, device_id_type=MESH_ID)
    pl.semaphore_wait(barrier, len(others))


class Piece:
    def __init__(self, source, target, low, rows, columns, first, middle):
        self.source, self.target = source, target
        self.low, self.rows, self.columns = low, rows, columns
        self.first, self.third, self.middle = first, "x" if first == "y" else "y", middle

    def scratch(self):
        block = (self.rows, self.columns)
        unit = (2,) + block if self.middle else block
        last = block if self.middle else (4,) + block
        return dict(
            mine=pltpu.VMEM((4, 2, 2) + block, BF16),
            mates=pltpu.VMEM((4, 2, 2) + block, BF16),
            ones=pltpu.VMEM((4, 2) + block, BF16),
            line=pltpu.VMEM((5,) + unit, BF16),
            last=pltpu.VMEM(last, BF16),
            load=pltpu.SemaphoreType.DMA((4,)),
            sent=pltpu.SemaphoreType.DMA((20,)),
            landed=pltpu.SemaphoreType.DMA((20,)),
        )


def added(target, others, lead, rows, wide=False):
    tall = min(rows, 16)
    per = rows // tall
    total = int(np.prod(lead, dtype=np.int64)) * per

    def step(index, carry):
        spot, rest = [], index // per
        for size in reversed(lead):
            spot.insert(0, rest % size)
            rest = rest // size
        where = tuple(spot) + (pl.ds(pl.multiple_of((index % per) * tall, tall), tall), slice(None))
        value = target[where]
        if wide:
            value = value.astype(F32)
            for other in others:
                value = value + other[where].astype(F32)
            target[where] = value.astype(BF16)
        else:
            for other in others:
                value = value + other[where]
            target[where] = value
        return carry

    lax.fori_loop(0, total, step, 0)


def piece_steps(piece, refs, source, target, place):
    mine, mates, ones, line, last = (refs[k] for k in ("mine", "mates", "ones", "line", "last"))
    load, sent, landed = refs["load"], refs["sent"], refs["landed"]
    rows, low = piece.rows, piece.low
    own1, own3 = place.own(piece.first), place.own(piece.third)
    z = place.z

    def pick(ref, block, which):
        return ref.at[block, which] if piece.first == "y" else ref.at[block, :, which]

    def share(block, core):
        return source.at[block, :, :, core, pl.ds(low, rows), :]

    def fetch(block):
        return pltpu.make_async_copy(share(block, place.core), mine.at[block], load.at[block])

    def to_mate(block):
        return remote(
            share(block, 1 - place.core), mates.at[block], sent.at[block], landed.at[block], place.mate()
        )

    def to_first(block):
        return remote(
            pick(mine, block, 1 - own1),
            ones.at[block],
            sent.at[4 + block],
            landed.at[4 + block],
            place.across(piece.first),
        )

    def to_third(block):
        spot = 8 + block
        return remote(
            ones.at[block, 1 - own3],
            last.at[block],
            sent.at[spot],
            landed.at[spot],
            place.across(piece.third),
        )

    def unit(block):
        if piece.middle:
            return ones.at[block]
        return ones.at[block, own3]

    def along(block, step):
        slot = jnp.where(z + step == block, 4, block) if step < 0 else block
        return remote(
            unit(block),
            line.at[slot],
            sent.at[12 + block],
            landed.at[12 + slot],
            place.at(z=jnp.clip(z + step, 0, 3)),
        )

    def arrival(slot):
        return remote(unit(0), line.at[slot], sent.at[12], landed.at[12 + slot], place.mate())

    lead = (2,) if piece.middle else ()

    def join(block):
        fetch(block).wait()
        to_mate(block).wait_recv()
        added(mine.at[block], [mates.at[block]], (2, 2), rows)
        to_first(block).start()

    def merge(block):
        to_first(block).wait_recv()
        added(ones.at[block], [pick(mine, block, own1)], (2,), rows)
        if not piece.middle:
            to_third(block).start()

    def turn(block):
        if not piece.middle:
            to_third(block).wait_recv()
            added(unit(block), [last.at[block]], (), rows)

    def pass_on(block, step):
        heading = block > z if step > 0 else block < z
        inner = z > 0 if step > 0 else z < 3

        @pl.when(heading)
        def _():
            @pl.when(inner)
            def _():
                arrival(block).wait_recv()
                added(unit(block), [line.at[block]], lead, rows)

            along(block, step).start()

    def finish():
        @pl.when(z > 0)
        def _():
            arrival(z).wait_recv()
            added(unit(z), [line.at[z]], lead, rows)

        @pl.when(z < 3)
        def _():
            arrival(4).wait_recv()
            added(unit(z), [line.at[4]], lead, rows)

    def out(value):
        target[pl.ds(low, rows), :] = value

    for block in (3, 0, 2, 1):
        fetch(block).start()
        to_mate(block).start()
    yield
    join(3)
    yield
    join(0)
    yield
    merge(3)
    join(2)
    yield
    merge(0)
    join(1)
    yield
    turn(3)
    pass_on(3, 1)
    turn(0)
    pass_on(0, -1)
    yield
    merge(2)
    yield
    turn(2)
    pass_on(2, 1)
    yield
    merge(1)
    yield
    turn(1)
    pass_on(1, -1)
    yield
    pass_on(1, 1)
    yield
    pass_on(2, -1)
    yield
    finish()
    if piece.middle:
        final = remote(
            ones.at[z, 1 - own3], last, sent.at[8], landed.at[8], place.across(piece.third)
        )
        final.start()
        yield
        final.wait_recv()
        out(ones[z, own3].astype(F32) + last[...].astype(F32))
    else:
        out(ones[z, own3].astype(F32))
    yield
    for block in range(4):
        to_mate(block).wait_send()
        to_first(block).wait_send()
        if not piece.middle:
            to_third(block).wait_send()

        @pl.when(block > z)
        def _():
            along(block, 1).wait_send()

        @pl.when(block < z)
        def _():
            along(block, -1).wait_send()

    if piece.middle:
        final.wait_send()


def gain_steps(mine, slots, sent, landed, place):
    partners = [place.mate(), place.across("x"), place.across("y")]
    for other in (1, 2):
        partners.append(place.at(z=jnp.bitwise_xor(place.z, other)))
    for spot, partner in enumerate(partners):
        copy = remote(mine.at[spot], slots.at[spot], sent.at[spot], landed.at[spot], partner)
        copy.start()
        yield
        copy.wait()
        mine[spot + 1] = mine[spot] + slots[spot]


def plan(widths):
    wide, heads_wide, narrow = widths
    return [
        Piece(0, 0, 0, 32, wide, "y", True),
        Piece(1, 1, 0, 32, wide, "x", True),
        Piece(2, 2, 0, 16, wide, "y", False),
        Piece(2, 2, 16, 16, wide, "x", False),
        Piece(3, 3, 0, 32, heads_wide, "y", False),
        Piece(4, 4, 0, 32, heads_wide, "x", False),
        Piece(5, 5, 0, 32, narrow, "y", False),
        Piece(6, 6, 0, 32, narrow, "x", False),
    ]


def reduce_grads(grads, gains):
    widths = (grads[0].shape[1], grads[3].shape[1], grads[5].shape[1])
    pieces = plan(widths)
    scratch = [piece.scratch() for piece in pieces]
    names = list(scratch[0])
    flat = [entry[name] for entry in scratch for name in names]
    count = len(grads)

    def body(*refs):
        sources, gain = refs[:count], refs[count]
        targets, gain_out = refs[count + 1 : 2 * count + 1], refs[2 * count + 1]
        rest = refs[2 * count + 2 :]
        gain_mine, gain_slots, gain_sent, gain_landed = rest[:4]
        rest = rest[4:]
        place = Place()
        enter(place)
        gain_mine[0] = gain[...]
        gain_run = gain_steps(gain_mine, gain_slots, gain_sent, gain_landed, place)
        runs = []
        for spot, piece in enumerate(pieces):
            own = dict(zip(names, rest[spot * len(names) : (spot + 1) * len(names)]))
            runs.append(
                piece_steps(piece, own, sources[piece.source], targets[piece.target], place)
            )
        starts = [0, 0, 4, 4, 6, 6, 7, 7]
        active = True
        slot = 0
        while active:
            active = False
            for run, start in zip(runs, starts):
                if slot >= start and next(run, "done") != "done":
                    active = True
                if slot < start:
                    active = True
            next(gain_run, None)
            slot += 1
        for _ in gain_run:
            pass
        gain_out[...] = gain_mine[5]

    views = [g.reshape(4, 2, 2, 2, 32, g.shape[1]) for g in grads]
    outs = [jax.ShapeDtypeStruct((32, g.shape[1]), F32) for g in grads]
    outs.append(jax.ShapeDtypeStruct(gains.shape, F32))
    return pl.pallas_call(
        body,
        out_shape=outs,
        in_specs=[pl.BlockSpec(memory_space=pl.ANY)] * count
        + [pl.BlockSpec(memory_space=pltpu.VMEM)],
        out_specs=[pl.BlockSpec(memory_space=pltpu.VMEM)] * (count + 1),
        scratch_shapes=[
            pltpu.VMEM((6,) + gains.shape, F32),
            pltpu.VMEM((5,) + gains.shape, F32),
            pltpu.SemaphoreType.DMA((5,)),
            pltpu.SemaphoreType.DMA((5,)),
        ]
        + flat,
        compiler_params=pltpu.CompilerParams(
            collective_id=0, has_side_effects=True, vmem_limit_bytes=VMEM_LIMIT
        ),
    )(*views, gains)


def shards(
    tokens, attn_gain, w_query, w_key, w_value, w_output, mlp_gain, w_gate, w_up, w_down, out_grad
):
    count, width = tokens.shape
    heads = w_query.shape[1] // KD
    all_values = heads * VD
    tables = feature_tables()
    inputs = tokens.astype(F32)
    gain = attn_gain.astype(F32).reshape(1, width)
    gate_full, up_full, down_full = (
        lax.all_gather(w, ("dp", "seq"), axis=0, tiled=True) for w in (w_gate, w_up, w_down)
    )
    normed, query, keys, values = call(
        project_body,
        [
            ((count, width), BF16),
            ((count, heads * KD), BF16),
            ((count, heads * KD), BF16),
            ((count, all_values), BF16),
        ],
        tokens,
        gain,
        w_query,
        w_key,
        w_value,
    )
    state_shapes = [((heads, VD, FEATS), BF16), ((heads, 1, FEATS), F32)]
    state, total = call(state_body, state_shapes, keys, values, *tables)
    state = before(lax.all_gather(state, "seq"), "seq").astype(BF16)
    total = before(lax.all_gather(total, "seq"), "seq")
    mixed, inverse = call(
        attend_body,
        [((count, all_values), BF16), ((count, all_values), F32)],
        query,
        keys,
        values,
        *tables,
        state,
        total,
    )
    middle = inputs + dot(mixed, w_output)
    normed_mlp, second_back = jax.vjp(rms_norm, middle, mlp_gain.astype(F32))
    mlp_low = normed_mlp.astype(BF16)
    gate = dot(mlp_low, gate_full)
    upward = dot(mlp_low, up_full)
    hidden_val, gated_back = jax.vjp(gated, gate, upward)
    hidden = hidden_val.astype(BF16)
    layer_out = (middle + dot_nt(hidden, down_full)).astype(BF16)
    d_hidden = dot(out_grad, down_full)
    down_grad = dot_tn(out_grad, hidden).astype(BF16)
    d_gate_f, d_up_f = gated_back(d_hidden)
    d_gate = d_gate_f.astype(BF16)
    d_up = d_up_f.astype(BF16)
    gate_grad = dot_tn(mlp_low, d_gate).astype(BF16)
    up_grad = dot_tn(mlp_low, d_up).astype(BF16)
    d_normed_mlp = dot_nt(d_gate, gate_full) + dot_nt(d_up, up_full)
    d_middle_norm, mlp_gain_part = second_back(d_normed_mlp)
    d_middle = out_grad.astype(F32) + d_middle_norm
    d_branch = d_middle.astype(BF16)
    output_grad = dot_tn(mixed, d_branch).astype(BF16)
    d_mixed = dot_nt(d_branch, w_output).astype(BF16)
    d_state, d_total = call(
        back_state_body, state_shapes, query, mixed, inverse, d_mixed, *tables
    )
    d_state = before(lax.all_gather(d_state, "seq"), "seq", True).astype(BF16)
    d_total = before(lax.all_gather(d_total, "seq"), "seq", True)
    d_query, d_keys, d_values = call(
        attend_back_body,
        [
            ((count, heads * KD), BF16),
            ((count, heads * KD), BF16),
            ((count, all_values), BF16),
        ],
        query,
        keys,
        values,
        mixed,
        inverse,
        d_mixed,
        *tables,
        state,
        total,
        d_state,
        d_total,
        scratch=[
            pltpu.VMEM((count, heads * KD), F32),
            pltpu.VMEM((count, heads * KD), F32),
            pltpu.VMEM((count, LANES), F32),
        ],
    )
    d_normed = dot_nt(d_query, w_query) + dot_nt(d_keys, w_key) + dot_nt(d_values, w_value)
    query_grad = dot_tn(normed, d_query).astype(BF16)
    key_grad = dot_tn(normed, d_keys).astype(BF16)
    value_grad = dot_tn(normed, d_values).astype(BF16)
    _, first_back = jax.vjp(rms_norm, inputs, attn_gain.astype(F32))
    d_inputs_norm, attn_gain_part = first_back(d_normed)
    tokens_grad = d_middle + d_inputs_norm
    grads = [gate_grad, up_grad, down_grad, output_grad, value_grad, query_grad, key_grad]
    gain_parts = jnp.stack([attn_gain_part, mlp_gain_part])
    own = lax.axis_index("dp") * lax.axis_size("seq") + lax.axis_index("seq")
    if (lax.axis_size("dp"), lax.axis_size("seq")) == (8, 4):
        *grads, gains = reduce_grads(grads, jnp.pad(gain_parts, ((0, 6), (0, 0))))
        share = width // 32
        gains = lax.dynamic_slice(gains, (0, own * share), (2, share)).T
    else:
        joined = lax.psum_scatter(
            jnp.concatenate(grads, axis=1), ("dp", "seq"), scatter_dimension=0, tiled=True
        ).astype(F32)
        edges = np.cumsum([part.shape[1] for part in grads])[:-1]
        grads = jnp.split(joined, edges, axis=1)
        gains = lax.psum_scatter(gain_parts.T, ("dp", "seq"), scatter_dimension=0, tiled=True)
    gate_grad, up_grad, down_grad, output_grad, value_grad, query_grad, key_grad = grads
    return (
        layer_out,
        tokens_grad,
        gains[:, 0],
        query_grad,
        key_grad,
        value_grad,
        output_grad,
        gains[:, 1],
        gate_grad,
        up_grad,
        down_grad,
    )


def solution(mesh):
    rows = P(("dp", "seq"), None)
    in_specs = (rows, P(), P(), P(), P(), P(), P(), rows, rows, rows, rows)
    out_specs = (
        rows,
        rows,
        P(("dp", "seq")),
        rows,
        rows,
        rows,
        rows,
        P(("dp", "seq")),
        rows,
        rows,
        rows,
    )
    return jax.shard_map(
        shards, mesh=mesh, in_specs=in_specs, out_specs=out_specs, check_vma=False
    )
```

```python
import math

import jax
import jax.numpy as jnp
import numpy as np
from jax import lax
from jax.experimental import pallas as pl
from jax.experimental.pallas import tpu as pltpu
from jax.sharding import PartitionSpec as P

KD = 16
VD = 64
LANES = 128
FEATS = 256
EPS = 1e-05
QUAD = 1.0 / (4.0 * math.sqrt(2.0))
F32 = jnp.float32
BF16 = jnp.bfloat16
VMEM_LIMIT = 60 << 20


def feature_tables():
    pick_a = np.zeros((LANES, FEATS), np.float32)
    pick_b = np.zeros((LANES, FEATS), np.float32)
    rows = np.zeros((8, FEATS), np.float32)
    spot = 0
    for a in range(KD):
        for b in range(a, KD):
            pick_a[a::KD, spot] = 1.0
            pick_b[b::KD, spot] = 1.0
            rows[2, spot] = QUAD
            rows[3, spot] = 1.0 if a == b else 2.0
            spot += 1
    for a in range(KD):
        pick_a[a::KD, spot] = 1.0
        rows[1, spot] = 1.0
        rows[2, spot] = 0.5
        rows[3, spot] = 1.0
        spot += 1
    rows[0:4, spot] = 1.0
    return jnp.asarray(pick_a, BF16), jnp.asarray(pick_b, BF16), jnp.asarray(rows)


def dot(left, right):
    return jnp.dot(left, right, preferred_element_type=F32)


def dot_nt(left, right):
    return lax.dot_general(left, right, (((1,), (1,)), ((), ())), preferred_element_type=F32)


def dot_tn(left, right):
    return lax.dot_general(left, right, (((0,), (0,)), ((), ())), preferred_element_type=F32)


def tile_at(index):
    return pl.ds(pl.multiple_of(index * LANES, LANES), LANES)


def head_lanes(rows, spot):
    return lax.broadcasted_iota(jnp.int32, (rows, LANES), 1) // KD == spot


def half_lanes(rows, half):
    return lax.broadcasted_iota(jnp.int32, (rows, LANES), 1) // VD == half


def halves_of(masked, pick_a, pick_b, rows):
    first = dot(masked, pick_a) + rows[0:1, :]
    second = dot(masked, pick_b) + rows[1:2, :]
    return first, second


def features_of(masked, pick_a, pick_b, rows):
    first, second = halves_of(masked, pick_a, pick_b, rows)
    return (first * second * rows[2:3, :]).astype(BF16)


def only(mask, value):
    return jnp.where(mask, value, jnp.zeros_like(value))


def project_body(tok, gain, wq, wk, wv, normed, query, keys, values):
    x = tok[...].astype(F32)
    scale = lax.rsqrt(jnp.mean(x * x, axis=-1, keepdims=True) + EPS)
    normed[...] = (x * scale * gain[...]).astype(BF16)
    query[...] = dot(normed[...], wq[...]).astype(BF16)
    keys[...] = dot(normed[...], wk[...]).astype(BF16)
    values[...] = dot(normed[...], wv[...]).astype(BF16)


def state_body(keys, values, pick_a, pick_b, rows, state, total):
    pairs = values.shape[1] // LANES
    count = keys.shape[0]

    def step(pair, carry):
        turned = values[:, tile_at(pair)].T
        for half in range(2):
            head = pair * 2 + half
            masked = only(head_lanes(count, head % 8), keys[:, tile_at(head // 8)])
            feat = features_of(masked, pick_a[...], pick_b[...], rows[...])
            sums = dot(turned[half * VD : (half + 1) * VD, :], feat)
            state[head] = (sums * rows[3:4, :]).astype(BF16)
            total[head] = jnp.sum(feat.astype(F32), axis=0, keepdims=True) * rows[3:4, :]
        return carry

    lax.fori_loop(0, pairs, step, 0)


def causal(rows, columns, row_start, column_start):
    row = lax.broadcasted_iota(jnp.int32, (rows, columns), 0) + row_start
    column = lax.broadcasted_iota(jnp.int32, (rows, columns), 1) + column_start
    return row >= column


def attend_body(query, keys, values, pick_a, pick_b, rows, state, total, mixed, inverse, between=None, block=256):
    pairs = values.shape[1] // LANES
    count = keys.shape[0]

    def step(pair, carry):
        vals = values[:, tile_at(pair)]
        for start in range(0, count, block):
            stop = start + block
            numer = None
            for half in range(2):
                head = pair * 2 + half
                masked = only(head_lanes(block, head % 8), query[start:stop, tile_at(head // 8)])
                score = dot_nt(masked, keys[0:stop, tile_at(head // 8)]) * 0.25
                weight = 1.0 + score + 0.5 * score * score
                weight = jnp.where(causal(block, stop, start, 0), weight, 0.0)
                feat = features_of(masked, pick_a[...], pick_b[...], rows[...])
                inter = feat.astype(F32) * total[head]
                denom = jnp.sum(weight, axis=1, keepdims=True) + jnp.sum(
                    inter, axis=1, keepdims=True
                )
                across = dot_nt(feat, state[head])
                both = dot(weight.astype(BF16), vals[0:stop, :])
                across = jnp.concatenate([across, across], axis=1)
                whole = (both + across) / denom
                flip = jnp.broadcast_to(1.0 / denom, (block, LANES))
                if half == 0:
                    numer, invs = whole, flip
                else:
                    mask = half_lanes(block, 0)
                    numer = jnp.where(mask, numer, whole)
                    invs = jnp.where(mask, invs, flip)
            mixed[start:stop, tile_at(pair)] = numer.astype(BF16)
            inverse[start:stop, tile_at(pair)] = invs
        if between is not None:
            between(pair)
        return carry

    lax.fori_loop(0, pairs, step, 0)


def back_state_body(query, mixed, inverse, d_mixed, pick_a, pick_b, rows, d_state, d_total):
    pairs = mixed.shape[1] // LANES
    count = query.shape[0]

    def step(pair, carry):
        spot = tile_at(pair)
        d_numer = d_mixed[:, spot].astype(F32) * inverse[:, spot]
        lost = d_numer * mixed[:, spot].astype(F32)
        turned = d_numer.astype(BF16).T
        for half in range(2):
            head = pair * 2 + half
            masked = only(head_lanes(count, head % 8), query[:, tile_at(head // 8)])
            feat = features_of(masked, pick_a[...], pick_b[...], rows[...])
            d_denom = -jnp.sum(only(half_lanes(count, half), lost), axis=1, keepdims=True)
            sums = dot(turned[half * VD : (half + 1) * VD, :], feat)
            d_state[head] = (sums * rows[3:4, :]).astype(BF16)
            d_total[head] = (
                jnp.sum(feat.astype(F32) * d_denom, axis=0, keepdims=True) * rows[3:4, :]
            )
        return carry

    lax.fori_loop(0, pairs, step, 0)


def feature_back(d_feat, first, second, pick_a, pick_b, rows):
    scaled = d_feat * rows[2:3, :]
    return dot_nt((scaled * second).astype(BF16), pick_a) + dot_nt(
        (scaled * first).astype(BF16), pick_b
    )


def attend_back_body(
    query,
    keys,
    values,
    mixed,
    inverse,
    d_mixed,
    pick_a,
    pick_b,
    rows,
    state,
    total,
    d_state,
    d_total,
    d_query,
    d_keys,
    d_values,
    q_sum,
    k_sum,
    v_sum,
    between=None,
    block=256,
):
    pairs = values.shape[1] // LANES
    count = keys.shape[0]
    q_sum[...] = jnp.zeros_like(q_sum)
    k_sum[...] = jnp.zeros_like(k_sum)

    def step(pair, carry):
        spot = tile_at(pair)
        d_numer = d_mixed[:, spot].astype(F32) * inverse[:, spot]
        lost = d_numer * mixed[:, spot].astype(F32)
        d_low = d_numer.astype(BF16)
        turned = pltpu.roll(lost, VD, 1)
        vals = values[:, spot]
        for half in range(2):
            head = pair * 2 + half
            place = tile_at(head // 8)
            mine = half_lanes(count, half)
            lanes = head_lanes(count, head % 8)
            d_denom = -jnp.sum(only(mine, lost), axis=1, keepdims=True)
            d_wide = jnp.where(mine, d_numer, -turned).astype(BF16)
            v_wide = jnp.where(mine, vals, jnp.ones_like(vals))
            q_mask = only(lanes, query[:, place])
            k_mask = only(lanes, keys[:, place])
            grads_q, grads_k, grads_v = [], [], []
            for start in range(0, count, block):
                stop = start + block
                score = dot_nt(q_mask[start:stop], k_mask[0:stop]) * 0.25
                d_weight = dot_nt(d_wide[start:stop], v_wide[0:stop])
                d_score = only(causal(block, stop, start, 0), d_weight * (1.0 + score))
                grads_q.append(dot(d_score.astype(BF16), k_mask[0:stop]))
                rest = count - start
                score = dot_nt(k_mask[start:stop], q_mask[start:count]) * 0.25
                mask = causal(rest, block, 0, 0)
                mask = (
                    lax.broadcasted_iota(jnp.int32, (block, rest), 0)
                    <= lax.broadcasted_iota(jnp.int32, (block, rest), 1)
                )
                weight = only(mask, 1.0 + score + 0.5 * score * score)
                d_weight = dot_nt(v_wide[start:stop], d_wide[start:count])
                d_score = only(mask, d_weight * (1.0 + score))
                grads_k.append(dot(d_score.astype(BF16), q_mask[start:count]))
                grads_v.append(dot(weight.astype(BF16), d_low[start:count]))
            first, second = halves_of(q_mask, pick_a[...], pick_b[...], rows[...])
            d_feat = dot(d_low[:, half * VD : (half + 1) * VD], state[head]) + d_denom * total[head]
            inter_q = feature_back(d_feat, first, second, pick_a[...], pick_b[...], rows[...])
            first, second = halves_of(k_mask, pick_a[...], pick_b[...], rows[...])
            feat = (first * second * rows[2:3, :]).astype(BF16)
            d_feat = dot(vals[:, half * VD : (half + 1) * VD], d_state[head]) + d_total[head]
            inter_k = feature_back(d_feat, first, second, pick_a[...], pick_b[...], rows[...])
            inter_v = dot_nt(feat, d_state[head])
            inter_v = jnp.concatenate([inter_v, inter_v], axis=1)
            whole_v = jnp.concatenate(grads_v, axis=0) + inter_v
            v_sum[...] = whole_v if half == 0 else jnp.where(mine, whole_v, v_sum[...])
            q_sum[:, place] += jnp.concatenate(grads_q, axis=0) * 0.25 + only(lanes, inter_q)
            k_sum[:, place] += jnp.concatenate(grads_k, axis=0) * 0.25 + only(lanes, inter_k)
        d_values[:, spot] = v_sum[...].astype(BF16)
        if between is not None:
            between(pair)
        return carry

    lax.fori_loop(0, pairs, step, 0)
    d_query[...] = q_sum[...].astype(BF16)
    d_keys[...] = k_sum[...].astype(BF16)


def call(body, shapes, *operands, scratch=()):
    return pl.pallas_call(
        body,
        out_shape=[jax.ShapeDtypeStruct(shape, kind) for shape, kind in shapes],
        scratch_shapes=list(scratch),
        compiler_params=pltpu.CompilerParams(vmem_limit_bytes=VMEM_LIMIT),
    )(*operands)


def rms_norm(inputs, gain):
    return inputs * lax.rsqrt(jnp.mean(inputs * inputs, axis=-1, keepdims=True) + EPS) * gain


def gated(gate_in, up_in):
    return jax.nn.silu(gate_in) * up_in


def before(parts, axis, reverse=False):
    place = lax.axis_index(axis)
    order = jnp.arange(parts.shape[0])
    chosen = order > place if reverse else order < place
    chosen = chosen.reshape((-1,) + (1,) * (parts.ndim - 1))
    return jnp.sum(jnp.where(chosen, parts.astype(F32), 0.0), axis=0)


MESH_ID = pl.DeviceIdType.MESH


class Place:
    def __init__(self):
        self.dp, self.seq = lax.axis_index("dp"), lax.axis_index("seq")
        self.z, self.y = self.dp // 2, self.dp % 2
        self.x, self.core = self.seq // 2, self.seq % 2
        self.zh, self.zl = self.z // 2, self.z % 2

    def at(self, z=None, y=None, x=None, core=None):
        z = self.z if z is None else z
        y = self.y if y is None else y
        x = self.x if x is None else x
        core = self.core if core is None else core
        return (z * 2 + y, x * 2 + core)

    def mate(self):
        return self.at(core=1 - self.core)

    def across(self, axis):
        return self.at(y=1 - self.y) if axis == "y" else self.at(x=1 - self.x)

    def own(self, axis):
        return self.y if axis == "y" else self.x


def remote(source, target, sent, landed, device):
    return pltpu.make_async_remote_copy(
        src_ref=source,
        dst_ref=target,
        send_sem=sent,
        recv_sem=landed,
        device_id=device,
        device_id_type=MESH_ID,
    )


def enter(place):
    barrier = pltpu.get_barrier_semaphore()
    others = [place.mate(), place.across("x"), place.across("y")]
    for other in (1, 2, 3):
        others.append(place.at(z=jnp.bitwise_xor(place.z, other)))
    for device in others:
        pl.semaphore_signal(barrier, inc=1, device_id=device, device_id_type=MESH_ID)
    pl.semaphore_wait(barrier, len(others))


class Clock:
    def __init__(self):
        self.entries, self.slot = [], 0

    def add(self, run, start=0):
        self.entries.append([max(start, self.slot), run])

    def tick(self):
        for entry in reversed(list(self.entries)):
            if self.slot >= entry[0]:
                pause = next(entry[1], None)
                if pause is None:
                    self.entries.remove(entry)
                else:
                    entry[0] = self.slot + pause
        self.slot += 1

    def drain(self):
        while self.entries:
            self.tick()


def spread_steps(shard, whole, rows, columns, first, sems, place):
    sent, landed, local = sems
    zh, zl = place.zh, place.zl
    every = slice(None)
    third = "x" if first == "y" else "y"

    def grid(one, three):
        return (one, three) if first == "y" else (three, one)

    def block(high, low, one, three, core=None):
        core = place.core if core is None else core
        return whole.at[(high, low) + grid(one, three) + (core, rows, columns)]

    own1, own3 = place.own(first), place.own(third)
    mine = shard.at[rows, columns]

    def keep():
        return pltpu.make_async_copy(mine, block(zh, zl, own1, own3), local)

    def move(ref, spot, device):
        return remote(ref, ref, sent.at[spot], landed.at[spot], device)

    def far(high):
        source = mine
        return remote(
            source, block(high, zl, own1, own3), sent.at[0], landed.at[0],
            place.at(z=jnp.bitwise_xor(place.z, 2)),
        )

    def cross(three):
        return move(block(every, zl, own1, three), 1, place.across(third))

    def near(low):
        return move(block(every, low, own1, every), 2, place.at(z=jnp.bitwise_xor(place.z, 1)))

    def over(one):
        return move(block(every, every, one, every), 3, place.across(first))

    def mate(core):
        return move(block(every, every, every, every, core), 4, place.mate())

    keep().start()
    far(zh).start()
    yield 1
    keep().wait()
    far(1 - zh).wait_recv()
    cross(own3).start()
    yield 1
    cross(1 - own3).wait_recv()
    near(zl).start()
    yield 1
    near(1 - zl).wait_recv()
    over(own1).start()
    yield 2
    over(1 - own1).wait_recv()
    mate(place.core).start()
    yield 1
    mate(1 - place.core).wait_recv()
    far(zh).wait_send()
    cross(own3).wait_send()
    near(zl).wait_send()
    over(own1).wait_send()
    mate(place.core).wait_send()


def added(target, others, lead):
    def step(index, carry):
        spot, rest = [], index
        for size in reversed(lead):
            spot.insert(0, rest % size)
            rest = rest // size
        where = tuple(spot)
        value = target[where]
        for other in others:
            value = value + other[where]
        target[where] = value
        return carry

    lax.fori_loop(0, int(np.prod(lead)), step, 0)


def reduce_steps(source, rows, columns, first, refs, sems, place, put):
    mine, mates, over, near, cross, far = refs
    sent, landed, local = sems
    zh, zl = place.zh, place.zl
    third = "x" if first == "y" else "y"
    own1, own3 = place.own(first), place.own(third)
    every = slice(None)

    def share(core):
        return source.at[every, every, every, every, core, rows, columns]

    def pick(which):
        return mine.at[:, :, which] if first == "y" else mine.at[:, :, :, which]

    def fetch():
        return pltpu.make_async_copy(share(place.core), mine, local)

    def send(ref, target, spot, device):
        return remote(ref, target, sent.at[spot], landed.at[spot], device)

    def to_mate():
        return send(share(1 - place.core), mates, 0, place.mate())

    def to_over():
        return send(pick(1 - own1), over, 1, place.across(first))

    def to_near():
        return send(over.at[:, 1 - zl], near, 2, place.at(z=jnp.bitwise_xor(place.z, 1)))

    def to_cross():
        return send(near.at[:, 1 - own3], cross, 3, place.across(third))

    def to_far():
        return send(cross.at[1 - zh], far, 4, place.at(z=jnp.bitwise_xor(place.z, 2)))

    fetch().start()
    to_mate().start()
    yield 1
    fetch().wait()
    to_mate().wait_recv()
    added(mine, [mates], (2, 2, 2, 2))
    to_over().start()
    yield 2
    to_over().wait_recv()
    added(over, [pick(own1)], (2, 2, 2))
    to_near().start()
    yield 1
    to_over().wait_send()
    to_near().wait_recv()
    added(near, [over.at[:, zl]], (2, 2))
    to_cross().start()
    yield 1
    to_cross().wait_recv()
    added(cross, [near.at[:, own3]], (2,))
    to_far().start()
    yield 1
    to_far().wait_recv()
    put(cross[zh].astype(F32) + far[...].astype(F32))
    to_mate().wait_send()
    to_near().wait_send()
    to_cross().wait_send()
    to_far().wait_send()


def reduce_shapes(rows, columns, count=(), keep=None):
    keep = count if keep is None else keep
    return [
        pltpu.VMEM(keep + (2, 2, 2, 2, rows, columns), BF16),
        pltpu.VMEM(count + (2, 2, 2, 2, rows, columns), BF16),
        pltpu.VMEM(count + (2, 2, 2, rows, columns), BF16),
        pltpu.VMEM(count + (2, 2, rows, columns), BF16),
        pltpu.VMEM(count + (2, rows, columns), BF16),
        pltpu.VMEM(count + (rows, columns), BF16),
    ]


def gain_steps(mine, slots, sent, landed, place):
    partners = [place.mate(), place.across("x"), place.across("y")]
    for other in (1, 2):
        partners.append(place.at(z=jnp.bitwise_xor(place.z, other)))
    for spot, partner in enumerate(partners):

        def swap():
            return remote(mine.at[spot], slots.at[spot], sent.at[spot], landed.at[spot], partner)

        swap().start()
        yield 1
        swap().wait()
        mine[spot + 1] = mine[spot] + slots[spot]


def exchange_steps(state, total, near, far, sent, landed, place, reverse):
    (near_state, near_total), (far_state, far_total) = near, far
    half = state.shape[0] // 2
    giving = place.x == (1 if reverse else 0)
    taking = place.x == (0 if reverse else 1)
    second = place.core == (0 if reverse else 1)

    def to_mate():
        return [
            remote(state, near_state, sent.at[0], landed.at[0], place.mate()),
            remote(total, near_total, sent.at[1], landed.at[1], place.mate()),
        ]

    def move(spot, core, device):
        part = pl.ds(core * half, half)
        return [
            remote(ref.at[part], ref.at[part], sent.at[spot + i], landed.at[spot + i], device)
            for i, ref in enumerate((far_state, far_total))
        ]

    def over():
        return move(2, place.core, place.across("x"))

    def share(core):
        return move(4, core, place.mate())

    for copy in to_mate():
        copy.start()
    yield
    for copy in to_mate():
        copy.wait_recv()

    @pl.when(giving)
    def _():
        def add(index, carry):
            head = place.core * half + index
            far_state[head] = state[head] + near_state[head]
            far_total[head] = total[head] + near_total[head]
            return carry

        lax.fori_loop(0, half, add, 0)
        for copy in over():
            copy.start()

    yield

    @pl.when(taking)
    def _():
        for copy in over():
            copy.wait_recv()
        for copy in share(place.core):
            copy.start()

    yield

    @pl.when(taking)
    def _():
        for copy in share(1 - place.core):
            copy.wait_recv()
        for copy in share(place.core):
            copy.wait_send()

    for copy in to_mate():
        copy.wait_send()

    @pl.when(giving)
    def _():
        for copy in over():
            copy.wait_send()

    def fill(act):
        def one(head, carry):
            state[head], total[head] = act(head)
            return carry

        lax.fori_loop(0, 2 * half, one, 0)

    @pl.when(jnp.logical_and(giving, second))
    def _():
        fill(lambda head: (near_state[head], near_total[head]))

    @pl.when(jnp.logical_and(giving, jnp.logical_not(second)))
    def _():
        fill(lambda head: (jnp.zeros_like(state[head]), jnp.zeros_like(total[head])))

    @pl.when(jnp.logical_and(taking, second))
    def _():
        fill(
            lambda head: (
                far_state[head] + near_state[head],
                far_total[head] + near_total[head],
            )
        )

    @pl.when(jnp.logical_and(taking, jnp.logical_not(second)))
    def _():
        fill(lambda head: (far_state[head], far_total[head]))

    yield


def normalize(value, gain):
    return value * lax.rsqrt(jnp.mean(value * value, axis=-1, keepdims=True) + EPS) * gain


GRID = (2, 2, 2, 2, 2)


def shape(dims, kind):
    return jax.ShapeDtypeStruct(dims, kind)


def padded(columns):
    return -(-columns // FEATS) * FEATS


def front(tokens, gain, wq, wk, wv, wo, gain2, tables, shards3):
    count, width = tokens.shape
    heads = wq.shape[1] // KD
    rows, columns = shards3[0].shape
    full = padded(columns)
    half = full // 2
    tall = rows // 2

    def body(
        tok, gain, wq, wk, wv, wo, gain2, pick_a, pick_b, table, shard0, shard1, shard2,
        whole0, whole1, whole2, normed, query, keys, values, mixed, inverse, state, total,
        middle, low_mlp, near_state, near_total, far_state, far_total, ex_sent, ex_landed,
        wide, sent, landed, local,
    ):
        place = Place()
        enter(place)
        wholes = (whole0, whole1, whole2)
        for spot, shard in enumerate((shard0, shard1, shard2)):
            wide[spot, :, columns:full] = jnp.zeros((rows, full - columns), BF16)
            wide[spot, :, 0:columns] = shard[...]
        clock = Clock()
        order = 0
        for part in range(2):
            for weight in range(3):
                for kind, first in enumerate("xy"):
                    run = spread_steps(
                        wide.at[weight], wholes[weight], pl.ds(kind * tall, tall),
                        pl.ds(part * half, half), first,
                        (sent.at[order], landed.at[order], local.at[order]), place,
                    )
                    clock.add(run, order)
                    order += 1
        clock.tick()
        clock.tick()
        project_body(tok, gain, wq, wk, wv, normed, query, keys, values)
        clock.tick()
        state_body(keys, values, pick_a, pick_b, table, state, total)
        swap = exchange_steps(
            state, total, (near_state, near_total), (far_state, far_total), ex_sent, ex_landed,
            place, False,
        )
        next(swap)
        clock.tick()
        next(swap)
        clock.tick()
        next(swap)
        next(swap)

        def between(pair):
            for spot in (1, 3, 5, 7):

                @pl.when(pair == spot)
                def _():
                    clock.tick()

        attend_body(query, keys, values, pick_a, pick_b, table, state, total, mixed, inverse, between)
        middle[...] = tok[...].astype(F32) + dot(mixed[...], wo[...])
        clock.tick()
        low_mlp[...] = normalize(middle[...], gain2[...]).astype(BF16)
        clock.drain()

    vmem = pl.BlockSpec(memory_space=pltpu.VMEM)
    free = pl.BlockSpec(memory_space=pl.ANY)
    states = ((heads, VD, FEATS), BF16), ((heads, 1, FEATS), F32)
    out_shape = [shape(GRID + (rows, full), BF16)] * 3 + [
        shape((count, width), BF16),
        shape((count, heads * KD), BF16),
        shape((count, heads * KD), BF16),
        shape((count, heads * VD), BF16),
        shape((count, heads * VD), BF16),
        shape((count, heads * VD), F32),
        shape(*states[0]),
        shape(*states[1]),
        shape((count, width), F32),
        shape((count, width), BF16),
    ]
    scratch = [pltpu.VMEM(*entry) for entry in states * 2]
    scratch += [pltpu.SemaphoreType.DMA((6,))] * 2
    scratch += [
        pltpu.VMEM((3, rows, full), BF16),
        pltpu.SemaphoreType.DMA((12, 5)),
        pltpu.SemaphoreType.DMA((12, 5)),
        pltpu.SemaphoreType.DMA((12,)),
    ]
    return pl.pallas_call(
        body,
        out_shape=out_shape,
        in_specs=[vmem] * 13,
        out_specs=[free] * 3 + [vmem] * 10,
        scratch_shapes=scratch,
        compiler_params=pltpu.CompilerParams(
            collective_id=1, has_side_effects=True, vmem_limit_bytes=VMEM_LIMIT
        ),
    )(tokens, gain, wq, wk, wv, wo, gain2, *tables, *shards3)


def rms_back(value, gain, grad):
    scale = lax.rsqrt(jnp.mean(value * value, axis=-1, keepdims=True) + EPS)
    unit = value * scale
    inner = grad * gain
    back = scale * (inner - unit * jnp.mean(inner * unit, axis=-1, keepdims=True))
    return back, jnp.sum(grad * unit, axis=0, keepdims=True)


def feed(low_mlp, out_grad, middle, mixed, wo, gain2, wholes):
    count, width = low_mlp.shape
    depth = wholes[0].shape[0]
    full = wholes[0].shape[1]
    tile = FEATS
    steps = full // tile

    def body(
        low, og, mid, mix, wo, gain2, whole0, whole1, whole2,
        grad0, grad1, grad2, out, d_mixed, d_middle, out_g, gain_part,
        low_t, og_t, acc_out, acc_back, tiles, made, in_sem, out_sem,
    ):
        wholes_in, grads = (whole0, whole1, whole2), (grad0, grad1, grad2)

        def columns(step):
            return pl.ds(pl.multiple_of(step * tile, tile), tile)

        def load(step, slot):
            return [
                pltpu.make_async_copy(ref.at[:, columns(step)], tiles.at[slot, i], in_sem.at[slot, i])
                for i, ref in enumerate(wholes_in)
            ]

        def save(step, slot):
            return [
                pltpu.make_async_copy(made.at[slot, i], ref.at[:, columns(step)], out_sem.at[slot, i])
                for i, ref in enumerate(grads)
            ]

        for copy in load(0, 0):
            copy.start()
        low_t[...] = low[...].T
        og_t[...] = og[...].T
        acc_out[...] = mid[...]
        acc_back[...] = jnp.zeros_like(acc_back)

        def step(index, carry):
            slot = index % 2

            @pl.when(index + 1 < steps)
            def _():
                for copy in load(index + 1, 1 - slot):
                    copy.start()

            for copy in load(index, slot):
                copy.wait()

            @pl.when(index >= 2)
            def _():
                for copy in save(index - 2, slot):
                    copy.wait()

            gate_w, up_w, down_w = (tiles.at[slot, i] for i in range(3))
            gate = dot(low[...], gate_w[...])
            upward = dot(low[...], up_w[...])
            d_hidden = dot(og[...], down_w[...])
            sig = 1.0 / (1.0 + jnp.exp(-gate))
            silu = gate * sig
            hidden = (silu * upward).astype(BF16)
            d_gate = (d_hidden * upward * (sig * (1.0 + gate * (1.0 - sig)))).astype(BF16)
            d_up = (d_hidden * silu).astype(BF16)
            acc_out[...] += dot_nt(hidden, down_w[...])
            acc_back[...] += dot_nt(d_gate, gate_w[...]) + dot_nt(d_up, up_w[...])
            made[slot, 0] = dot(low_t[...], d_gate).astype(BF16)
            made[slot, 1] = dot(low_t[...], d_up).astype(BF16)
            made[slot, 2] = dot(og_t[...], hidden).astype(BF16)
            for copy in save(index, slot):
                copy.start()
            return carry

        lax.fori_loop(0, steps, step, 0)
        out[...] = acc_out[...].astype(BF16)
        back, part = rms_back(mid[...], gain2[...], acc_back[...])
        gain_part[...] = part
        d_middle[...] = og[...].astype(F32) + back
        branch = d_middle[...].astype(BF16)
        out_g[...] = dot_tn(mix[...], branch).astype(BF16)
        d_mixed[...] = dot_nt(branch, wo[...]).astype(BF16)
        for index in (steps - 2, steps - 1):
            for copy in save(index, index % 2):
                copy.wait()

    vmem = pl.BlockSpec(memory_space=pltpu.VMEM)
    free = pl.BlockSpec(memory_space=pl.ANY)
    return pl.pallas_call(
        body,
        out_shape=[shape((depth, full), BF16)] * 3
        + [
            shape((count, width), BF16),
            shape(mixed.shape, BF16),
            shape((count, width), F32),
            shape((mixed.shape[1], width), BF16),
            shape((1, width), F32),
        ],
        in_specs=[vmem] * 6 + [free] * 3,
        out_specs=[free] * 3 + [vmem] * 5,
        scratch_shapes=[
            pltpu.VMEM((width, count), BF16),
            pltpu.VMEM((width, count), BF16),
            pltpu.VMEM((count, width), F32),
            pltpu.VMEM((count, width), F32),
            pltpu.VMEM((2, 3, depth, tile), BF16),
            pltpu.VMEM((2, 3, depth, tile), BF16),
            pltpu.SemaphoreType.DMA((2, 3)),
            pltpu.SemaphoreType.DMA((2, 3)),
        ],
        compiler_params=pltpu.CompilerParams(vmem_limit_bytes=VMEM_LIMIT),
    )(low_mlp, out_grad, middle, mixed, wo, gain2, *wholes)


def back(
    tokens, gain, normed, query, keys, values, mixed, inverse, d_mixed, d_middle, tables,
    state, total, wq, wk, wv, gain_part, ff_grads, out_g, columns,
):
    count, width = tokens.shape
    heads = wq.shape[1] // KD
    full = ff_grads[0].shape[1]
    half = full // 2
    rows = width // 32
    tall = rows // 2
    heads_wide, narrow = heads * VD, heads * KD
    late = heads_wide + 2 * narrow
    kept = 6

    def body(
        tok, gain, normed, query, keys, values, mixed, inverse, d_mixed, d_middle, pick_a, pick_b,
        table, state, total, wq, wk, wv, gain_part, ff0, ff1, ff2, out_g,
        g_ff0, g_ff1, g_ff2, g_out, g_value, g_query, g_keys, g_gain, g_tok,
        d_state, d_total, near_state, near_total, far_state, far_total, ex_sent, ex_landed,
        d_query, d_keys, d_values, q_sum, k_sum, v_sum, late_g,
        gain_mine, gain_slots, gain_sent, gain_landed, *rest,
    ):
        ff_refs, out_refs, late_refs, (sent, landed, local) = rest[:6], rest[6:12], rest[12:18], rest[18:]
        place = Place()
        enter(place)
        clock = Clock()
        order = 0

        def sems(index):
            return sent.at[index], landed.at[index], local.at[index]

        for part in range(2):
            for weight, (source, target) in enumerate(zip((ff0, ff1, ff2), (g_ff0, g_ff1, g_ff2))):
                for kind, first in enumerate("xy"):
                    here = (part * half, min(columns, (part + 1) * half))

                    def put(value, target=target, kind=kind, here=here):
                        target[kind * tall : (kind + 1) * tall, here[0] : here[1]] = value[
                            :, 0 : here[1] - here[0]
                        ]

                    refs = [ff_refs[0].at[order % kept]] + [ref.at[order] for ref in ff_refs[1:]]
                    run = reduce_steps(
                        source, pl.ds(kind * tall, tall), pl.ds(part * half, half), first, refs,
                        sems(order), place, put,
                    )
                    clock.add(run, order)
                    order += 1
        for kind, first in enumerate("xy"):

            def put_out(value, kind=kind):
                g_out[kind * tall : (kind + 1) * tall, :] = value

            run = reduce_steps(
                out_g, pl.ds(kind * tall, tall), slice(None), first,
                [ref.at[kind] for ref in out_refs], sems(order), place, put_out,
            )
            clock.add(run, order)
            order += 1
        clock.tick()
        back_state_body(query, mixed, inverse, d_mixed, pick_a, pick_b, table, d_state, d_total)
        swap = exchange_steps(
            d_state, d_total, (near_state, near_total), (far_state, far_total), ex_sent, ex_landed,
            place, True,
        )
        next(swap)
        clock.tick()
        next(swap)
        clock.tick()
        next(swap)
        clock.tick()
        next(swap)

        def between(pair):
            for spot in range(heads // 2):

                @pl.when(pair == spot)
                def _():
                    clock.tick()

        attend_back_body(
            query, keys, values, mixed, inverse, d_mixed, pick_a, pick_b, table, state, total,
            d_state, d_total, d_query, d_keys, d_values, q_sum, k_sum, v_sum, between,
        )
        grid = GRID + (rows,)
        for start, ref in ((0, d_values), (heads_wide, d_query), (heads_wide + narrow, d_keys)):
            wide = ref.shape[1]
            late_g[:, :, :, :, :, :, start : start + wide] = (
                dot_tn(normed[...], ref[...]).astype(BF16).reshape(grid + (wide,))
            )
        for kind, first in enumerate("xy"):

            def put_late(value, kind=kind):
                where = slice(kind * tall, (kind + 1) * tall)
                g_value[where, :] = value[:, 0:heads_wide]
                g_query[where, :] = value[:, heads_wide : heads_wide + narrow]
                g_keys[where, :] = value[:, heads_wide + narrow : late]

            run = reduce_steps(
                late_g, pl.ds(kind * tall, tall), slice(None), first,
                [ref.at[kind] for ref in late_refs], sems(order), place, put_late,
            )
            clock.add(run)
            order += 1
        clock.tick()
        d_normed = dot_nt(d_query[...], wq[...])
        d_normed += dot_nt(d_keys[...], wk[...]) + dot_nt(d_values[...], wv[...])
        value, part = rms_back(tok[...].astype(F32), gain[...], d_normed)
        g_tok[...] = d_middle[...] + value
        gain_mine[0] = jnp.concatenate(
            [part, gain_part[...], jnp.zeros((6, width), F32)], axis=0
        )
        clock.add(gain_steps(gain_mine, gain_slots, gain_sent, gain_landed, place))
        clock.drain()
        g_gain[...] = gain_mine[5]

    vmem = pl.BlockSpec(memory_space=pltpu.VMEM)
    free = pl.BlockSpec(memory_space=pl.ANY)
    states = ((heads, VD, FEATS), BF16), ((heads, 1, FEATS), F32)
    views = [g.reshape(GRID + (rows, g.shape[1])) for g in (*ff_grads, out_g)]
    chunks = 16
    scratch = [pltpu.VMEM(*entry) for entry in states * 3]
    scratch += [pltpu.SemaphoreType.DMA((6,))] * 2
    scratch += [
        pltpu.VMEM((count, narrow), BF16),
        pltpu.VMEM((count, narrow), BF16),
        pltpu.VMEM((count, heads_wide), BF16),
        pltpu.VMEM((count, narrow), F32),
        pltpu.VMEM((count, narrow), F32),
        pltpu.VMEM((count, LANES), F32),
        pltpu.VMEM(GRID + (rows, late), BF16),
        pltpu.VMEM((6, 8, width), F32),
        pltpu.VMEM((5, 8, width), F32),
        pltpu.SemaphoreType.DMA((5,)),
        pltpu.SemaphoreType.DMA((5,)),
    ]
    scratch += reduce_shapes(tall, half, (12,), (kept,))
    scratch += reduce_shapes(tall, width, (2,))
    scratch += reduce_shapes(tall, late, (2,))
    scratch += [
        pltpu.SemaphoreType.DMA((chunks, 5)),
        pltpu.SemaphoreType.DMA((chunks, 5)),
        pltpu.SemaphoreType.DMA((chunks,)),
    ]
    return pl.pallas_call(
        body,
        out_shape=[shape((rows, columns), F32)] * 3
        + [
            shape((rows, width), F32),
            shape((rows, heads_wide), F32),
            shape((rows, narrow), F32),
            shape((rows, narrow), F32),
            shape((8, width), F32),
            shape((count, width), F32),
        ],
        in_specs=[vmem] * 19 + [free] * 4,
        out_specs=[vmem] * 9,
        scratch_shapes=scratch,
        compiler_params=pltpu.CompilerParams(
            collective_id=0, has_side_effects=True, vmem_limit_bytes=VMEM_LIMIT
        ),
    )(
        tokens, gain, normed, query, keys, values, mixed, inverse, d_mixed, d_middle, *tables,
        state, total, wq, wk, wv, gain_part, *views,
    )


def general(
    tokens, attn_gain, w_query, w_key, w_value, w_output, mlp_gain, w_gate, w_up, w_down, out_grad
):
    count, width = tokens.shape
    heads = w_query.shape[1] // KD
    all_values = heads * VD
    tables = feature_tables()
    inputs = tokens.astype(F32)
    gain = attn_gain.astype(F32).reshape(1, width)
    gate_full, up_full, down_full = (
        lax.all_gather(w, ("dp", "seq"), axis=0, tiled=True) for w in (w_gate, w_up, w_down)
    )
    normed, query, keys, values = call(
        project_body,
        [
            ((count, width), BF16),
            ((count, heads * KD), BF16),
            ((count, heads * KD), BF16),
            ((count, all_values), BF16),
        ],
        tokens,
        gain,
        w_query,
        w_key,
        w_value,
    )
    state_shapes = [((heads, VD, FEATS), BF16), ((heads, 1, FEATS), F32)]
    state, total = call(state_body, state_shapes, keys, values, *tables)
    state = before(lax.all_gather(state, "seq"), "seq").astype(BF16)
    total = before(lax.all_gather(total, "seq"), "seq")
    mixed, inverse = call(
        attend_body,
        [((count, all_values), BF16), ((count, all_values), F32)],
        query,
        keys,
        values,
        *tables,
        state,
        total,
    )
    middle = inputs + dot(mixed, w_output)
    normed_mlp, second_back = jax.vjp(rms_norm, middle, mlp_gain.astype(F32))
    mlp_low = normed_mlp.astype(BF16)
    gate = dot(mlp_low, gate_full)
    upward = dot(mlp_low, up_full)
    hidden_val, gated_back = jax.vjp(gated, gate, upward)
    hidden = hidden_val.astype(BF16)
    layer_out = (middle + dot_nt(hidden, down_full)).astype(BF16)
    d_hidden = dot(out_grad, down_full)
    down_grad = dot_tn(out_grad, hidden).astype(BF16)
    d_gate_f, d_up_f = gated_back(d_hidden)
    d_gate = d_gate_f.astype(BF16)
    d_up = d_up_f.astype(BF16)
    gate_grad = dot_tn(mlp_low, d_gate).astype(BF16)
    up_grad = dot_tn(mlp_low, d_up).astype(BF16)
    d_normed_mlp = dot_nt(d_gate, gate_full) + dot_nt(d_up, up_full)
    d_middle_norm, mlp_gain_part = second_back(d_normed_mlp)
    d_middle = out_grad.astype(F32) + d_middle_norm
    d_branch = d_middle.astype(BF16)
    output_grad = dot_tn(mixed, d_branch).astype(BF16)
    d_mixed = dot_nt(d_branch, w_output).astype(BF16)
    d_state, d_total = call(
        back_state_body, state_shapes, query, mixed, inverse, d_mixed, *tables
    )
    d_state = before(lax.all_gather(d_state, "seq"), "seq", True).astype(BF16)
    d_total = before(lax.all_gather(d_total, "seq"), "seq", True)
    d_query, d_keys, d_values = call(
        attend_back_body,
        [
            ((count, heads * KD), BF16),
            ((count, heads * KD), BF16),
            ((count, all_values), BF16),
        ],
        query,
        keys,
        values,
        mixed,
        inverse,
        d_mixed,
        *tables,
        state,
        total,
        d_state,
        d_total,
        scratch=[
            pltpu.VMEM((count, heads * KD), F32),
            pltpu.VMEM((count, heads * KD), F32),
            pltpu.VMEM((count, LANES), F32),
        ],
    )
    d_normed = dot_nt(d_query, w_query) + dot_nt(d_keys, w_key) + dot_nt(d_values, w_value)
    query_grad = dot_tn(normed, d_query).astype(BF16)
    key_grad = dot_tn(normed, d_keys).astype(BF16)
    value_grad = dot_tn(normed, d_values).astype(BF16)
    _, first_back = jax.vjp(rms_norm, inputs, attn_gain.astype(F32))
    d_inputs_norm, attn_gain_part = first_back(d_normed)
    tokens_grad = d_middle + d_inputs_norm
    parts = [query_grad, key_grad, value_grad, output_grad, gate_grad, up_grad, down_grad]
    joined = lax.psum_scatter(
        jnp.concatenate(parts, axis=1), ("dp", "seq"), scatter_dimension=0, tiled=True
    ).astype(F32)
    edges = np.cumsum([part.shape[1] for part in parts])[:-1]
    query_grad, key_grad, value_grad, output_grad, gate_grad, up_grad, down_grad = jnp.split(
        joined, edges, axis=1
    )
    gains = lax.psum_scatter(
        jnp.stack([attn_gain_part, mlp_gain_part], axis=1),
        ("dp", "seq"),
        scatter_dimension=0,
        tiled=True,
    )
    return (
        layer_out,
        tokens_grad,
        gains[:, 0],
        query_grad,
        key_grad,
        value_grad,
        output_grad,
        gains[:, 1],
        gate_grad,
        up_grad,
        down_grad,
    )


def shards(
    tokens, attn_gain, w_query, w_key, w_value, w_output, mlp_gain, w_gate, w_up, w_down, out_grad
):
    args = (
        tokens, attn_gain, w_query, w_key, w_value, w_output, mlp_gain, w_gate, w_up, w_down, out_grad
    )
    if (lax.axis_size("dp"), lax.axis_size("seq")) != (8, 4):
        return general(*args)
    width = tokens.shape[1]
    tables = feature_tables()
    gain = attn_gain.astype(F32).reshape(1, width)
    gain2 = mlp_gain.astype(F32).reshape(1, width)
    (
        *wholes, normed, query, keys, values, mixed, inverse, state, total, middle, low_mlp
    ) = front(
        tokens, gain, w_query, w_key, w_value, w_output, gain2, tables, (w_gate, w_up, w_down)
    )
    wholes = [whole.reshape(width, whole.shape[-1]) for whole in wholes]
    *ff_grads, layer_out, d_mixed, d_middle, out_g, gain_part = feed(
        low_mlp, out_grad, middle, mixed, w_output, gain2, wholes
    )
    gate_grad, up_grad, down_grad, output_grad, value_grad, query_grad, key_grad, gains, tok_grad = back(
        tokens, gain, normed, query, keys, values, mixed, inverse, d_mixed, d_middle, tables,
        state, total, w_query, w_key, w_value, gain_part, ff_grads, out_g, w_gate.shape[1],
    )
    share = width // 32
    own = lax.axis_index("dp") * 4 + lax.axis_index("seq")
    gains = lax.dynamic_slice(gains, (0, own * share), (2, share))
    return (
        layer_out,
        tok_grad,
        gains[0],
        query_grad,
        key_grad,
        value_grad,
        output_grad,
        gains[1],
        gate_grad,
        up_grad,
        down_grad,
    )


def solution(mesh):
    rows = P(("dp", "seq"), None)
    in_specs = (rows, P(), P(), P(), P(), P(), P(), rows, rows, rows, rows)
    out_specs = (
        rows,
        rows,
        P(("dp", "seq")),
        rows,
        rows,
        rows,
        rows,
        P(("dp", "seq")),
        rows,
        rows,
        rows,
    )
    return jax.shard_map(
        shards, mesh=mesh, in_specs=in_specs, out_specs=out_specs, check_vma=False
    )
```

```python
import math

import jax
import jax.numpy as jnp
import numpy as np
from jax import lax
from jax.experimental import pallas as pl
from jax.experimental.pallas import tpu as pltpu
from jax.sharding import PartitionSpec as P

KD = 16
VD = 64
LANES = 128
FEATS = 256
EPS = 1e-05
QUAD = 1.0 / (4.0 * math.sqrt(2.0))
F32 = jnp.float32
BF16 = jnp.bfloat16
VMEM_LIMIT = 62 << 20


def feature_tables():
    pick_a = np.zeros((LANES, FEATS), np.float32)
    pick_b = np.zeros((LANES, FEATS), np.float32)
    rows = np.zeros((8, FEATS), np.float32)
    spot = 0
    for a in range(KD):
        for b in range(a, KD):
            pick_a[a::KD, spot] = 1.0
            pick_b[b::KD, spot] = 1.0
            rows[2, spot] = QUAD
            rows[3, spot] = 1.0 if a == b else 2.0
            spot += 1
    for a in range(KD):
        pick_a[a::KD, spot] = 1.0
        rows[1, spot] = 1.0
        rows[2, spot] = 0.5
        rows[3, spot] = 1.0
        spot += 1
    rows[0:4, spot] = 1.0
    return jnp.asarray(pick_a, BF16), jnp.asarray(pick_b, BF16), jnp.asarray(rows)


def dot(left, right):
    return jnp.dot(left, right, preferred_element_type=F32)


def dot_nt(left, right):
    return lax.dot_general(left, right, (((1,), (1,)), ((), ())), preferred_element_type=F32)


def dot_tn(left, right):
    return lax.dot_general(left, right, (((0,), (0,)), ((), ())), preferred_element_type=F32)


def tile_at(index):
    return pl.ds(pl.multiple_of(index * LANES, LANES), LANES)


def head_lanes(rows, spot):
    return lax.broadcasted_iota(jnp.int32, (rows, LANES), 1) // KD == spot


def half_lanes(rows, half):
    return lax.broadcasted_iota(jnp.int32, (rows, LANES), 1) // VD == half


def halves_of(masked, pick_a, pick_b, rows):
    first = dot(masked, pick_a) + rows[0:1, :]
    second = dot(masked, pick_b) + rows[1:2, :]
    return first, second


def features_of(masked, pick_a, pick_b, rows):
    first, second = halves_of(masked, pick_a, pick_b, rows)
    return (first * second * rows[2:3, :]).astype(BF16)


def only(mask, value):
    return jnp.where(mask, value, jnp.zeros_like(value))


def project_body(tok, gain, wq, wk, wv, normed, query, keys, values):
    x = tok[...].astype(F32)
    scale = lax.rsqrt(jnp.mean(x * x, axis=-1, keepdims=True) + EPS)
    normed[...] = (x * scale * gain[...]).astype(BF16)
    query[...] = dot(normed[...], wq[...]).astype(BF16)
    keys[...] = dot(normed[...], wk[...]).astype(BF16)
    values[...] = dot(normed[...], wv[...]).astype(BF16)


def state_body(keys, values, pick_a, pick_b, rows, state, total, between=None):
    pairs = values.shape[1] // LANES
    count = keys.shape[0]

    def step(pair, carry):
        turned = values[:, tile_at(pair)].T
        for half in range(2):
            head = pair * 2 + half
            masked = only(head_lanes(count, head % 8), keys[:, tile_at(head // 8)])
            feat = features_of(masked, pick_a[...], pick_b[...], rows[...])
            sums = dot(turned[half * VD : (half + 1) * VD, :], feat)
            state[head] = (sums * rows[3:4, :]).astype(BF16)
            total[head] = jnp.sum(feat.astype(F32), axis=0, keepdims=True) * rows[3:4, :]
        if between is not None:
            between(pair)
        return carry

    lax.fori_loop(0, pairs, step, 0)


def causal(rows, columns, row_start, column_start):
    row = lax.broadcasted_iota(jnp.int32, (rows, columns), 0) + row_start
    column = lax.broadcasted_iota(jnp.int32, (rows, columns), 1) + column_start
    return row >= column


def attend_body(query, keys, values, pick_a, pick_b, rows, state, total, mixed, inverse, between=None, block=256):
    pairs = values.shape[1] // LANES
    count = keys.shape[0]

    def step(pair, carry):
        vals = values[:, tile_at(pair)]
        for start in range(0, count, block):
            stop = start + block
            numer = None
            for half in range(2):
                head = pair * 2 + half
                masked = only(head_lanes(block, head % 8), query[start:stop, tile_at(head // 8)])
                score = dot_nt(masked, keys[0:stop, tile_at(head // 8)]) * 0.25
                weight = 1.0 + score + 0.5 * score * score
                weight = jnp.where(causal(block, stop, start, 0), weight, 0.0)
                feat = features_of(masked, pick_a[...], pick_b[...], rows[...])
                inter = feat.astype(F32) * total[head]
                denom = jnp.sum(weight, axis=1, keepdims=True) + jnp.sum(
                    inter, axis=1, keepdims=True
                )
                across = dot_nt(feat, state[head])
                both = dot(weight.astype(BF16), vals[0:stop, :])
                across = jnp.concatenate([across, across], axis=1)
                whole = (both + across) / denom
                flip = jnp.broadcast_to(1.0 / denom, (block, LANES))
                if half == 0:
                    numer, invs = whole, flip
                else:
                    mask = half_lanes(block, 0)
                    numer = jnp.where(mask, numer, whole)
                    invs = jnp.where(mask, invs, flip)
            mixed[start:stop, tile_at(pair)] = numer.astype(BF16)
            inverse[start:stop, tile_at(pair)] = invs
        if between is not None:
            between(pair)
        return carry

    lax.fori_loop(0, pairs, step, 0)


def attend_inside(query, keys, values, numer, denoms, between, block=256):
    pairs = values.shape[1] // LANES
    count = keys.shape[0]

    def step(pair, carry):
        vals = values[:, tile_at(pair)]
        for start in range(0, count, block):
            stop = start + block
            for half in range(2):
                head = pair * 2 + half
                masked = only(head_lanes(block, head % 8), query[start:stop, tile_at(head // 8)])
                score = dot_nt(masked, keys[0:stop, tile_at(head // 8)]) * 0.25
                weight = 1.0 + score + 0.5 * score * score
                weight = jnp.where(causal(block, stop, start, 0), weight, 0.0)
                flip = jnp.broadcast_to(jnp.sum(weight, axis=1, keepdims=True), (block, LANES))
                both = dot(weight.astype(BF16), vals[0:stop, :])
                if half == 0:
                    whole, wides = both, flip
                else:
                    mask = half_lanes(block, 0)
                    numer[start:stop, tile_at(pair)] = jnp.where(mask, whole, both)
                    denoms[start:stop, tile_at(pair)] = jnp.where(mask, wides, flip)
        between(pair)
        return carry

    lax.fori_loop(0, pairs, step, 0)


def attend_before(query, pick_a, pick_b, rows, state, total, numer, inverse, mixed, between):
    count = query.shape[0]
    pairs = mixed.shape[1] // LANES

    def step(pair, carry):
        spot = tile_at(pair)
        for half in range(2):
            head = pair * 2 + half
            masked = only(head_lanes(count, head % 8), query[:, tile_at(head // 8)])
            feat = features_of(masked, pick_a[...], pick_b[...], rows[...])
            inter = jnp.sum(feat.astype(F32) * total[head], axis=1, keepdims=True)
            inter = jnp.broadcast_to(inter, (count, LANES))
            across = dot_nt(feat, state[head])
            across = jnp.concatenate([across, across], axis=1)
            if half == 0:
                whole, wides = across, inter
            else:
                mask = half_lanes(count, 0)
                whole = jnp.where(mask, whole, across)
                wides = jnp.where(mask, wides, inter)
        flipped = 1.0 / (inverse[:, spot] + wides)
        inverse[:, spot] = flipped
        mixed[:, spot] = ((numer[:, spot] + whole) * flipped).astype(BF16)
        between(pair)
        return carry

    lax.fori_loop(0, pairs, step, 0)


def back_state_body(query, mixed, inverse, d_mixed, pick_a, pick_b, rows, d_state, d_total, between=None):
    pairs = mixed.shape[1] // LANES
    count = query.shape[0]

    def step(pair, carry):
        spot = tile_at(pair)
        d_numer = d_mixed[:, spot].astype(F32) * inverse[:, spot]
        lost = d_numer * mixed[:, spot].astype(F32)
        turned = d_numer.astype(BF16).T
        for half in range(2):
            head = pair * 2 + half
            masked = only(head_lanes(count, head % 8), query[:, tile_at(head // 8)])
            feat = features_of(masked, pick_a[...], pick_b[...], rows[...])
            d_denom = -jnp.sum(only(half_lanes(count, half), lost), axis=1, keepdims=True)
            sums = dot(turned[half * VD : (half + 1) * VD, :], feat)
            d_state[head] = (sums * rows[3:4, :]).astype(BF16)
            d_total[head] = (
                jnp.sum(feat.astype(F32) * d_denom, axis=0, keepdims=True) * rows[3:4, :]
            )
        if between is not None:
            between(pair)
        return carry

    lax.fori_loop(0, pairs, step, 0)


def feature_back(d_feat, first, second, pick_a, pick_b, rows):
    scaled = d_feat * rows[2:3, :]
    return dot_nt((scaled * second).astype(BF16), pick_a) + dot_nt(
        (scaled * first).astype(BF16), pick_b
    )


def attend_back_body(
    query,
    keys,
    values,
    mixed,
    inverse,
    d_mixed,
    pick_a,
    pick_b,
    rows,
    state,
    total,
    d_state,
    d_total,
    d_query,
    d_keys,
    d_values,
    q_sum,
    k_sum,
    v_sum,
    between=None,
    block=256,
):
    pairs = values.shape[1] // LANES
    count = keys.shape[0]
    q_sum[...] = jnp.zeros_like(q_sum)
    k_sum[...] = jnp.zeros_like(k_sum)

    def step(pair, carry):
        spot = tile_at(pair)
        d_numer = d_mixed[:, spot].astype(F32) * inverse[:, spot]
        lost = d_numer * mixed[:, spot].astype(F32)
        d_low = d_numer.astype(BF16)
        turned = pltpu.roll(lost, VD, 1)
        vals = values[:, spot]
        for half in range(2):
            head = pair * 2 + half
            place = tile_at(head // 8)
            mine = half_lanes(count, half)
            lanes = head_lanes(count, head % 8)
            d_denom = -jnp.sum(only(mine, lost), axis=1, keepdims=True)
            d_wide = jnp.where(mine, d_numer, -turned).astype(BF16)
            v_wide = jnp.where(mine, vals, jnp.ones_like(vals))
            q_mask = only(lanes, query[:, place])
            k_mask = only(lanes, keys[:, place])
            grads_q, grads_k, grads_v = [], [], []
            for start in range(0, count, block):
                stop = start + block
                score = dot_nt(q_mask[start:stop], k_mask[0:stop]) * 0.25
                d_weight = dot_nt(d_wide[start:stop], v_wide[0:stop])
                d_score = only(causal(block, stop, start, 0), d_weight * (1.0 + score))
                grads_q.append(dot(d_score.astype(BF16), k_mask[0:stop]))
                rest = count - start
                score = dot_nt(k_mask[start:stop], q_mask[start:count]) * 0.25
                mask = causal(rest, block, 0, 0)
                mask = (
                    lax.broadcasted_iota(jnp.int32, (block, rest), 0)
                    <= lax.broadcasted_iota(jnp.int32, (block, rest), 1)
                )
                weight = only(mask, 1.0 + score + 0.5 * score * score)
                d_weight = dot_nt(v_wide[start:stop], d_wide[start:count])
                d_score = only(mask, d_weight * (1.0 + score))
                grads_k.append(dot(d_score.astype(BF16), q_mask[start:count]))
                grads_v.append(dot(weight.astype(BF16), d_low[start:count]))
            first, second = halves_of(q_mask, pick_a[...], pick_b[...], rows[...])
            d_feat = dot(d_low[:, half * VD : (half + 1) * VD], state[head]) + d_denom * total[head]
            inter_q = feature_back(d_feat, first, second, pick_a[...], pick_b[...], rows[...])
            first, second = halves_of(k_mask, pick_a[...], pick_b[...], rows[...])
            feat = (first * second * rows[2:3, :]).astype(BF16)
            d_feat = dot(vals[:, half * VD : (half + 1) * VD], d_state[head]) + d_total[head]
            inter_k = feature_back(d_feat, first, second, pick_a[...], pick_b[...], rows[...])
            inter_v = dot_nt(feat, d_state[head])
            inter_v = jnp.concatenate([inter_v, inter_v], axis=1)
            whole_v = jnp.concatenate(grads_v, axis=0) + inter_v
            v_sum[...] = whole_v if half == 0 else jnp.where(mine, whole_v, v_sum[...])
            q_sum[:, place] += jnp.concatenate(grads_q, axis=0) * 0.25 + only(lanes, inter_q)
            k_sum[:, place] += jnp.concatenate(grads_k, axis=0) * 0.25 + only(lanes, inter_k)
        d_values[:, spot] = v_sum[...].astype(BF16)
        if between is not None:
            between(pair)
        return carry

    lax.fori_loop(0, pairs, step, 0)
    d_query[...] = q_sum[...].astype(BF16)
    d_keys[...] = k_sum[...].astype(BF16)


def attend_back_inside(
    query, keys, values, mixed, inverse, d_mixed, pick_a, pick_b, rows, state, total, q_sum, k_sum,
    v_part, between, block=256,
):
    pairs = values.shape[1] // LANES
    count = keys.shape[0]
    q_sum[...] = jnp.zeros_like(q_sum)
    k_sum[...] = jnp.zeros_like(k_sum)

    def step(pair, carry):
        spot = tile_at(pair)
        d_numer = d_mixed[:, spot].astype(F32) * inverse[:, spot]
        lost = d_numer * mixed[:, spot].astype(F32)
        d_low = d_numer.astype(BF16)
        turned = pltpu.roll(lost, VD, 1)
        vals = values[:, spot]
        for half in range(2):
            head = pair * 2 + half
            place = tile_at(head // 8)
            mine = half_lanes(count, half)
            lanes = head_lanes(count, head % 8)
            d_denom = -jnp.sum(only(mine, lost), axis=1, keepdims=True)
            d_wide = jnp.where(mine, d_numer, -turned).astype(BF16)
            v_wide = jnp.where(mine, vals, jnp.ones_like(vals))
            q_mask = only(lanes, query[:, place])
            k_mask = only(lanes, keys[:, place])
            grads_q, grads_k, grads_v = [], [], []
            for start in range(0, count, block):
                stop = start + block
                score = dot_nt(q_mask[start:stop], k_mask[0:stop]) * 0.25
                d_weight = dot_nt(d_wide[start:stop], v_wide[0:stop])
                d_score = only(causal(block, stop, start, 0), d_weight * (1.0 + score))
                grads_q.append(dot(d_score.astype(BF16), k_mask[0:stop]))
                rest = count - start
                score = dot_nt(k_mask[start:stop], q_mask[start:count]) * 0.25
                mask = (
                    lax.broadcasted_iota(jnp.int32, (block, rest), 0)
                    <= lax.broadcasted_iota(jnp.int32, (block, rest), 1)
                )
                weight = only(mask, 1.0 + score + 0.5 * score * score)
                d_weight = dot_nt(v_wide[start:stop], d_wide[start:count])
                d_score = only(mask, d_weight * (1.0 + score))
                grads_k.append(dot(d_score.astype(BF16), q_mask[start:count]))
                grads_v.append(dot(weight.astype(BF16), d_low[start:count]))
            first, second = halves_of(q_mask, pick_a[...], pick_b[...], rows[...])
            d_feat = dot(d_low[:, half * VD : (half + 1) * VD], state[head]) + d_denom * total[head]
            inter_q = feature_back(d_feat, first, second, pick_a[...], pick_b[...], rows[...])
            whole_v = jnp.concatenate(grads_v, axis=0)
            v_part[:, spot] = whole_v if half == 0 else jnp.where(mine, whole_v, v_part[:, spot])
            q_sum[:, place] += jnp.concatenate(grads_q, axis=0) * 0.25 + only(lanes, inter_q)
            k_sum[:, place] += jnp.concatenate(grads_k, axis=0) * 0.25
            between(pair, half)
        return carry

    lax.fori_loop(0, pairs, step, 0)


def attend_back_after(
    keys, values, pick_a, pick_b, rows, d_state, d_total, k_sum, v_part, d_values, between, ended
):
    pairs = values.shape[1] // LANES
    count = keys.shape[0]

    def step(pair, carry):
        spot = tile_at(pair)
        vals = values[:, spot]
        for half in range(2):
            head = pair * 2 + half
            place = tile_at(head // 8)
            lanes = head_lanes(count, head % 8)
            k_mask = only(lanes, keys[:, place])
            first, second = halves_of(k_mask, pick_a[...], pick_b[...], rows[...])
            feat = (first * second * rows[2:3, :]).astype(BF16)
            d_feat = dot(vals[:, half * VD : (half + 1) * VD], d_state[head]) + d_total[head]
            inter_k = feature_back(d_feat, first, second, pick_a[...], pick_b[...], rows[...])
            inter_v = dot_nt(feat, d_state[head])
            inter_v = jnp.concatenate([inter_v, inter_v], axis=1)
            k_sum[:, place] += only(lanes, inter_k)
            whole_v = v_part[:, spot] + inter_v
            mask = half_lanes(count, half)
            whole_v = whole_v if half == 0 else jnp.where(mask, whole_v, v_part[:, spot])
            if half == 0:
                v_part[:, spot] = jnp.where(mask, whole_v, v_part[:, spot])
            else:
                d_values[:, spot] = whole_v.astype(BF16)
            between(pair, half)
        ended(pair)
        return carry

    lax.fori_loop(0, pairs, step, 0)


def call(body, shapes, *operands, scratch=()):
    return pl.pallas_call(
        body,
        out_shape=[jax.ShapeDtypeStruct(shape, kind) for shape, kind in shapes],
        scratch_shapes=list(scratch),
        compiler_params=pltpu.CompilerParams(vmem_limit_bytes=VMEM_LIMIT),
    )(*operands)


def rms_norm(inputs, gain):
    return inputs * lax.rsqrt(jnp.mean(inputs * inputs, axis=-1, keepdims=True) + EPS) * gain


def gated(gate_in, up_in):
    return jax.nn.silu(gate_in) * up_in


def before(parts, axis, reverse=False):
    place = lax.axis_index(axis)
    order = jnp.arange(parts.shape[0])
    chosen = order > place if reverse else order < place
    chosen = chosen.reshape((-1,) + (1,) * (parts.ndim - 1))
    return jnp.sum(jnp.where(chosen, parts.astype(F32), 0.0), axis=0)


MESH_ID = pl.DeviceIdType.MESH


class Place:
    def __init__(self):
        self.dp, self.seq = lax.axis_index("dp"), lax.axis_index("seq")
        self.z, self.y = self.dp // 2, self.dp % 2
        self.x, self.core = self.seq // 2, self.seq % 2
        self.zh, self.zl = self.z // 2, self.z % 2

    def at(self, z=None, y=None, x=None, core=None):
        z = self.z if z is None else z
        y = self.y if y is None else y
        x = self.x if x is None else x
        core = self.core if core is None else core
        return (z * 2 + y, x * 2 + core)

    def mate(self):
        return self.at(core=1 - self.core)

    def across(self, axis):
        return self.at(y=1 - self.y) if axis == "y" else self.at(x=1 - self.x)

    def own(self, axis):
        return self.y if axis == "y" else self.x


def remote(source, target, sent, landed, device):
    return pltpu.make_async_remote_copy(
        src_ref=source,
        dst_ref=target,
        send_sem=sent,
        recv_sem=landed,
        device_id=device,
        device_id_type=MESH_ID,
    )


def enter(place):
    barrier = pltpu.get_barrier_semaphore()
    others = [place.mate(), place.across("x"), place.across("y")]
    for other in (1, 2, 3):
        others.append(place.at(z=jnp.bitwise_xor(place.z, other)))
    for device in others:
        pl.semaphore_signal(barrier, inc=1, device_id=device, device_id_type=MESH_ID)
    pl.semaphore_wait(barrier, len(others))


class Gather:
    def __init__(self, shard, whole, rows, columns, first, sems, place):
        self.shard, self.whole, self.rows, self.columns = shard, whole, rows, columns
        self.first, self.third = first, "x" if first == "y" else "y"
        self.sems, self.place = sems, place

    def block(self, high, low, one, three, core=None):
        core = self.place.core if core is None else core
        grid = (one, three) if self.first == "y" else (three, one)
        return self.whole.at[(high, low) + grid + (core, self.rows, self.columns)]

    def move(self, ref, spot, device, source=None):
        sent, landed, _ = self.sems
        source = ref if source is None else source
        return remote(source, ref, sent.at[spot], landed.at[spot], device)

    def copies(self):
        place, every = self.place, slice(None)
        own1, own3 = place.own(self.first), place.own(self.third)
        mine = self.shard.at[self.rows, self.columns]
        block = self.block
        zh, zl = place.zh, place.zl

        def keep():
            return pltpu.make_async_copy(mine, block(zh, zl, own1, own3), self.sems[2])

        def far(high):
            device = place.at(z=jnp.bitwise_xor(place.z, 2))
            return self.move(block(high, zl, own1, own3), 0, device, mine)

        def cross(three):
            return self.move(block(every, zl, own1, three), 1, place.across(self.third))

        def near(low):
            device = place.at(z=jnp.bitwise_xor(place.z, 1))
            return self.move(block(every, low, own1, every), 2, device)

        def over(one):
            return self.move(block(every, every, one, every), 3, place.across(self.first))

        def mate(core):
            return self.move(block(every, every, every, every, core), 4, place.mate())

        return keep, [
            (far, zh, 1 - zh),
            (cross, own3, 1 - own3),
            (near, zl, 1 - zl),
            (over, own1, 1 - own1),
            (mate, place.core, 1 - place.core),
        ]

    def step(self, index):
        keep, stages = self.copies()
        if index == 0:
            keep().start()
        if index == 1:
            keep().wait()
        if index > 0:
            act, _, theirs = stages[index - 1]
            act(theirs).wait_recv()
        if index < 5:
            act, own, _ = stages[index]
            act(own).start()
        else:
            for act, own, _ in stages:
                act(own).wait_send()


class Pool:
    def __init__(self, refs, sems, free, place, chunks):
        self.refs, self.sems, self.free, self.place, self.chunks = refs, sems, free, place, chunks
        self.kept, self.landing = refs[0].shape[0], refs[1].shape[0]


class Chunk:
    def __init__(self, pool, order, source, rows, columns, first, put):
        self.pool, self.place, self.put = pool, pool.place, put
        self.order = order
        self.source, self.rows, self.columns, self.first = source, rows, columns, first
        self.third = "x" if first == "y" else "y"
        self.width = columns.size

    def ref(self, kind):
        spot = self.order
        if kind == 0:
            spot = spot % self.pool.kept
        if kind == 1:
            spot = spot % self.pool.landing
        return self.pool.refs[kind].at[spot]

    def cut(self, ref):
        return ref.at[(slice(None),) * (len(ref.shape) - 1) + (pl.ds(0, self.width),)]

    def share(self, core):
        every = slice(None)
        return self.source.at[every, every, every, every, core, self.rows, self.columns]

    def pick(self, which):
        mine = self.ref(0)
        return mine.at[:, :, which] if self.first == "y" else mine.at[:, :, :, which]

    def fetch(self):
        return pltpu.make_async_copy(
            self.share(self.place.core), self.cut(self.ref(0)), self.pool.sems[2].at[self.order]
        )

    def send(self, ref, target, spot, device):
        sent, landed = self.pool.sems[0].at[self.order, spot], self.pool.sems[1].at[self.order, spot]
        return remote(ref, self.cut(target), sent, landed, device)

    def to_mate(self):
        return self.send(self.share(1 - self.place.core), self.ref(1), 0, self.place.mate())

    def to_over(self):
        own = self.place.own(self.first)
        return self.send(
            self.cut(self.pick(1 - own)), self.ref(2), 1, self.place.across(self.first)
        )

    def to_near(self):
        place = self.place
        source = self.cut(self.ref(2).at[:, 1 - place.zl])
        return self.send(source, self.ref(3), 2, place.at(z=jnp.bitwise_xor(place.z, 1)))

    def to_cross(self):
        own = self.place.own(self.third)
        source = self.cut(self.ref(3).at[:, 1 - own])
        return self.send(source, self.ref(4), 3, self.place.across(self.third))

    def to_far(self):
        place = self.place
        source = self.cut(self.ref(4).at[1 - place.zh])
        return self.send(source, self.ref(5), 4, place.at(z=jnp.bitwise_xor(place.z, 2)))

    def view(self, ref):
        return self.cut(ref)

    def step(self, index):
        pool, place, order = self.pool, self.place, self.order
        if index == 0:
            if order >= pool.landing:
                pl.semaphore_wait(pool.free, 1)
            self.fetch().start()
            self.to_mate().start()
        elif index == 1:
            self.fetch().wait()
            self.to_mate().wait_recv()
            mine = self.cut(self.ref(0))
            mine[...] = mine[...] + self.cut(self.ref(1))[...]
            if order + pool.landing < pool.chunks:
                pl.semaphore_signal(
                    pool.free, inc=1, device_id=place.mate(), device_id_type=MESH_ID
                )
            self.to_over().start()
        elif index == 2:
            self.to_over().wait()
            over = self.cut(self.ref(2))
            over[...] = over[...] + self.cut(self.pick(place.own(self.first)))[...]
            self.to_near().start()
        elif index == 3:
            self.to_near().wait_recv()
            near = self.cut(self.ref(3))
            near[...] = near[...] + self.cut(self.ref(2).at[:, place.zl])[...]
            self.to_cross().start()
        elif index == 4:
            self.to_cross().wait_recv()
            cross = self.cut(self.ref(4))
            cross[...] = cross[...] + self.cut(self.ref(3).at[:, place.own(self.third)])[...]
            self.to_far().start()
        else:
            self.to_far().wait_recv()
            final = self.cut(self.ref(4).at[place.zh])[...].astype(F32)
            self.put(final + self.cut(self.ref(5))[...].astype(F32))
            self.to_mate().wait_send()
            self.to_near().wait_send()
            self.to_cross().wait_send()
            self.to_far().wait_send()


class Gains:
    def __init__(self, mine, slots, sent, landed, place):
        self.mine, self.slots, self.sent, self.landed, self.place = mine, slots, sent, landed, place

    def swap(self, spot):
        place = self.place
        partner = [
            place.mate,
            lambda: place.across("x"),
            lambda: place.across("y"),
            lambda: place.at(z=jnp.bitwise_xor(place.z, 1)),
            lambda: place.at(z=jnp.bitwise_xor(place.z, 2)),
        ][spot]()
        return remote(
            self.mine.at[spot], self.slots.at[spot], self.sent.at[spot], self.landed.at[spot], partner
        )

    def step(self, index):
        if index > 0:
            self.swap(index - 1).wait()
            self.mine[index] = self.mine[index - 1] + self.slots[index - 1]
        if index < 5:
            self.swap(index).start()


class Exchange:
    def __init__(self, state, total, near, far, sent, landed, place, reverse):
        self.state, self.total, self.near, self.far = state, total, near, far
        self.sent, self.landed, self.place, self.reverse = sent, landed, place, reverse
        self.half = state.shape[0] // 2

    def move(self, source, target, spot, device):
        return remote(source, target, self.sent.at[spot], self.landed.at[spot], device)

    def to_mate(self):
        pairs = zip((self.state, self.total), self.near)
        return [self.move(a, b, i, self.place.mate()) for i, (a, b) in enumerate(pairs)]

    def part(self, spot, core, device):
        part = pl.ds(core * self.half, self.half)
        return [
            self.move(ref.at[part], ref.at[part], spot + i, device) for i, ref in enumerate(self.far)
        ]

    def over(self):
        return self.part(2, self.place.core, self.place.across("x"))

    def share(self, core):
        return self.part(4, core, self.place.mate())

    def step(self, index):
        place, reverse = self.place, self.reverse
        giving = place.x == (1 if reverse else 0)
        taking = place.x == (0 if reverse else 1)
        second = place.core == (0 if reverse else 1)
        state, total = self.state, self.total
        (near_state, near_total), (far_state, far_total) = self.near, self.far
        if index == 0:
            for copy in self.to_mate():
                copy.start()
        elif index == 1:
            for copy in self.to_mate():
                copy.wait_recv()

            @pl.when(giving)
            def _():
                part = pl.ds(place.core * self.half, self.half)
                far_state[part] = state[part] + near_state[part]
                far_total[part] = total[part] + near_total[part]
                for copy in self.over():
                    copy.start()

        elif index == 2:

            @pl.when(taking)
            def _():
                for copy in self.over():
                    copy.wait_recv()
                for copy in self.share(place.core):
                    copy.start()

        else:

            @pl.when(taking)
            def _():
                for copy in self.share(1 - place.core):
                    copy.wait_recv()
                for copy in self.share(place.core):
                    copy.wait_send()

            for copy in self.to_mate():
                copy.wait_send()

            @pl.when(giving)
            def _():
                for copy in self.over():
                    copy.wait_send()

            @pl.when(jnp.logical_and(giving, second))
            def _():
                state[...] = near_state[...]
                total[...] = near_total[...]

            @pl.when(jnp.logical_and(giving, jnp.logical_not(second)))
            def _():
                state[...] = jnp.zeros_like(state)
                total[...] = jnp.zeros_like(total)

            @pl.when(jnp.logical_and(taking, second))
            def _():
                state[...] = far_state[...] + near_state[...]
                total[...] = far_total[...] + near_total[...]

            @pl.when(jnp.logical_and(taking, jnp.logical_not(second)))
            def _():
                state[...] = far_state[...]
                total[...] = far_total[...]


class Work:
    def __init__(self):
        self.kinds = ([], [], [], [])

    def pause(self, name):
        for code in PLAN.get(name, ()):
            self.kinds[code // 1000][code % 1000 // 10].step(code % 10)

    def between(self, prefix, count, halves=False):
        def hook(index, half=""):
            for spot in range(count):
                name = f"{prefix}{spot}{half}"
                if name in PLAN:

                    @pl.when(index == spot)
                    def _():
                        self.pause(name)

        return hook


PLAN = {
    's': (0, 10, 20, 30, 40,),
    'qk': (50, 1, 60,),
    'v': (2, 11, 21,),
    'st0': (31, 70, 80,),
    'st1': (41,),
    'st2': (90,),
    'st3': (51,),
    'st4': (12, 61,),
    'st6': (3,),
    'st7': (22,),
    'e0': (2000,),
    'a0': (71,),
    'a1': (32, 81, 2001,),
    'a3': (42,),
    'a4': (4, 13,),
    'a5': (52, 23,),
    'a6': (5,),
    'a7': (62, 33,),
    'e0w': (72, 91, 14, 2002, 43, 53, 15, 82, 2003,),
    'b1': (34,),
    'b2': (24,),
    'b3': (63, 100,),
    'b4': (92,),
    'b5': (35,),
    'b6': (25,),
    'b7': (73,),
    'po': (54, 110, 120,),
    'nm': (44, 83, 130,),
    'p0': (55, 101, 140, 45,),
    'm0': (74, 93, 150, 160,),
    't0': (64, 102, 111,),
    'm1': (75, 121, 131,),
    't1': (65, 141, 170,),
    'm2': (84, 151, 94, 161, 112, 122, 85, 103, 95, 132, 171, 113, 142, 123, 152, 104, 133, 105, 162, 114, 143, 172, 115,),
    't2': (124,),
    'm3': (153,),
    't3': (125, 134,),
    'm4': (163,),
    't4': (135, 144, 173, 1000, 1010, 1020, 1030,),
    't5': (145, 154, 1001, 1040,),
    'm6': (1011, 164, 1050, 1021, 155, 174, 165, 1031, 1002, 175,),
    't6': (1041,),
    'm7': (1003, 1012,),
    't7': (1022, 1051,),
    'm8': (1013, 1004, 1032,),
    't8': (1042, 1023, 1060, 1070, 1080, 1090,),
    'm9': (1005, 1014, 1052,),
    't9': (1033, 1024, 1061, 1071, 1100, 1110,),
    'm10': (1015, 1034,),
    'ft': (1025, 1035, 1043, 1053, 1081, 1072, 1091,),
    'dm': (1062, 1120, 1130,),
    'c2': (1044,),
    'c3': (1054, 1073,),
    'c5': (1101, 1111,),
    'c6': (1092,),
    'c7': (1045,),
    'e1': (2010,),
    'og': (1055, 1074, 1082, 1063, 1140, 2011, 1150,),
    'd01': (1075, 1112,),
    'd10': (1064, 1083, 1102,),
    'd11': (1093,),
    'd20': (1084, 1113,),
    'd21': (2012, 1065, 1121, 1131, 1160, 1170,),
    'd30': (2013, 1094, 1085, 1114,),
    'd31': (1103,),
    'd40': (1095, 1141, 1151,),
    'd41': (1115, 1132,),
    'd50': (1104,),
    'd51': (1122, 1161, 1180, 1190, 1171,),
    'd61': (1105, 1142, 1200,),
    'd70': (1152, 1210,),
    'd71': (1123, 1133, 1181,),
    'f00': (1191,),
    'f01': (1162,),
    'f11': (1134, 1143, 1153,),
    'f20': (1124, 1201, 1211,),
    'f21': (1172,),
    'la': (1135, 1144, 1154, 1163, 1220, 1230, 1125,),
    'f41': (1182,),
    'f50': (1173, 1192, 1221,),
    'f51': (1145, 1164, 1231,),
    'f60': (1202, 1155,),
    'f61': (1174,),
    'f70': (1183, 1212, 1193,),
    'lb': (1165, 1203, 1240, 1250,),
    'dn': (1175, 1184, 1194, 1204, 1213, 1222, 1241, 1251,),
    'z': (1185, 1195, 1214, 1232, 3000, 1205, 1223, 3001, 1215, 1252, 1242, 3002, 1233, 1224, 3003, 1253, 1234, 1243, 1254, 1225, 3004, 1235, 1244, 1255, 3005, 1245,),
}


def normalize(value, gain):
    return value * lax.rsqrt(jnp.mean(value * value, axis=-1, keepdims=True) + EPS) * gain


GRID = (2, 2, 2, 2, 2)
PARTS = (3, 7, 11)
BAND = 128
TILE = 256


def shape(dims, kind):
    return jax.ShapeDtypeStruct(dims, kind)


def padded(columns):
    return -(-columns // TILE) * TILE


def bands(count, act, size=BAND):
    def step(index, carry):
        act(pl.ds(pl.multiple_of(index * size, size), size))
        return carry

    lax.fori_loop(0, count // size, step, 0)


def rms_back(value, gain, grad):
    scale = lax.rsqrt(jnp.mean(value * value, axis=-1, keepdims=True) + EPS)
    unit = value * scale
    inner = grad * gain
    back = scale * (inner - unit * jnp.mean(inner * unit, axis=-1, keepdims=True))
    return back, jnp.sum(grad * unit, axis=0, keepdims=True)


def front_phase(work, r):
    def norm(band):
        r.normed[band, :] = normalize(r.tok[band, :].astype(F32), r.gain[...]).astype(BF16)

    bands(r.count, norm)
    r.query[...] = dot(r.normed[...], r.wq[...]).astype(BF16)
    r.keys[...] = dot(r.normed[...], r.wk[...]).astype(BF16)
    work.pause("qk")

    def project(band):
        r.values[:, band] = dot(r.normed[...], r.wv[:, band]).astype(BF16)

    bands(r.heads * VD, project, TILE)
    work.pause("v")
    pairs = r.heads // 2
    tables = r.pick_a, r.pick_b, r.table
    state_body(r.keys, r.values, *tables, r.state, r.total, work.between("st", pairs))
    work.pause("e0")
    attend_inside(r.query, r.keys, r.values, r.middle, r.inverse, work.between("a", pairs))
    work.pause("e0w")
    attend_before(
        r.query, *tables, r.state, r.total, r.middle, r.inverse, r.mixed, work.between("b", pairs)
    )

    def project_out(band):
        r.middle[:, band] = r.tok[:, band].astype(F32) + dot(r.mixed[...], r.wo[:, band])

    bands(r.width, project_out, TILE)
    work.pause("po")

    def norm_again(band):
        r.low[band, :] = normalize(r.middle[band, :], r.gain2[...]).astype(BF16)

    bands(r.count, norm_again)
    work.pause("nm")


def feed_phase(work, r, tiles, made, low_t, og_t, acc_out, acc_back, in_sem, out_sem):
    steps = PARTS[-1]

    def columns(step):
        return pl.ds(pl.multiple_of(step * TILE, TILE), TILE)

    def load(step, slot):
        return [
            pltpu.make_async_copy(ref.at[:, columns(step)], tiles.at[slot, i], in_sem.at[slot, i])
            for i, ref in enumerate(r.wholes_flat)
        ]

    def save(step, slot):
        return [
            pltpu.make_async_copy(made.at[slot, i], ref.at[:, columns(step)], out_sem.at[slot, i])
            for i, ref in enumerate(r.grads_flat)
        ]

    low_t[...] = r.low[...].T
    og_t[...] = r.og[...].T
    acc_out[...] = r.middle[...]
    acc_back[...] = jnp.zeros_like(acc_back)
    work.pause("p0")
    for copy in load(0, 0):
        copy.start()
    in_tile, after_tile = work.between("m", steps), work.between("t", steps)

    def step(index, carry):
        slot = index % 2
        for copy in load(index, slot):
            copy.wait()

        @pl.when(index >= 1)
        def _():
            for copy in save(index - 1, 1 - slot):
                copy.wait()

        gate_w, up_w, down_w = (tiles.at[slot, i] for i in range(3))
        gate = dot(r.low[...], gate_w[...])
        upward = dot(r.low[...], up_w[...])
        d_hidden = dot(r.og[...], down_w[...])
        sig = 1.0 / (1.0 + jnp.exp(-gate))
        silu = gate * sig
        hidden = (silu * upward).astype(BF16)
        d_gate = (d_hidden * upward * (sig * (1.0 + gate * (1.0 - sig)))).astype(BF16)
        d_up = (d_hidden * silu).astype(BF16)
        acc_out[...] += dot_nt(hidden, down_w[...])
        in_tile(index)

        @pl.when(index + 1 < steps)
        def _():
            for copy in load(index + 1, 1 - slot):
                copy.start()

        acc_back[...] += dot_nt(d_gate, gate_w[...]) + dot_nt(d_up, up_w[...])
        made[slot, 0] = dot(low_t[...], d_gate).astype(BF16)
        made[slot, 1] = dot(low_t[...], d_up).astype(BF16)
        made[slot, 2] = dot(og_t[...], hidden).astype(BF16)
        for copy in save(index, slot):
            copy.start()
        after_tile(index)
        return carry

    lax.fori_loop(0, steps, step, 0)

    def store_out(band):
        r.out[band, :] = acc_out[band, :].astype(BF16)

    bands(r.count, store_out)
    r.gain_mine[0] = jnp.zeros(r.gain_mine.shape[1:], F32)

    def middle_back(band):
        value, part = rms_back(r.middle[band, :], r.gain2[...], acc_back[band, :])
        r.gain_mine[0, 1:2, :] += part
        value = r.og[band, :].astype(F32) + value
        r.middle[band, :] = value
        r.low[band, :] = value.astype(BF16)

    bands(r.count, middle_back)
    for copy in save(steps - 1, (steps - 1) % 2):
        copy.wait()
    work.pause("ft")

    def mixed_back(band):
        r.d_mixed[:, band] = dot_nt(r.low[...], r.wo[band, :]).astype(BF16)

    bands(r.heads * VD, mixed_back, TILE)
    work.pause("dm")


def back_phase(work, r, d_query, d_keys, d_values, q_sum, k_sum, turned, v_part):
    heads_wide, narrow = r.heads * VD, r.heads * KD
    pairs = r.heads // 2
    tables = r.pick_a, r.pick_b, r.table
    back_state_body(
        r.query, r.mixed, r.inverse, r.d_mixed, *tables, r.d_state, r.d_total,
        work.between("c", pairs),
    )
    work.pause("e1")
    turned[...] = r.mixed[...].T

    def out_grads(band):
        r.out_g[:, band] = dot(turned[...], r.low[:, band]).astype(BF16)

    bands(r.width, out_grads, TILE)
    work.pause("og")
    turned[...] = r.normed[...].T
    attend_back_inside(
        r.query, r.keys, r.values, r.mixed, r.inverse, r.d_mixed, *tables, r.state, r.total,
        q_sum, k_sum, v_part, work.between("d", pairs),
    )
    work.pause("e1w")
    grid = GRID + (r.rows,)

    def late(part):
        v_wide, narrow_half = heads_wide // 2, narrow // 2
        base, at = part * r.late, 0
        q_part = slice(part * narrow_half, (part + 1) * narrow_half)
        d_query[:, q_part] = q_sum[:, q_part].astype(BF16)
        d_keys[:, q_part] = k_sum[:, q_part].astype(BF16)
        for ref, wide in ((d_values, v_wide), (d_query, narrow_half), (d_keys, narrow_half)):
            for start in range(0, wide, TILE):
                size = min(TILE, wide - start)
                low = part * wide + start
                value = dot(turned[...], ref[:, low : low + size]).astype(BF16)
                spot = base + at + start
                r.late_g[:, :, :, :, :, :, spot : spot + size] = value.reshape(grid + (size,))
            at += wide

    def ended(pair):
        @pl.when(pair == pairs // 2 - 1)
        def _():
            late(0)
            work.pause("la")

    attend_back_after(
        r.keys, r.values, *tables, r.d_state, r.d_total, k_sum, v_part, d_values,
        work.between("f", pairs), ended,
    )
    late(1)
    work.pause("lb")

    def back_norm(band):
        v_part[:, band] = (
            dot_nt(d_query[...], r.wq[band, :])
            + dot_nt(d_keys[...], r.wk[band, :])
            + dot_nt(d_values[...], r.wv[band, :])
        )

    bands(r.width, back_norm, TILE)
    work.pause("dn")

    def tokens_back(band):
        value, part = rms_back(r.tok[band, :].astype(F32), r.gain[...], v_part[band, :])
        r.gain_mine[0, 0:1, :] += part
        r.middle[band, :] = r.middle[band, :] + value

    bands(r.count, tokens_back)


class Refs:
    pass


def layer(tokens, gain, wq, wk, wv, wo, gain2, tables, shards3, out_grad):
    count, width = tokens.shape
    heads = wq.shape[1] // KD
    rows, columns = shards3[0].shape
    full = padded(columns)
    tall = rows // 2
    heads_wide, narrow = heads * VD, heads * KD
    late = heads_wide // 2 + narrow
    edges = [0] + [part * TILE for part in PARTS]
    widest = max(late, width // 2, *[high - low for low, high in zip(edges, edges[1:])])
    chunks = 6 * len(PARTS) + 8
    gathers = 6 * len(PARTS)
    states = ((heads, VD, FEATS), BF16), ((heads, 1, FEATS), F32)
    sem = pltpu.SemaphoreType.DMA

    inputs = dict(
        tok=tokens, gain=gain, wq=wq, wk=wk, wv=wv, wo=wo, gain2=gain2, pick_a=tables[0],
        pick_b=tables[1], table=tables[2], shard0=shards3[0], shard1=shards3[1],
        shard2=shards3[2], og=out_grad,
    )
    free_outs = dict(
        whole0=shape((width, full), BF16), whole1=shape((width, full), BF16),
        whole2=shape((width, full), BF16), grad0=shape((width, full), BF16),
        grad1=shape((width, full), BF16), grad2=shape((width, full), BF16),
    )
    outs = dict(
        out=shape((count, width), BF16),
        middle=shape((count, width), F32),
        g0=shape((rows, columns), F32), g1=shape((rows, columns), F32),
        g2=shape((rows, columns), F32), g_out=shape((rows, width), F32),
        g_value=shape((rows, heads_wide), F32), g_query=shape((rows, narrow), F32),
        g_keys=shape((rows, narrow), F32), g_gain=shape((8, width), F32),
    )
    scratch = dict(
        normed=pltpu.VMEM((count, width), BF16),
        query=pltpu.VMEM((count, narrow), BF16),
        keys=pltpu.VMEM((count, narrow), BF16),
        values=pltpu.VMEM((count, heads_wide), BF16),
        mixed=pltpu.VMEM((count, heads_wide), BF16),
        inverse=pltpu.VMEM((count, heads_wide), F32),
        state=pltpu.VMEM(*states[0]), total=pltpu.VMEM(*states[1]),
        d_state=pltpu.VMEM(*states[0]), d_total=pltpu.VMEM(*states[1]),
        near_state=pltpu.VMEM(*states[0]), near_total=pltpu.VMEM(*states[1]),
        far_state=pltpu.VMEM(*states[0]), far_total=pltpu.VMEM(*states[1]),
        ex_sent=sem((6,)), ex_landed=sem((6,)),
        low=pltpu.VMEM((count, width), BF16),
        d_mixed=pltpu.VMEM((count, heads_wide), BF16),
        out_g=pltpu.VMEM((width, width), BF16),
        late_g=pltpu.VMEM(GRID + (rows, 2 * late), BF16),
        wide=pltpu.VMEM((3, rows, full), BF16),
        ag_sent=sem((gathers, 5)), ag_landed=sem((gathers, 5)), ag_local=sem((gathers,)),
        gain_mine=pltpu.VMEM((6, 8, width), F32),
        gain_slots=pltpu.VMEM((5, 8, width), F32),
        gain_sent=sem((5,)), gain_landed=sem((5,)),
        p0=pltpu.VMEM((6, 2, 2, 2, 2, tall, widest), BF16),
        p1=pltpu.VMEM((6, 2, 2, 2, 2, tall, widest), BF16),
        p2=pltpu.VMEM((chunks, 2, 2, 2, tall, widest), BF16),
        p3=pltpu.VMEM((chunks, 2, 2, tall, widest), BF16),
        p4=pltpu.VMEM((chunks, 2, tall, widest), BF16),
        p5=pltpu.VMEM((chunks, tall, widest), BF16),
        rs_sent=sem((chunks, 5)), rs_landed=sem((chunks, 5)), rs_local=sem((chunks,)),
        credit=pltpu.SemaphoreType.REGULAR,
    )
    names = list(inputs) + list(free_outs) + list(outs) + list(scratch)

    def body(*refs):
        r = Refs()
        for name, ref in zip(names, refs):
            setattr(r, name, ref)
        r.count, r.width, r.heads, r.rows, r.late = count, width, heads, rows, late
        r.place = place = Place()
        r.wholes_flat = [r.whole0, r.whole1, r.whole2]
        r.grads_flat = [r.grad0, r.grad1, r.grad2]
        grid = GRID + (rows,)
        wholes = [ref.reshape(grid + (full,)) for ref in r.wholes_flat]
        grads = [ref.reshape(grid + (full,)) for ref in r.grads_flat]
        enter(place)
        work = Work()
        gather_list, sum_list, exchange_list, gain_list = work.kinds
        for spot, shard in enumerate((r.shard0, r.shard1, r.shard2)):
            r.wide[spot, :, columns:full] = jnp.zeros((rows, full - columns), BF16)
            r.wide[spot, :, 0:columns] = shard[...]
        for low, high in zip(edges, edges[1:]):
            for weight in range(3):
                for kind, first in enumerate("xy"):
                    order = len(gather_list)
                    gather_list.append(
                        Gather(
                            r.wide.at[weight], wholes[weight], pl.ds(kind * tall, tall),
                            pl.ds(low, high - low), first,
                            (r.ag_sent.at[order], r.ag_landed.at[order], r.ag_local.at[order]), place,
                        )
                    )
        pool = Pool(
            [r.p0, r.p1, r.p2, r.p3, r.p4, r.p5], (r.rs_sent, r.rs_landed, r.rs_local), r.credit,
            place, chunks,
        )

        def sums(source, low, high, target):
            for kind, first in enumerate("xy"):

                def put(value, kind=kind):
                    target(slice(kind * tall, (kind + 1) * tall), value)

                chunk_rows, chunk_columns = pl.ds(kind * tall, tall), pl.ds(low, high - low)
                sum_list.append(
                    Chunk(pool, len(sum_list), source, chunk_rows, chunk_columns, first, put)
                )

        def into(ref, low, high):
            def put(where, value):
                ref[where, low:high] = value[:, 0 : high - low]

            return put

        for low, high in zip(edges, edges[1:]):
            for source, target in zip(grads, (r.g0, r.g1, r.g2)):
                sums(source, low, high, into(target, low, min(high, columns)))
        half = width // 2
        for low in (0, half):
            sums(r.out_g.reshape(grid + (width,)), low, low + half, into(r.g_out, low, low + half))
        v_wide, narrow_half = heads_wide // 2, narrow // 2
        for part in range(2):

            def put_late(where, value, part=part):
                at = 0
                for ref, wide in ((r.g_value, v_wide), (r.g_query, narrow_half), (r.g_keys, narrow_half)):
                    ref[where, part * wide : (part + 1) * wide] = value[:, at : at + wide]
                    at += wide

            sums(r.late_g, part * late, (part + 1) * late, put_late)
        for state, total, reverse in ((r.state, r.total, False), (r.d_state, r.d_total, True)):
            exchange_list.append(
                Exchange(
                    state, total, (r.near_state, r.near_total), (r.far_state, r.far_total),
                    r.ex_sent, r.ex_landed, place, reverse,
                )
            )
        gain_list.append(Gains(r.gain_mine, r.gain_slots, r.gain_sent, r.gain_landed, place))
        work.pause("s")
        front_phase(work, r)
        pl.run_scoped(
            lambda *buffers: feed_phase(work, r, *buffers),
            pltpu.VMEM((2, 3, width, TILE), BF16),
            pltpu.VMEM((2, 3, width, TILE), BF16),
            pltpu.VMEM((width, count), BF16),
            pltpu.VMEM((width, count), BF16),
            pltpu.VMEM((count, width), F32),
            pltpu.VMEM((count, width), F32),
            sem((2, 3)),
            sem((2, 3)),
        )
        pl.run_scoped(
            lambda *buffers: back_phase(work, r, *buffers),
            pltpu.VMEM((count, narrow), BF16),
            pltpu.VMEM((count, narrow), BF16),
            pltpu.VMEM((count, heads_wide), BF16),
            pltpu.VMEM((count, narrow), F32),
            pltpu.VMEM((count, narrow), F32),
            pltpu.VMEM((width, count), BF16),
            pltpu.VMEM((count, width), F32),
        )
        work.pause("z")
        r.g_gain[...] = r.gain_mine[5]

    vmem = pl.BlockSpec(memory_space=pltpu.VMEM)
    free = pl.BlockSpec(memory_space=pl.ANY)
    results = pl.pallas_call(
        body,
        out_shape=list(free_outs.values()) + list(outs.values()),
        in_specs=[vmem] * len(inputs),
        out_specs=[free] * len(free_outs) + [vmem] * len(outs),
        scratch_shapes=list(scratch.values()),
        compiler_params=pltpu.CompilerParams(
            collective_id=0, has_side_effects=True, vmem_limit_bytes=VMEM_LIMIT
        ),
    )(*inputs.values())
    return results[len(free_outs) :]


def general(
    tokens, attn_gain, w_query, w_key, w_value, w_output, mlp_gain, w_gate, w_up, w_down, out_grad
):
    count, width = tokens.shape
    heads = w_query.shape[1] // KD
    all_values = heads * VD
    tables = feature_tables()
    inputs = tokens.astype(F32)
    gain = attn_gain.astype(F32).reshape(1, width)
    gate_full, up_full, down_full = (
        lax.all_gather(w, ("dp", "seq"), axis=0, tiled=True) for w in (w_gate, w_up, w_down)
    )
    normed, query, keys, values = call(
        project_body,
        [
            ((count, width), BF16),
            ((count, heads * KD), BF16),
            ((count, heads * KD), BF16),
            ((count, all_values), BF16),
        ],
        tokens,
        gain,
        w_query,
        w_key,
        w_value,
    )
    state_shapes = [((heads, VD, FEATS), BF16), ((heads, 1, FEATS), F32)]
    state, total = call(state_body, state_shapes, keys, values, *tables)
    state = before(lax.all_gather(state, "seq"), "seq").astype(BF16)
    total = before(lax.all_gather(total, "seq"), "seq")
    mixed, inverse = call(
        attend_body,
        [((count, all_values), BF16), ((count, all_values), F32)],
        query,
        keys,
        values,
        *tables,
        state,
        total,
    )
    middle = inputs + dot(mixed, w_output)
    normed_mlp, second_back = jax.vjp(rms_norm, middle, mlp_gain.astype(F32))
    mlp_low = normed_mlp.astype(BF16)
    gate = dot(mlp_low, gate_full)
    upward = dot(mlp_low, up_full)
    hidden_val, gated_back = jax.vjp(gated, gate, upward)
    hidden = hidden_val.astype(BF16)
    layer_out = (middle + dot_nt(hidden, down_full)).astype(BF16)
    d_hidden = dot(out_grad, down_full)
    down_grad = dot_tn(out_grad, hidden).astype(BF16)
    d_gate_f, d_up_f = gated_back(d_hidden)
    d_gate = d_gate_f.astype(BF16)
    d_up = d_up_f.astype(BF16)
    gate_grad = dot_tn(mlp_low, d_gate).astype(BF16)
    up_grad = dot_tn(mlp_low, d_up).astype(BF16)
    d_normed_mlp = dot_nt(d_gate, gate_full) + dot_nt(d_up, up_full)
    d_middle_norm, mlp_gain_part = second_back(d_normed_mlp)
    d_middle = out_grad.astype(F32) + d_middle_norm
    d_branch = d_middle.astype(BF16)
    output_grad = dot_tn(mixed, d_branch).astype(BF16)
    d_mixed = dot_nt(d_branch, w_output).astype(BF16)
    d_state, d_total = call(
        back_state_body, state_shapes, query, mixed, inverse, d_mixed, *tables
    )
    d_state = before(lax.all_gather(d_state, "seq"), "seq", True).astype(BF16)
    d_total = before(lax.all_gather(d_total, "seq"), "seq", True)
    d_query, d_keys, d_values = call(
        attend_back_body,
        [
            ((count, heads * KD), BF16),
            ((count, heads * KD), BF16),
            ((count, all_values), BF16),
        ],
        query,
        keys,
        values,
        mixed,
        inverse,
        d_mixed,
        *tables,
        state,
        total,
        d_state,
        d_total,
        scratch=[
            pltpu.VMEM((count, heads * KD), F32),
            pltpu.VMEM((count, heads * KD), F32),
            pltpu.VMEM((count, LANES), F32),
        ],
    )
    d_normed = dot_nt(d_query, w_query) + dot_nt(d_keys, w_key) + dot_nt(d_values, w_value)
    query_grad = dot_tn(normed, d_query).astype(BF16)
    key_grad = dot_tn(normed, d_keys).astype(BF16)
    value_grad = dot_tn(normed, d_values).astype(BF16)
    _, first_back = jax.vjp(rms_norm, inputs, attn_gain.astype(F32))
    d_inputs_norm, attn_gain_part = first_back(d_normed)
    tokens_grad = d_middle + d_inputs_norm
    parts = [query_grad, key_grad, value_grad, output_grad, gate_grad, up_grad, down_grad]
    joined = lax.psum_scatter(
        jnp.concatenate(parts, axis=1), ("dp", "seq"), scatter_dimension=0, tiled=True
    ).astype(F32)
    edges = np.cumsum([part.shape[1] for part in parts])[:-1]
    query_grad, key_grad, value_grad, output_grad, gate_grad, up_grad, down_grad = jnp.split(
        joined, edges, axis=1
    )
    gains = lax.psum_scatter(
        jnp.stack([attn_gain_part, mlp_gain_part], axis=1),
        ("dp", "seq"),
        scatter_dimension=0,
        tiled=True,
    )
    return (
        layer_out,
        tokens_grad,
        gains[:, 0],
        query_grad,
        key_grad,
        value_grad,
        output_grad,
        gains[:, 1],
        gate_grad,
        up_grad,
        down_grad,
    )


def shards(
    tokens, attn_gain, w_query, w_key, w_value, w_output, mlp_gain, w_gate, w_up, w_down, out_grad
):
    args = (
        tokens, attn_gain, w_query, w_key, w_value, w_output, mlp_gain, w_gate, w_up, w_down, out_grad
    )
    if (lax.axis_size("dp"), lax.axis_size("seq")) != (8, 4):
        return general(*args)
    width = tokens.shape[1]
    tables = feature_tables()
    gain = attn_gain.astype(F32).reshape(1, width)
    gain2 = mlp_gain.astype(F32).reshape(1, width)
    (
        layer_out, tok_grad, gate_grad, up_grad, down_grad, output_grad, value_grad, query_grad,
        key_grad, gains,
    ) = layer(
        tokens, gain, w_query, w_key, w_value, w_output, gain2, tables, (w_gate, w_up, w_down),
        out_grad,
    )
    share = width // 32
    own = lax.axis_index("dp") * 4 + lax.axis_index("seq")
    gains = lax.dynamic_slice(gains, (0, own * share), (2, share))
    return (
        layer_out,
        tok_grad,
        gains[0],
        query_grad,
        key_grad,
        value_grad,
        output_grad,
        gains[1],
        gate_grad,
        up_grad,
        down_grad,
    )


def solution(mesh):
    rows = P(("dp", "seq"), None)
    in_specs = (rows, P(), P(), P(), P(), P(), P(), rows, rows, rows, rows)
    out_specs = (
        rows,
        rows,
        P(("dp", "seq")),
        rows,
        rows,
        rows,
        rows,
        P(("dp", "seq")),
        rows,
        rows,
        rows,
    )
    return jax.shard_map(
        shards, mesh=mesh, in_specs=in_specs, out_specs=out_specs, check_vma=False
    )
```

```python
import functools
import math

import jax
import jax.numpy as jnp
import numpy as np
from jax import lax
from jax.experimental import pallas as pl
from jax.experimental.pallas import tpu as pltpu
from jax.sharding import PartitionSpec as P

KD = 16
VD = 64
LANES = 128
FEATS = 256
EPS = 1e-05
QUAD = 1.0 / (4.0 * math.sqrt(2.0))
F32 = jnp.float32
BF16 = jnp.bfloat16
VMEM_LIMIT = 62 << 20


def feature_tables():
    pick_a = np.zeros((LANES, FEATS), np.float32)
    pick_b = np.zeros((LANES, FEATS), np.float32)
    rows = np.zeros((8, FEATS), np.float32)
    spot = 0
    for a in range(KD):
        for b in range(a, KD):
            pick_a[a::KD, spot] = 1.0
            pick_b[b::KD, spot] = 1.0
            rows[2, spot] = QUAD
            rows[3, spot] = 1.0 if a == b else 2.0
            spot += 1
    for a in range(KD):
        pick_a[a::KD, spot] = 1.0
        rows[1, spot] = 1.0
        rows[2, spot] = 0.5
        rows[3, spot] = 1.0
        spot += 1
    rows[0:4, spot] = 1.0
    return jnp.asarray(pick_a, BF16), jnp.asarray(pick_b, BF16), jnp.asarray(rows)


def dot(left, right):
    return jnp.dot(left, right, preferred_element_type=F32)


def dot_nt(left, right):
    return lax.dot_general(left, right, (((1,), (1,)), ((), ())), preferred_element_type=F32)


def dot_tn(left, right):
    return lax.dot_general(left, right, (((0,), (0,)), ((), ())), preferred_element_type=F32)


def tile_at(index):
    return pl.ds(pl.multiple_of(index * LANES, LANES), LANES)


def head_lanes(rows, spot):
    return lax.broadcasted_iota(jnp.int32, (rows, LANES), 1) // KD == spot


def half_lanes(rows, half):
    return lax.broadcasted_iota(jnp.int32, (rows, LANES), 1) // VD == half


def halves_of(masked, pick_a, pick_b, rows):
    first = dot(masked, pick_a) + rows[0:1, :]
    second = dot(masked, pick_b) + rows[1:2, :]
    return first, second


def features_of(masked, pick_a, pick_b, rows):
    first, second = halves_of(masked, pick_a, pick_b, rows)
    return (first * second * rows[2:3, :]).astype(BF16)


def only(mask, value):
    return jnp.where(mask, value, jnp.zeros_like(value))


def project_body(tok, gain, wq, wk, wv, normed, query, keys, values):
    x = tok[...].astype(F32)
    scale = lax.rsqrt(jnp.mean(x * x, axis=-1, keepdims=True) + EPS)
    normed[...] = (x * scale * gain[...]).astype(BF16)
    query[...] = dot(normed[...], wq[...]).astype(BF16)
    keys[...] = dot(normed[...], wk[...]).astype(BF16)
    values[...] = dot(normed[...], wv[...]).astype(BF16)


def state_body(keys, values, pick_a, pick_b, rows, state, total, between=None):
    pairs = values.shape[1] // LANES
    count = keys.shape[0]

    def step(pair, carry):
        turned = values[:, tile_at(pair)].T
        for half in range(2):
            head = pair * 2 + half
            masked = only(head_lanes(count, head % 8), keys[:, tile_at(head // 8)])
            feat = features_of(masked, pick_a[...], pick_b[...], rows[...])
            sums = dot(turned[half * VD : (half + 1) * VD, :], feat)
            state[head] = (sums * rows[3:4, :]).astype(BF16)
            total[head] = jnp.sum(feat.astype(F32), axis=0, keepdims=True) * rows[3:4, :]
        if between is not None:
            between(pair)
        return carry

    lax.fori_loop(0, pairs, step, 0)


def causal(rows, columns, row_start, column_start):
    row = lax.broadcasted_iota(jnp.int32, (rows, columns), 0) + row_start
    column = lax.broadcasted_iota(jnp.int32, (rows, columns), 1) + column_start
    return row >= column


def attend_body(query, keys, values, pick_a, pick_b, rows, state, total, mixed, inverse, between=None, block=256):
    pairs = values.shape[1] // LANES
    count = keys.shape[0]

    def step(pair, carry):
        vals = values[:, tile_at(pair)]
        for start in range(0, count, block):
            stop = start + block
            numer = None
            for half in range(2):
                head = pair * 2 + half
                masked = only(head_lanes(block, head % 8), query[start:stop, tile_at(head // 8)])
                score = dot_nt(masked, keys[0:stop, tile_at(head // 8)]) * 0.25
                weight = 1.0 + score + 0.5 * score * score
                weight = jnp.where(causal(block, stop, start, 0), weight, 0.0)
                feat = features_of(masked, pick_a[...], pick_b[...], rows[...])
                inter = feat.astype(F32) * total[head]
                denom = jnp.sum(weight, axis=1, keepdims=True) + jnp.sum(
                    inter, axis=1, keepdims=True
                )
                across = dot_nt(feat, state[head])
                both = dot(weight.astype(BF16), vals[0:stop, :])
                across = jnp.concatenate([across, across], axis=1)
                whole = (both + across) / denom
                flip = jnp.broadcast_to(1.0 / denom, (block, LANES))
                if half == 0:
                    numer, invs = whole, flip
                else:
                    mask = half_lanes(block, 0)
                    numer = jnp.where(mask, numer, whole)
                    invs = jnp.where(mask, invs, flip)
            mixed[start:stop, tile_at(pair)] = numer.astype(BF16)
            inverse[start:stop, tile_at(pair)] = invs
        if between is not None:
            between(pair)
        return carry

    lax.fori_loop(0, pairs, step, 0)


def attend_inside(query, keys, values, numer, denoms, between, block=256):
    pairs = values.shape[1] // LANES
    count = keys.shape[0]

    def step(pair, carry):
        vals = values[:, tile_at(pair)]
        for start in range(0, count, block):
            stop = start + block
            for half in range(2):
                head = pair * 2 + half
                masked = only(head_lanes(block, head % 8), query[start:stop, tile_at(head // 8)])
                score = dot_nt(masked, keys[0:stop, tile_at(head // 8)]) * 0.25
                weight = 1.0 + score + 0.5 * score * score
                weight = jnp.where(causal(block, stop, start, 0), weight, 0.0)
                flip = jnp.broadcast_to(jnp.sum(weight, axis=1, keepdims=True), (block, LANES))
                both = dot(weight.astype(BF16), vals[0:stop, :])
                if half == 0:
                    whole, wides = both, flip
                else:
                    mask = half_lanes(block, 0)
                    numer[start:stop, tile_at(pair)] = jnp.where(mask, whole, both)
                    denoms[start:stop, tile_at(pair)] = jnp.where(mask, wides, flip)
        between(pair)
        return carry

    lax.fori_loop(0, pairs, step, 0)


def attend_before(query, pick_a, pick_b, rows, state, total, numer, inverse, mixed, between):
    count = query.shape[0]
    pairs = mixed.shape[1] // LANES

    def step(pair, carry):
        spot = tile_at(pair)
        for half in range(2):
            head = pair * 2 + half
            masked = only(head_lanes(count, head % 8), query[:, tile_at(head // 8)])
            feat = features_of(masked, pick_a[...], pick_b[...], rows[...])
            inter = jnp.sum(feat.astype(F32) * total[head], axis=1, keepdims=True)
            inter = jnp.broadcast_to(inter, (count, LANES))
            across = dot_nt(feat, state[head])
            across = jnp.concatenate([across, across], axis=1)
            if half == 0:
                whole, wides = across, inter
            else:
                mask = half_lanes(count, 0)
                whole = jnp.where(mask, whole, across)
                wides = jnp.where(mask, wides, inter)
        flipped = 1.0 / (inverse[:, spot] + wides)
        inverse[:, spot] = flipped
        mixed[:, spot] = ((numer[:, spot] + whole) * flipped).astype(BF16)
        between(pair)
        return carry

    lax.fori_loop(0, pairs, step, 0)


def back_state_body(query, mixed, inverse, d_mixed, pick_a, pick_b, rows, d_state, d_total, between=None):
    pairs = mixed.shape[1] // LANES
    count = query.shape[0]

    def step(pair, carry):
        spot = tile_at(pair)
        d_numer = d_mixed[:, spot].astype(F32) * inverse[:, spot]
        lost = d_numer * mixed[:, spot].astype(F32)
        turned = d_numer.astype(BF16).T
        for half in range(2):
            head = pair * 2 + half
            masked = only(head_lanes(count, head % 8), query[:, tile_at(head // 8)])
            feat = features_of(masked, pick_a[...], pick_b[...], rows[...])
            d_denom = -jnp.sum(only(half_lanes(count, half), lost), axis=1, keepdims=True)
            sums = dot(turned[half * VD : (half + 1) * VD, :], feat)
            d_state[head] = (sums * rows[3:4, :]).astype(BF16)
            d_total[head] = (
                jnp.sum(feat.astype(F32) * d_denom, axis=0, keepdims=True) * rows[3:4, :]
            )
        if between is not None:
            between(pair)
        return carry

    lax.fori_loop(0, pairs, step, 0)


def feature_back(d_feat, first, second, pick_a, pick_b, rows):
    scaled = d_feat * rows[2:3, :]
    return dot_nt((scaled * second).astype(BF16), pick_a) + dot_nt(
        (scaled * first).astype(BF16), pick_b
    )


def attend_back_body(
    query,
    keys,
    values,
    mixed,
    inverse,
    d_mixed,
    pick_a,
    pick_b,
    rows,
    state,
    total,
    d_state,
    d_total,
    d_query,
    d_keys,
    d_values,
    q_sum,
    k_sum,
    v_sum,
    between=None,
    block=256,
):
    pairs = values.shape[1] // LANES
    count = keys.shape[0]
    q_sum[...] = jnp.zeros_like(q_sum)
    k_sum[...] = jnp.zeros_like(k_sum)

    def step(pair, carry):
        spot = tile_at(pair)
        d_numer = d_mixed[:, spot].astype(F32) * inverse[:, spot]
        lost = d_numer * mixed[:, spot].astype(F32)
        d_low = d_numer.astype(BF16)
        turned = pltpu.roll(lost, VD, 1)
        vals = values[:, spot]
        for half in range(2):
            head = pair * 2 + half
            place = tile_at(head // 8)
            mine = half_lanes(count, half)
            lanes = head_lanes(count, head % 8)
            d_denom = -jnp.sum(only(mine, lost), axis=1, keepdims=True)
            d_wide = jnp.where(mine, d_numer, -turned).astype(BF16)
            v_wide = jnp.where(mine, vals, jnp.ones_like(vals))
            q_mask = only(lanes, query[:, place])
            k_mask = only(lanes, keys[:, place])
            grads_q, grads_k, grads_v = [], [], []
            for start in range(0, count, block):
                stop = start + block
                score = dot_nt(q_mask[start:stop], k_mask[0:stop]) * 0.25
                d_weight = dot_nt(d_wide[start:stop], v_wide[0:stop])
                d_score = only(causal(block, stop, start, 0), d_weight * (1.0 + score))
                grads_q.append(dot(d_score.astype(BF16), k_mask[0:stop]))
                rest = count - start
                score = dot_nt(k_mask[start:stop], q_mask[start:count]) * 0.25
                mask = causal(rest, block, 0, 0)
                mask = (
                    lax.broadcasted_iota(jnp.int32, (block, rest), 0)
                    <= lax.broadcasted_iota(jnp.int32, (block, rest), 1)
                )
                weight = only(mask, 1.0 + score + 0.5 * score * score)
                d_weight = dot_nt(v_wide[start:stop], d_wide[start:count])
                d_score = only(mask, d_weight * (1.0 + score))
                grads_k.append(dot(d_score.astype(BF16), q_mask[start:count]))
                grads_v.append(dot(weight.astype(BF16), d_low[start:count]))
            first, second = halves_of(q_mask, pick_a[...], pick_b[...], rows[...])
            d_feat = dot(d_low[:, half * VD : (half + 1) * VD], state[head]) + d_denom * total[head]
            inter_q = feature_back(d_feat, first, second, pick_a[...], pick_b[...], rows[...])
            first, second = halves_of(k_mask, pick_a[...], pick_b[...], rows[...])
            feat = (first * second * rows[2:3, :]).astype(BF16)
            d_feat = dot(vals[:, half * VD : (half + 1) * VD], d_state[head]) + d_total[head]
            inter_k = feature_back(d_feat, first, second, pick_a[...], pick_b[...], rows[...])
            inter_v = dot_nt(feat, d_state[head])
            inter_v = jnp.concatenate([inter_v, inter_v], axis=1)
            whole_v = jnp.concatenate(grads_v, axis=0) + inter_v
            v_sum[...] = whole_v if half == 0 else jnp.where(mine, whole_v, v_sum[...])
            q_sum[:, place] += jnp.concatenate(grads_q, axis=0) * 0.25 + only(lanes, inter_q)
            k_sum[:, place] += jnp.concatenate(grads_k, axis=0) * 0.25 + only(lanes, inter_k)
        d_values[:, spot] = v_sum[...].astype(BF16)
        if between is not None:
            between(pair)
        return carry

    lax.fori_loop(0, pairs, step, 0)
    d_query[...] = q_sum[...].astype(BF16)
    d_keys[...] = k_sum[...].astype(BF16)


def attend_back_inside(
    query, keys, values, mixed, inverse, d_mixed, pick_a, pick_b, rows, state, total, q_sum, k_sum,
    v_part, between, block=256,
):
    pairs = values.shape[1] // LANES
    count = keys.shape[0]
    q_sum[...] = jnp.zeros_like(q_sum)
    k_sum[...] = jnp.zeros_like(k_sum)

    def step(pair, carry):
        spot = tile_at(pair)
        d_numer = d_mixed[:, spot].astype(F32) * inverse[:, spot]
        lost = d_numer * mixed[:, spot].astype(F32)
        d_low = d_numer.astype(BF16)
        turned = pltpu.roll(lost, VD, 1)
        vals = values[:, spot]
        for half in range(2):
            head = pair * 2 + half
            place = tile_at(head // 8)
            mine = half_lanes(count, half)
            lanes = head_lanes(count, head % 8)
            d_denom = -jnp.sum(only(mine, lost), axis=1, keepdims=True)
            d_wide = jnp.where(mine, d_numer, -turned).astype(BF16)
            v_wide = jnp.where(mine, vals, jnp.ones_like(vals))
            q_mask = only(lanes, query[:, place])
            k_mask = only(lanes, keys[:, place])
            grads_q, grads_k, grads_v = [], [], []
            for start in range(0, count, block):
                stop = start + block
                score = dot_nt(q_mask[start:stop], k_mask[0:stop]) * 0.25
                d_weight = dot_nt(d_wide[start:stop], v_wide[0:stop])
                d_score = only(causal(block, stop, start, 0), d_weight * (1.0 + score))
                grads_q.append(dot(d_score.astype(BF16), k_mask[0:stop]))
                rest = count - start
                score = dot_nt(k_mask[start:stop], q_mask[start:count]) * 0.25
                mask = (
                    lax.broadcasted_iota(jnp.int32, (block, rest), 0)
                    <= lax.broadcasted_iota(jnp.int32, (block, rest), 1)
                )
                weight = only(mask, 1.0 + score + 0.5 * score * score)
                d_weight = dot_nt(v_wide[start:stop], d_wide[start:count])
                d_score = only(mask, d_weight * (1.0 + score))
                grads_k.append(dot(d_score.astype(BF16), q_mask[start:count]))
                grads_v.append(dot(weight.astype(BF16), d_low[start:count]))
            first, second = halves_of(q_mask, pick_a[...], pick_b[...], rows[...])
            d_feat = dot(d_low[:, half * VD : (half + 1) * VD], state[head]) + d_denom * total[head]
            inter_q = feature_back(d_feat, first, second, pick_a[...], pick_b[...], rows[...])
            whole_v = jnp.concatenate(grads_v, axis=0)
            v_part[:, spot] = whole_v if half == 0 else jnp.where(mine, whole_v, v_part[:, spot])
            q_sum[:, place] += jnp.concatenate(grads_q, axis=0) * 0.25 + only(lanes, inter_q)
            k_sum[:, place] += jnp.concatenate(grads_k, axis=0) * 0.25
        between(pair)
        return carry

    lax.fori_loop(0, pairs, step, 0)


def attend_back_after(
    keys, values, pick_a, pick_b, rows, d_state, d_total, k_sum, v_part, d_values, between, ended
):
    pairs = values.shape[1] // LANES
    count = keys.shape[0]

    def step(pair, carry):
        spot = tile_at(pair)
        vals = values[:, spot]
        for half in range(2):
            head = pair * 2 + half
            place = tile_at(head // 8)
            lanes = head_lanes(count, head % 8)
            k_mask = only(lanes, keys[:, place])
            first, second = halves_of(k_mask, pick_a[...], pick_b[...], rows[...])
            feat = (first * second * rows[2:3, :]).astype(BF16)
            d_feat = dot(vals[:, half * VD : (half + 1) * VD], d_state[head]) + d_total[head]
            inter_k = feature_back(d_feat, first, second, pick_a[...], pick_b[...], rows[...])
            inter_v = dot_nt(feat, d_state[head])
            inter_v = jnp.concatenate([inter_v, inter_v], axis=1)
            k_sum[:, place] += only(lanes, inter_k)
            whole_v = v_part[:, spot] + inter_v
            mask = half_lanes(count, half)
            whole_v = whole_v if half == 0 else jnp.where(mask, whole_v, v_part[:, spot])
            if half == 0:
                v_part[:, spot] = jnp.where(mask, whole_v, v_part[:, spot])
            else:
                d_values[:, spot] = whole_v.astype(BF16)
        between(pair)
        ended(pair)
        return carry

    lax.fori_loop(0, pairs, step, 0)


def call(body, shapes, *operands, scratch=()):
    return pl.pallas_call(
        body,
        out_shape=[jax.ShapeDtypeStruct(shape, kind) for shape, kind in shapes],
        scratch_shapes=list(scratch),
        compiler_params=pltpu.CompilerParams(vmem_limit_bytes=VMEM_LIMIT),
    )(*operands)


def rms_norm(inputs, gain):
    return inputs * lax.rsqrt(jnp.mean(inputs * inputs, axis=-1, keepdims=True) + EPS) * gain


def gated(gate_in, up_in):
    return jax.nn.silu(gate_in) * up_in


def before(parts, axis, reverse=False):
    place = lax.axis_index(axis)
    order = jnp.arange(parts.shape[0])
    chosen = order > place if reverse else order < place
    chosen = chosen.reshape((-1,) + (1,) * (parts.ndim - 1))
    return jnp.sum(jnp.where(chosen, parts.astype(F32), 0.0), axis=0)


MESH_ID = pl.DeviceIdType.MESH


class Place:
    def __init__(self):
        self.dp, self.seq = lax.axis_index("dp"), lax.axis_index("seq")
        self.z, self.y = self.dp // 2, self.dp % 2
        self.x, self.core = self.seq // 2, self.seq % 2
        self.zh, self.zl = self.z // 2, self.z % 2

    def at(self, z=None, y=None, x=None, core=None):
        z = self.z if z is None else z
        y = self.y if y is None else y
        x = self.x if x is None else x
        core = self.core if core is None else core
        return (z * 2 + y, x * 2 + core)

    def mate(self):
        return self.at(core=1 - self.core)

    def across(self, axis):
        return self.at(y=1 - self.y) if axis == "y" else self.at(x=1 - self.x)

    def own(self, axis):
        return self.y if axis == "y" else self.x


def remote(source, target, sent, landed, device):
    return pltpu.make_async_remote_copy(
        src_ref=source,
        dst_ref=target,
        send_sem=sent,
        recv_sem=landed,
        device_id=device,
        device_id_type=MESH_ID,
    )


def enter(place):
    barrier = pltpu.get_barrier_semaphore()
    others = [(place.dp, jnp.bitwise_xor(place.seq, other)) for other in range(1, 4)]
    others += [(jnp.bitwise_xor(place.dp, other), place.seq) for other in range(1, 8)]
    for device in others:
        pl.semaphore_signal(barrier, inc=1, device_id=device, device_id_type=MESH_ID)
    pl.semaphore_wait(barrier, len(others))


class Gather:
    def __init__(self, shard, whole, rows, columns, first, sems, place):
        self.shard, self.whole, self.rows, self.columns = shard, whole, rows, columns
        self.first, self.third = first, "x" if first == "y" else "y"
        self.sems, self.place = sems, place

    def block(self, high, low, one, three, core=None):
        core = self.place.core if core is None else core
        grid = (one, three) if self.first == "y" else (three, one)
        return self.whole.at[(high, low) + grid + (core, self.rows, self.columns)]

    def move(self, ref, spot, device, source=None):
        sent, landed, _ = self.sems
        source = ref if source is None else source
        return remote(source, ref, sent.at[spot], landed.at[spot], device)

    def copies(self):
        place, every = self.place, slice(None)
        own1, own3 = place.own(self.first), place.own(self.third)
        mine = self.shard.at[self.rows, self.columns]
        block = self.block
        zh, zl = place.zh, place.zl

        def keep():
            return pltpu.make_async_copy(mine, block(zh, zl, own1, own3), self.sems[2])

        def far(high):
            device = place.at(z=jnp.bitwise_xor(place.z, 2))
            return self.move(block(high, zl, own1, own3), 0, device, mine)

        def cross(three):
            return self.move(block(every, zl, own1, three), 1, place.across(self.third))

        def near(low):
            device = place.at(z=jnp.bitwise_xor(place.z, 1))
            return self.move(block(every, low, own1, every), 2, device)

        def over(one):
            return self.move(block(every, every, one, every), 3, place.across(self.first))

        def mate(core):
            return self.move(block(every, every, every, every, core), 4, place.mate())

        return keep, [
            (far, zh, 1 - zh),
            (cross, own3, 1 - own3),
            (near, zl, 1 - zl),
            (over, own1, 1 - own1),
            (mate, place.core, 1 - place.core),
        ]

    def step(self, index):
        keep, stages = self.copies()
        if index == 0:
            keep().start()
        if index == 1:
            keep().wait()
        if index > 0:
            act, _, theirs = stages[index - 1]
            act(theirs).wait_recv()
        if index < 5:
            act, own, _ = stages[index]
            act(own).start()
        else:
            for act, own, _ in stages:
                act(own).wait_send()


class Pool:
    def __init__(self, refs, sems, free, place, chunks):
        self.refs, self.sems, self.free, self.place, self.chunks = refs, sems, free, place, chunks
        self.kept, self.landing = refs[0].shape[0], refs[1].shape[0]


class Chunk:
    def __init__(self, pool, order, source, rows, columns, first, put):
        self.pool, self.place, self.put = pool, pool.place, put
        self.order = order
        self.source, self.rows, self.columns, self.first = source, rows, columns, first
        self.third = "x" if first == "y" else "y"
        self.width = columns.size

    def ref(self, kind):
        spot = self.order
        if kind == 0:
            spot = spot % self.pool.kept
        if kind == 1:
            spot = spot % self.pool.landing
        return self.pool.refs[kind].at[spot]

    def cut(self, ref):
        return ref.at[(slice(None),) * (len(ref.shape) - 1) + (pl.ds(0, self.width),)]

    def share(self, core):
        every = slice(None)
        return self.source.at[every, every, every, every, core, self.rows, self.columns]

    def pick(self, which):
        mine = self.ref(0)
        return mine.at[:, :, which] if self.first == "y" else mine.at[:, :, :, which]

    def fetch(self):
        return pltpu.make_async_copy(
            self.share(self.place.core), self.cut(self.ref(0)), self.pool.sems[2].at[self.order]
        )

    def send(self, ref, target, spot, device):
        sent, landed = self.pool.sems[0].at[self.order, spot], self.pool.sems[1].at[self.order, spot]
        return remote(ref, self.cut(target), sent, landed, device)

    def to_mate(self):
        return self.send(self.share(1 - self.place.core), self.ref(1), 0, self.place.mate())

    def to_over(self):
        own = self.place.own(self.first)
        return self.send(
            self.cut(self.pick(1 - own)), self.ref(2), 1, self.place.across(self.first)
        )

    def to_near(self):
        place = self.place
        source = self.cut(self.ref(2).at[:, 1 - place.zl])
        return self.send(source, self.ref(3), 2, place.at(z=jnp.bitwise_xor(place.z, 1)))

    def to_cross(self):
        own = self.place.own(self.third)
        source = self.cut(self.ref(3).at[:, 1 - own])
        return self.send(source, self.ref(4), 3, self.place.across(self.third))

    def to_far(self):
        place = self.place
        source = self.cut(self.ref(4).at[1 - place.zh])
        return self.send(source, self.ref(5), 4, place.at(z=jnp.bitwise_xor(place.z, 2)))

    def view(self, ref):
        return self.cut(ref)

    def step(self, index):
        pool, place, order = self.pool, self.place, self.order
        if index == 0:
            if order >= pool.landing:
                pl.semaphore_wait(pool.free, 1)
            self.fetch().start()
            self.to_mate().start()
        elif index == 1:
            self.fetch().wait()
            self.to_mate().wait_recv()
            mine = self.cut(self.ref(0))
            mine[...] = mine[...] + self.cut(self.ref(1))[...]
            if order + pool.landing < pool.chunks:
                pl.semaphore_signal(
                    pool.free, inc=1, device_id=place.mate(), device_id_type=MESH_ID
                )
            self.to_over().start()
        elif index == 2:
            self.to_over().wait()
            over = self.cut(self.ref(2))
            over[...] = over[...] + self.cut(self.pick(place.own(self.first)))[...]
            self.to_near().start()
        elif index == 3:
            self.to_near().wait_recv()
            near = self.cut(self.ref(3))
            near[...] = near[...] + self.cut(self.ref(2).at[:, place.zl])[...]
            self.to_cross().start()
        elif index == 4:
            self.to_cross().wait_recv()
            cross = self.cut(self.ref(4))
            cross[...] = cross[...] + self.cut(self.ref(3).at[:, place.own(self.third)])[...]
            self.to_far().start()
        else:
            self.to_far().wait_recv()
            final = self.cut(self.ref(4).at[place.zh])[...].astype(F32)
            self.put(final + self.cut(self.ref(5))[...].astype(F32))
            self.to_mate().wait_send()
            self.to_near().wait_send()
            self.to_cross().wait_send()
            self.to_far().wait_send()


class Gains:
    def __init__(self, mine, slots, sent, landed, place):
        self.mine, self.slots, self.sent, self.landed, self.place = mine, slots, sent, landed, place

    def swaps(self, index):
        place = self.place
        if index == 0:
            partners = [(place.dp, jnp.bitwise_xor(place.seq, k)) for k in range(1, 4)]
        else:
            partners = [(jnp.bitwise_xor(place.dp, k), place.seq) for k in range(1, 8)]
        for spot, partner in enumerate(partners):
            spot += 3 * index
            yield spot, remote(
                self.mine.at[index], self.slots.at[spot], self.sent.at[spot], self.landed.at[spot],
                partner,
            )

    def step(self, index):
        if index > 0:
            value = self.mine[index - 1]
            for spot, swap in self.swaps(index - 1):
                swap.wait()
                value = value + self.slots[spot]
            self.mine[index] = value
        if index < 2:
            for _, swap in self.swaps(index):
                swap.start()


class Exchange:
    def __init__(self, state, total, near, far, sent, landed, place, reverse):
        self.state, self.total, self.near, self.far = state, total, near, far
        self.sent, self.landed, self.place, self.reverse = sent, landed, place, reverse
        self.half = state.shape[0] // 2

    def move(self, source, target, spot, device):
        return remote(source, target, self.sent.at[spot], self.landed.at[spot], device)

    def to_mate(self):
        pairs = zip((self.state, self.total), self.near)
        return [self.move(a, b, i, self.place.mate()) for i, (a, b) in enumerate(pairs)]

    def part(self, spot, core, device):
        part = pl.ds(core * self.half, self.half)
        return [
            self.move(ref.at[part], ref.at[part], spot + i, device) for i, ref in enumerate(self.far)
        ]

    def over(self):
        return self.part(2, self.place.core, self.place.across("x"))

    def share(self, core):
        return self.part(4, core, self.place.mate())

    def step(self, index):
        place, reverse = self.place, self.reverse
        giving = place.x == (1 if reverse else 0)
        taking = place.x == (0 if reverse else 1)
        second = place.core == (0 if reverse else 1)
        state, total = self.state, self.total
        (near_state, near_total), (far_state, far_total) = self.near, self.far
        if index == 0:
            for copy in self.to_mate():
                copy.start()
        elif index == 1:
            for copy in self.to_mate():
                copy.wait_recv()

            @pl.when(giving)
            def _():
                part = pl.ds(place.core * self.half, self.half)
                far_state[part] = state[part] + near_state[part]
                far_total[part] = total[part] + near_total[part]
                for copy in self.over():
                    copy.start()

        elif index == 2:

            @pl.when(taking)
            def _():
                for copy in self.over():
                    copy.wait_recv()
                for copy in self.share(place.core):
                    copy.start()

        else:

            @pl.when(taking)
            def _():
                for copy in self.share(1 - place.core):
                    copy.wait_recv()
                for copy in self.share(place.core):
                    copy.wait_send()

            for copy in self.to_mate():
                copy.wait_send()

            @pl.when(giving)
            def _():
                for copy in self.over():
                    copy.wait_send()

            @pl.when(jnp.logical_and(giving, second))
            def _():
                state[...] = near_state[...]
                total[...] = near_total[...]

            @pl.when(jnp.logical_and(giving, jnp.logical_not(second)))
            def _():
                state[...] = jnp.zeros_like(state)
                total[...] = jnp.zeros_like(total)

            @pl.when(jnp.logical_and(taking, second))
            def _():
                state[...] = far_state[...] + near_state[...]
                total[...] = far_total[...] + near_total[...]

            @pl.when(jnp.logical_and(taking, jnp.logical_not(second)))
            def _():
                state[...] = far_state[...]
                total[...] = far_total[...]


class Work:
    def __init__(self):
        self.kinds = ([], [], [], [])

    def pause(self, name):
        for code in PLAN.get(name, ()):
            self.kinds[code // 1000][code % 1000 // 10].step(code % 10)

    def between(self, prefix, count, halves=False):
        def hook(index, half=""):
            for spot in range(count):
                name = f"{prefix}{spot}{half}"
                if name in PLAN:

                    @pl.when(index == spot)
                    def _():
                        self.pause(name)

        return hook


PLAN = {
    's': (0, 10, 20,),
    'qk': (30,),
    'v': (40, 1, 50,),
    'st1': (60,),
    'st2': (11,),
    'st3': (70,),
    'st4': (21,),
    'st5': (2,),
    'st6': (31,),
    'e0': (2000,),
    'a0': (41,),
    'a1': (12, 51,),
    'a2': (2001, 61,),
    'a4': (22,),
    'a6': (3,),
    'a7': (32,),
    'e0w': (13, 42, 2002, 71, 2003, 52,),
    'b0': (23,),
    'b2': (33,),
    'b3': (62,),
    'b4': (4,),
    'b5': (14,),
    'b6': (72,),
    'b7': (43,),
    'po': (5, 15, 53, 80,),
    'p0': (34, 90, 100, 24, 63, 110, 120, 73, 35, 25, 130, 140, 54, 150, 81, 44, 91, 160, 101, 170, 111, 55, 45,),
    'm0': (121, 131,),
    't0': (64, 74, 141,),
    'm1': (82, 92, 151, 161,),
    't1': (171,),
    'm2': (65, 75, 102,),
    'm3': (83, 112, 93, 122, 132, 103, 142, 113, 84, 152, 123, 94, 162, 85, 133, 95, 172, 104, 143, 114, 153, 105, 124, 163, 115,),
    't3': (134,),
    'm4': (125, 173, 1000, 1010, 1020, 1030,),
    't4': (135, 144,),
    'm5': (154, 1001, 1040,),
    't5': (1011, 164, 1021,),
    'm6': (1031,),
    't6': (145, 174,),
    'm7': (155, 1041, 165, 1002, 1050, 175,),
    't7': (1012,),
    'm8': (1051, 1060,),
    'm9': (1003, 1022, 1061, 1070, 1032, 1080,),
    'm10': (1013, 1071,),
    't10': (1042, 1081, 1090,),
    'ft': (1023, 1052, 1100,),
    'dm': (1004, 1091,),
    'c1': (1033, 1062, 1110,),
    'c2': (1014, 1101,),
    'c4': (1043, 1072, 1120,),
    'c5': (1005, 1111, 1024,),
    'e1': (2010,),
    'og': (2011, 1015, 1034, 1082, 1130,),
    'd0': (1025, 1044, 1035, 1053, 1063, 1092, 1140,),
    'd1': (1045, 1073, 1083, 1102, 1121, 1131, 1150,),
    'd2': (2012, 1064, 1084, 1093, 1112, 1160,),
    'd3': (2013, 1065, 1085, 1054, 1074, 1103, 1132, 1141, 1151, 1161,),
    'd4': (1055, 1094, 1104, 1122, 1170, 1180,),
    'd5': (1075, 1113, 1095, 1133, 1152, 1142, 1171, 1181, 1190, 1200,),
    'd6': (1105, 1123, 1191,),
    'd7': (1114, 1134, 1143, 1153, 1162, 1172, 1201, 1210,),
    'lq': (1220,),
    'f0': (1182, 1230,),
    'f1': (1115, 1124, 1135, 1154, 1211, 1221,),
    'f2': (1163,),
    'f3': (1192, 1144, 1231,),
    'l1': (1173, 1222, 1240,),
    'f4': (1183, 1202, 1250,),
    'f5': (1125, 1174, 1155, 1241,),
    'f6': (1184, 1193, 1212, 1251, 1145,),
    'l2': (1164, 1223, 1260, 1270,),
    'f7': (1203, 1232,),
    'l3': (1175, 1261, 1242, 1185, 1271, 1280, 1290,),
    'dn': (1165, 1194, 1204, 1224, 1213, 1233, 1252, 1262, 1243, 1281, 1291, 1272,),
    'z': (1195, 1205, 1225, 1214, 1234, 1244, 3000, 1282, 1292, 1253, 3001, 1263, 1273, 1254, 1215, 1264, 1235, 1245, 1274, 1283, 1293, 3002, 1284, 1294, 1255, 1265, 1275, 1285, 1295,),
}


def normalize(value, gain):
    return value * lax.rsqrt(jnp.mean(value * value, axis=-1, keepdims=True) + EPS) * gain


GRID = (2, 2, 2, 2, 2)
PARTS = (4, 8, 11)
BAND = 128
TILE = 256


def shape(dims, kind):
    return jax.ShapeDtypeStruct(dims, kind)


def padded(columns):
    return -(-columns // TILE) * TILE


def bands(count, act, size=BAND):
    def step(index, carry):
        act(pl.ds(pl.multiple_of(index * size, size), size))
        return carry

    lax.fori_loop(0, count // size, step, 0)


def rms_back(value, gain, grad):
    scale = lax.rsqrt(jnp.mean(value * value, axis=-1, keepdims=True) + EPS)
    unit = value * scale
    inner = grad * gain
    back = scale * (inner - unit * jnp.mean(inner * unit, axis=-1, keepdims=True))
    return back, jnp.sum(grad * unit, axis=0, keepdims=True)


def front_phase(work, r):
    r.ready("tok")

    def norm(band):
        r.normed[band, :] = normalize(r.tok[band, :].astype(F32), r.gain_row[...]).astype(BF16)

    bands(r.count, norm)
    r.ready("wq", "wk", "wv", "og", "wo")
    r.query[...] = dot(r.normed[...], r.wq[...]).astype(BF16)
    r.keys[...] = dot(r.normed[...], r.wk[...]).astype(BF16)
    work.pause("qk")

    def project(band):
        r.values[:, band] = dot(r.normed[...], r.wv[:, band]).astype(BF16)

    bands(r.heads * VD, project, TILE)
    work.pause("v")
    pairs = r.heads // 2
    tables = r.pick_a, r.pick_b, r.table
    state_body(r.keys, r.values, *tables, r.state, r.total, work.between("st", pairs))
    work.pause("e0")
    attend_inside(r.query, r.keys, r.values, r.middle, r.inverse, work.between("a", pairs))
    work.pause("e0w")
    attend_before(
        r.query, *tables, r.state, r.total, r.middle, r.inverse, r.mixed, work.between("b", pairs)
    )

    def project_out(band):
        r.middle[:, band] = r.tok[:, band].astype(F32) + dot(r.mixed[...], r.wo[:, band])

    bands(r.width, project_out, TILE)
    work.pause("po")

    def norm_again(band):
        r.low[band, :] = normalize(r.middle[band, :], r.gain2_row[...]).astype(BF16)

    bands(r.count, norm_again)
    work.pause("nm")


def feed_phase(work, r, tiles, made, low_t, og_t, acc_out, acc_back, in_sem, out_sem):
    steps = PARTS[-1]

    def columns(step):
        return pl.ds(pl.multiple_of(step * TILE, TILE), TILE)

    def load(step, slot):
        return [
            pltpu.make_async_copy(ref.at[:, columns(step)], tiles.at[slot, i], in_sem.at[slot, i])
            for i, ref in enumerate(r.wholes_flat)
        ]

    def save(step, slot):
        return [
            pltpu.make_async_copy(made.at[slot, i], ref.at[:, columns(step)], out_sem.at[slot, i])
            for i, ref in enumerate(r.grads_flat)
        ]

    low_t[...] = r.low[...].T
    og_t[...] = r.og[...].T
    acc_out[...] = r.middle[...]
    acc_back[...] = jnp.zeros_like(acc_back)
    work.pause("p0")
    for copy in load(0, 0):
        copy.start()
    in_tile, after_tile = work.between("m", steps), work.between("t", steps)

    def step(index, carry):
        slot = index % 2
        for copy in load(index, slot):
            copy.wait()

        crossing = functools.reduce(jnp.logical_or, [index + 1 == edge for edge in PARTS])

        @pl.when(jnp.logical_not(crossing))
        def _():
            for copy in load(index + 1, 1 - slot):
                copy.start()

        gate_w, up_w, down_w = (tiles.at[slot, i] for i in range(3))
        gate = dot(r.low[...], gate_w[...])
        upward = dot(r.low[...], up_w[...])
        d_hidden = dot(r.og[...], down_w[...])
        sig = 1.0 / (1.0 + jnp.exp(-gate))
        silu = gate * sig
        hidden = (silu * upward).astype(BF16)
        d_gate = (d_hidden * upward * (sig * (1.0 + gate * (1.0 - sig)))).astype(BF16)
        d_up = (d_hidden * silu).astype(BF16)
        acc_out[...] += dot_nt(hidden, down_w[...])

        @pl.when(index >= 1)
        def _():
            for copy in save(index - 1, 1 - slot):
                copy.wait()

        in_tile(index)

        @pl.when(jnp.logical_and(crossing, index + 1 < steps))
        def _():
            for copy in load(index + 1, 1 - slot):
                copy.start()

        acc_back[...] += dot_nt(d_gate, gate_w[...]) + dot_nt(d_up, up_w[...])
        made[slot, 0] = dot(low_t[...], d_gate).astype(BF16)
        made[slot, 1] = dot(low_t[...], d_up).astype(BF16)
        made[slot, 2] = dot(og_t[...], hidden).astype(BF16)
        for copy in save(index, slot):
            copy.start()
        after_tile(index)
        return carry

    lax.fori_loop(0, steps, step, 0)

    def store_out(band):
        r.out[band, :] = acc_out[band, :].astype(BF16)

    bands(r.count, store_out)
    r.ends[0]().start()
    r.gain_sum[...] = jnp.zeros(r.gain_sum.shape, F32)

    def middle_back(band):
        value, part = rms_back(r.middle[band, :], r.gain2_row[...], acc_back[band, :])
        r.gain_sum[1:2, :] += part
        value = r.og[band, :].astype(F32) + value
        r.middle[band, :] = value
        r.low[band, :] = value.astype(BF16)

    bands(r.count, middle_back)
    for copy in save(steps - 1, (steps - 1) % 2):
        copy.wait()
    work.pause("ft")

    def mixed_back(band):
        r.d_mixed[:, band] = dot_nt(r.low[...], r.wo[band, :]).astype(BF16)

    bands(r.heads * VD, mixed_back, TILE)
    work.pause("dm")


def back_phase(work, r, d_query, d_keys, d_values, q_sum, k_sum, turned, v_part):
    heads_wide, narrow = r.heads * VD, r.heads * KD
    pairs = r.heads // 2
    tables = r.pick_a, r.pick_b, r.table
    back_state_body(
        r.query, r.mixed, r.inverse, r.d_mixed, *tables, r.d_state, r.d_total,
        work.between("c", pairs),
    )
    work.pause("e1")
    turned[...] = r.mixed[...].T

    def out_grads(band):
        r.out_g[:, band] = dot(turned[...], r.low[:, band]).astype(BF16)

    bands(r.width, out_grads, TILE)
    work.pause("og")
    turned[...] = r.normed[...].T
    attend_back_inside(
        r.query, r.keys, r.values, r.mixed, r.inverse, r.d_mixed, *tables, r.state, r.total,
        q_sum, k_sum, v_part, work.between("d", pairs),
    )
    work.pause("e1w")
    grid = GRID + (r.rows,)
    late_refs = dict(q=(d_query, q_sum), k=(d_keys, k_sum), v=(d_values, None))

    def late(index):
        spot = sum(high - low for group in r.late_groups[:index] for _, low, high in group)
        for name, low, high in r.late_groups[index]:
            ref, wide = late_refs[name]
            if wide is not None:
                ref[:, low:high] = wide[:, low:high].astype(BF16)
            for start in range(low, high, TILE):
                stop = min(start + TILE, high)
                value = dot(turned[...], ref[:, start:stop]).astype(BF16)
                size = stop - start
                r.late_g[:, :, :, :, :, :, spot : spot + size] = value.reshape(grid + (size,))
                spot += size

    late(0)
    work.pause("lq")

    def ended(pair):
        for spot, index in ((pairs // 2 - 1, 1), (pairs - 2, 2)):

            @pl.when(pair == spot)
            def _(index=index):
                late(index)
                work.pause(f"l{index}")

    attend_back_after(
        r.keys, r.values, *tables, r.d_state, r.d_total, k_sum, v_part, d_values,
        work.between("f", pairs), ended,
    )
    late(3)
    work.pause("l3")

    def back_norm(band):
        v_part[:, band] = (
            dot_nt(d_query[...], r.wq[band, :])
            + dot_nt(d_keys[...], r.wk[band, :])
            + dot_nt(d_values[...], r.wv[band, :])
        )

    bands(r.width, back_norm, TILE)
    work.pause("dn")

    def tokens_back(band):
        value, part = rms_back(r.tok[band, :].astype(F32), r.gain_row[...], v_part[band, :])
        r.gain_sum[0:1, :] += part
        r.middle[band, :] = r.middle[band, :] + value

    bands(r.count, tokens_back)
    quarter = r.width // 4
    for which in range(2):
        for part in range(4):
            spot = 4 * which + part
            r.gain_mine[0, spot : spot + 1, :] = r.gain_sum[
                which : which + 1, part * quarter : (part + 1) * quarter
            ]


class Refs:
    pass


def layer(tokens, gain, wq, wk, wv, wo, gain2, tables, shards3, out_grad):
    count, width = tokens.shape
    heads = wq.shape[1] // KD
    rows, columns = shards3[0].shape
    full = padded(columns)
    tall = rows // 2
    heads_wide, narrow = heads * VD, heads * KD
    last = heads_wide - 2 * VD
    late_groups = (
        (("q", 0, narrow),),
        (("v", 0, heads_wide // 2), ("k", 0, narrow // 2)),
        (("v", heads_wide // 2, last),),
        (("v", last, heads_wide), ("k", narrow // 2, narrow)),
    )
    late_sizes = [sum(high - low for _, low, high in group) for group in late_groups]
    edges = [0] + [part * TILE for part in PARTS]
    widest = max(*late_sizes, width // 2, *[high - low for low, high in zip(edges, edges[1:])])
    chunks = 6 * len(PARTS) + 4 + 2 * len(late_groups)
    gathers = 6 * len(PARTS)
    states = ((heads, VD, FEATS), BF16), ((heads, 1, FEATS), F32)
    sem = pltpu.SemaphoreType.DMA

    loads = dict(
        shard0=shards3[0], shard1=shards3[1], shard2=shards3[2], tok=tokens, wq=wq, wk=wk, wv=wv,
        og=out_grad, wo=wo,
    )
    inputs = {name + "_in": value for name, value in loads.items()}
    inputs |= dict(
        gain=gain, gain2=gain2, pick_a=tables[0], pick_b=tables[1], table=tables[2]
    )
    free_outs = dict(
        whole0=shape((width, full), BF16), whole1=shape((width, full), BF16),
        whole2=shape((width, full), BF16), grad0=shape((width, full), BF16),
        grad1=shape((width, full), BF16), grad2=shape((width, full), BF16),
        out_end=shape((count, width), BF16), tok_end=shape((count, width), F32),
    )
    outs = dict(
        g0=shape((rows, columns), F32), g1=shape((rows, columns), F32),
        g2=shape((rows, columns), F32), g_out=shape((rows, width), F32),
        g_value=shape((rows, heads_wide), F32), g_query=shape((rows, narrow), F32),
        g_keys=shape((rows, narrow), F32), g_gain=shape((8, width // 4), F32),
    )
    scratch = {name: pltpu.VMEM(value.shape, value.dtype) for name, value in loads.items()}
    scratch |= dict(
        out=pltpu.VMEM((count, width), BF16),
        middle=pltpu.VMEM((count, width), F32),
        load_sem=sem((len(loads),)), end_sem=sem((2,)),
        gain_row=pltpu.VMEM((1, width), F32), gain2_row=pltpu.VMEM((1, width), F32),
        normed=pltpu.VMEM((count, width), BF16),
        query=pltpu.VMEM((count, narrow), BF16),
        keys=pltpu.VMEM((count, narrow), BF16),
        values=pltpu.VMEM((count, heads_wide), BF16),
        mixed=pltpu.VMEM((count, heads_wide), BF16),
        inverse=pltpu.VMEM((count, heads_wide), F32),
        state=pltpu.VMEM(*states[0]), total=pltpu.VMEM(*states[1]),
        d_state=pltpu.VMEM(*states[0]), d_total=pltpu.VMEM(*states[1]),
        near_state=pltpu.VMEM(*states[0]), near_total=pltpu.VMEM(*states[1]),
        far_state=pltpu.VMEM(*states[0]), far_total=pltpu.VMEM(*states[1]),
        ex_sent=sem((6,)), ex_landed=sem((6,)),
        low=pltpu.VMEM((count, width), BF16),
        d_mixed=pltpu.VMEM((count, heads_wide), BF16),
        out_g=pltpu.VMEM((width, width), BF16),
        late_g=pltpu.VMEM(GRID + (rows, sum(late_sizes)), BF16),
        wide=pltpu.VMEM((3, rows, full), BF16),
        ag_sent=sem((gathers, 5)), ag_landed=sem((gathers, 5)), ag_local=sem((gathers,)),
        gain_sum=pltpu.VMEM((8, width), F32),
        gain_mine=pltpu.VMEM((3, 8, width // 4), F32),
        gain_slots=pltpu.VMEM((10, 8, width // 4), F32),
        gain_sent=sem((10,)), gain_landed=sem((10,)),
        p0=pltpu.VMEM((5, 2, 2, 2, 2, tall, widest), BF16),
        p1=pltpu.VMEM((4, 2, 2, 2, 2, tall, widest), BF16),
        p2=pltpu.VMEM((chunks, 2, 2, 2, tall, widest), BF16),
        p3=pltpu.VMEM((chunks, 2, 2, tall, widest), BF16),
        p4=pltpu.VMEM((chunks, 2, tall, widest), BF16),
        p5=pltpu.VMEM((chunks, tall, widest), BF16),
        rs_sent=sem((chunks, 5)), rs_landed=sem((chunks, 5)), rs_local=sem((chunks,)),
        credit=pltpu.SemaphoreType.REGULAR,
    )
    names = list(inputs) + list(free_outs) + list(outs) + list(scratch)

    def body(*refs):
        r = Refs()
        for name, ref in zip(names, refs):
            setattr(r, name, ref)
        r.count, r.width, r.heads, r.rows = count, width, heads, rows
        r.late_groups = late_groups
        r.place = place = Place()
        r.wholes_flat = [r.whole0, r.whole1, r.whole2]
        r.grads_flat = [r.grad0, r.grad1, r.grad2]
        grid = GRID + (rows,)
        wholes = [ref.reshape(grid + (full,)) for ref in r.wholes_flat]
        grads = [ref.reshape(grid + (full,)) for ref in r.grads_flat]
        def load(name):
            spot = list(loads).index(name)
            source = getattr(r, name + "_in")
            return pltpu.make_async_copy(source, getattr(r, name), r.load_sem.at[spot])

        r.ready = lambda *wanted: [load(name).wait() for name in wanted]
        r.ends = [
            lambda: pltpu.make_async_copy(r.out, r.out_end, r.end_sem.at[0]),
            lambda: pltpu.make_async_copy(r.middle, r.tok_end, r.end_sem.at[1]),
        ]
        for name in loads:
            load(name).start()
        enter(place)
        work = Work()
        r.gain_row[...] = r.gain[...].astype(F32).reshape(1, width)
        r.gain2_row[...] = r.gain2[...].astype(F32).reshape(1, width)
        r.ready("shard0", "shard1", "shard2")
        gather_list, sum_list, exchange_list, gain_list = work.kinds
        for spot, shard in enumerate((r.shard0, r.shard1, r.shard2)):
            r.wide[spot, :, columns:full] = jnp.zeros((rows, full - columns), BF16)
            r.wide[spot, :, 0:columns] = shard[...]
        for low, high in zip(edges, edges[1:]):
            for weight in range(3):
                for kind, first in enumerate("xy"):
                    order = len(gather_list)
                    gather_list.append(
                        Gather(
                            r.wide.at[weight], wholes[weight], pl.ds(kind * tall, tall),
                            pl.ds(low, high - low), first,
                            (r.ag_sent.at[order], r.ag_landed.at[order], r.ag_local.at[order]), place,
                        )
                    )
        pool = Pool(
            [r.p0, r.p1, r.p2, r.p3, r.p4, r.p5], (r.rs_sent, r.rs_landed, r.rs_local), r.credit,
            place, chunks,
        )

        def sums(source, low, high, target, firsts="xy"):
            for kind, first in enumerate(firsts):

                def put(value, kind=kind):
                    target(slice(kind * tall, (kind + 1) * tall), value)

                chunk_rows, chunk_columns = pl.ds(kind * tall, tall), pl.ds(low, high - low)
                sum_list.append(
                    Chunk(pool, len(sum_list), source, chunk_rows, chunk_columns, first, put)
                )

        def into(ref, low, high):
            def put(where, value):
                ref[where, low:high] = value[:, 0 : high - low]

            return put

        for low, high in zip(edges, edges[1:]):
            for source, target in zip(grads, (r.g0, r.g1, r.g2)):
                sums(source, low, high, into(target, low, min(high, columns)))
        half = width // 2
        for low in (0, half):
            target = into(r.g_out, low, low + half)
            sums(r.out_g.reshape(grid + (width,)), low, low + half, target, "yy")
        late_ends = dict(q=r.g_query, k=r.g_keys, v=r.g_value)
        spot = 0
        for group, size in zip(late_groups, late_sizes):

            def put_late(where, value, group=group):
                at = 0
                for name, low, high in group:
                    late_ends[name][where, low:high] = value[:, at : at + high - low]
                    at += high - low

            sums(r.late_g, spot, spot + size, put_late)
            spot += size
        for state, total, reverse in ((r.state, r.total, False), (r.d_state, r.d_total, True)):
            exchange_list.append(
                Exchange(
                    state, total, (r.near_state, r.near_total), (r.far_state, r.far_total),
                    r.ex_sent, r.ex_landed, place, reverse,
                )
            )
        gain_list.append(Gains(r.gain_mine, r.gain_slots, r.gain_sent, r.gain_landed, place))
        work.pause("s")
        front_phase(work, r)
        pl.run_scoped(
            lambda *buffers: feed_phase(work, r, *buffers),
            pltpu.VMEM((2, 3, width, TILE), BF16),
            pltpu.VMEM((2, 3, width, TILE), BF16),
            pltpu.VMEM((width, count), BF16),
            pltpu.VMEM((width, count), BF16),
            pltpu.VMEM((count, width), F32),
            pltpu.VMEM((count, width), F32),
            sem((2, 3)),
            sem((2, 3)),
        )
        pl.run_scoped(
            lambda *buffers: back_phase(work, r, *buffers),
            pltpu.VMEM((count, narrow), BF16),
            pltpu.VMEM((count, narrow), BF16),
            pltpu.VMEM((count, heads_wide), BF16),
            pltpu.VMEM((count, narrow), F32),
            pltpu.VMEM((count, narrow), F32),
            pltpu.VMEM((width, count), BF16),
            pltpu.VMEM((count, width), F32),
        )
        r.ends[1]().start()
        work.pause("z")
        r.ends[0]().wait()
        r.ends[1]().wait()
        r.g_gain[...] = r.gain_mine[2]

    vmem = pl.BlockSpec(memory_space=pltpu.VMEM)
    free = pl.BlockSpec(memory_space=pl.ANY)
    results = pl.pallas_call(
        body,
        out_shape=list(free_outs.values()) + list(outs.values()),
        in_specs=[free] * len(loads) + [vmem] * 5,
        out_specs=[free] * len(free_outs) + [vmem] * len(outs),
        scratch_shapes=list(scratch.values()),
        compiler_params=pltpu.CompilerParams(
            collective_id=0, has_side_effects=True, vmem_limit_bytes=VMEM_LIMIT
        ),
    )(*inputs.values())
    return results[6:]


def hand_over(results, gains):
    quarter = gains.shape[1]
    share = quarter // 8
    count = len(results)

    def body(*refs):
        sources, gain, targets = refs[:count], refs[count], refs[count + 1 : 2 * count + 1]
        first, second, sems = refs[2 * count + 1 :]
        copies = [
            pltpu.make_async_copy(a, b, sems.at[i]) for i, (a, b) in enumerate(zip(sources, targets))
        ]
        for copy in copies:
            copy.start()
        own = lax.axis_index("dp") * 4 + lax.axis_index("seq")
        turned = pltpu.roll(gain[...], lax.rem(quarter - own % 8 * share, quarter), 1)[:, 0:share]
        row = lax.broadcasted_iota(jnp.int32, turned.shape, 0)
        for ref, start in ((first, 0), (second, 4)):
            ref[...] = jnp.sum(only(row == start + own // 8, turned), axis=0, keepdims=True)
        for copy in copies:
            copy.wait()

    vmem = pl.BlockSpec(memory_space=pltpu.VMEM)
    free = pl.BlockSpec(memory_space=pl.ANY)
    return pl.pallas_call(
        body,
        out_shape=[shape(value.shape, value.dtype) for value in results] + [shape((1, share), F32)] * 2,
        in_specs=[vmem] * (count + 1),
        out_specs=[free] * count + [vmem] * 2,
        scratch_shapes=[pltpu.SemaphoreType.DMA((count,))],
    )(*results, gains)


def general(
    tokens, attn_gain, w_query, w_key, w_value, w_output, mlp_gain, w_gate, w_up, w_down, out_grad
):
    count, width = tokens.shape
    heads = w_query.shape[1] // KD
    all_values = heads * VD
    tables = feature_tables()
    inputs = tokens.astype(F32)
    gain = attn_gain.astype(F32).reshape(1, width)
    gate_full, up_full, down_full = (
        lax.all_gather(w, ("dp", "seq"), axis=0, tiled=True) for w in (w_gate, w_up, w_down)
    )
    normed, query, keys, values = call(
        project_body,
        [
            ((count, width), BF16),
            ((count, heads * KD), BF16),
            ((count, heads * KD), BF16),
            ((count, all_values), BF16),
        ],
        tokens,
        gain,
        w_query,
        w_key,
        w_value,
    )
    state_shapes = [((heads, VD, FEATS), BF16), ((heads, 1, FEATS), F32)]
    state, total = call(state_body, state_shapes, keys, values, *tables)
    state = before(lax.all_gather(state, "seq"), "seq").astype(BF16)
    total = before(lax.all_gather(total, "seq"), "seq")
    mixed, inverse = call(
        attend_body,
        [((count, all_values), BF16), ((count, all_values), F32)],
        query,
        keys,
        values,
        *tables,
        state,
        total,
    )
    middle = inputs + dot(mixed, w_output)
    normed_mlp, second_back = jax.vjp(rms_norm, middle, mlp_gain.astype(F32))
    mlp_low = normed_mlp.astype(BF16)
    gate = dot(mlp_low, gate_full)
    upward = dot(mlp_low, up_full)
    hidden_val, gated_back = jax.vjp(gated, gate, upward)
    hidden = hidden_val.astype(BF16)
    layer_out = (middle + dot_nt(hidden, down_full)).astype(BF16)
    d_hidden = dot(out_grad, down_full)
    down_grad = dot_tn(out_grad, hidden).astype(BF16)
    d_gate_f, d_up_f = gated_back(d_hidden)
    d_gate = d_gate_f.astype(BF16)
    d_up = d_up_f.astype(BF16)
    gate_grad = dot_tn(mlp_low, d_gate).astype(BF16)
    up_grad = dot_tn(mlp_low, d_up).astype(BF16)
    d_normed_mlp = dot_nt(d_gate, gate_full) + dot_nt(d_up, up_full)
    d_middle_norm, mlp_gain_part = second_back(d_normed_mlp)
    d_middle = out_grad.astype(F32) + d_middle_norm
    d_branch = d_middle.astype(BF16)
    output_grad = dot_tn(mixed, d_branch).astype(BF16)
    d_mixed = dot_nt(d_branch, w_output).astype(BF16)
    d_state, d_total = call(
        back_state_body, state_shapes, query, mixed, inverse, d_mixed, *tables
    )
    d_state = before(lax.all_gather(d_state, "seq"), "seq", True).astype(BF16)
    d_total = before(lax.all_gather(d_total, "seq"), "seq", True)
    d_query, d_keys, d_values = call(
        attend_back_body,
        [
            ((count, heads * KD), BF16),
            ((count, heads * KD), BF16),
            ((count, all_values), BF16),
        ],
        query,
        keys,
        values,
        mixed,
        inverse,
        d_mixed,
        *tables,
        state,
        total,
        d_state,
        d_total,
        scratch=[
            pltpu.VMEM((count, heads * KD), F32),
            pltpu.VMEM((count, heads * KD), F32),
            pltpu.VMEM((count, LANES), F32),
        ],
    )
    d_normed = dot_nt(d_query, w_query) + dot_nt(d_keys, w_key) + dot_nt(d_values, w_value)
    query_grad = dot_tn(normed, d_query).astype(BF16)
    key_grad = dot_tn(normed, d_keys).astype(BF16)
    value_grad = dot_tn(normed, d_values).astype(BF16)
    _, first_back = jax.vjp(rms_norm, inputs, attn_gain.astype(F32))
    d_inputs_norm, attn_gain_part = first_back(d_normed)
    tokens_grad = d_middle + d_inputs_norm
    parts = [query_grad, key_grad, value_grad, output_grad, gate_grad, up_grad, down_grad]
    joined = lax.psum_scatter(
        jnp.concatenate(parts, axis=1), ("dp", "seq"), scatter_dimension=0, tiled=True
    ).astype(F32)
    edges = np.cumsum([part.shape[1] for part in parts])[:-1]
    query_grad, key_grad, value_grad, output_grad, gate_grad, up_grad, down_grad = jnp.split(
        joined, edges, axis=1
    )
    gains = lax.psum_scatter(
        jnp.stack([attn_gain_part, mlp_gain_part], axis=1),
        ("dp", "seq"),
        scatter_dimension=0,
        tiled=True,
    )
    return (
        layer_out,
        tokens_grad,
        gains[:, 0],
        query_grad,
        key_grad,
        value_grad,
        output_grad,
        gains[:, 1],
        gate_grad,
        up_grad,
        down_grad,
    )


def shards(
    tokens, attn_gain, w_query, w_key, w_value, w_output, mlp_gain, w_gate, w_up, w_down, out_grad
):
    args = (
        tokens, attn_gain, w_query, w_key, w_value, w_output, mlp_gain, w_gate, w_up, w_down, out_grad
    )
    if (lax.axis_size("dp"), lax.axis_size("seq")) != (8, 4):
        return general(*args)
    *results, gains = layer(
        tokens, attn_gain, w_query, w_key, w_value, w_output, mlp_gain, feature_tables(),
        (w_gate, w_up, w_down), out_grad,
    )
    *results, gain_grad, gain2_grad = hand_over(results, gains)
    layer_out, tok_grad, gate_grad, up_grad, down_grad, output_grad, value_grad, query_grad, key_grad = results
    return (
        layer_out,
        tok_grad,
        gain_grad.reshape(-1),
        query_grad,
        key_grad,
        value_grad,
        output_grad,
        gain2_grad.reshape(-1),
        gate_grad,
        up_grad,
        down_grad,
    )


def solution(mesh):
    rows = P(("dp", "seq"), None)
    in_specs = (rows, P(), P(), P(), P(), P(), P(), rows, rows, rows, rows)
    out_specs = (
        rows,
        rows,
        P(("dp", "seq")),
        rows,
        rows,
        rows,
        rows,
        P(("dp", "seq")),
        rows,
        rows,
        rows,
    )
    return jax.shard_map(
        shards, mesh=mesh, in_specs=in_specs, out_specs=out_specs, check_vma=False
    )
```

```python
import functools
import math

import jax
import jax.numpy as jnp
import numpy as np
from jax import lax
from jax.experimental import pallas as pl
from jax.experimental.pallas import tpu as pltpu
from jax.sharding import PartitionSpec as P

KD = 16
VD = 64
LANES = 128
FEATS = 256
EPS = 1e-05
QUAD = 1.0 / (4.0 * math.sqrt(2.0))
F32 = jnp.float32
BF16 = jnp.bfloat16
VMEM_LIMIT = 62 << 20


def feature_tables():
    pick_a = np.zeros((LANES, FEATS), np.float32)
    pick_b = np.zeros((LANES, FEATS), np.float32)
    rows = np.zeros((8, FEATS), np.float32)
    spot = 0
    for a in range(KD):
        for b in range(a, KD):
            pick_a[a::KD, spot] = 1.0
            pick_b[b::KD, spot] = 1.0
            rows[2, spot] = QUAD
            rows[3, spot] = 1.0 if a == b else 2.0
            spot += 1
    for a in range(KD):
        pick_a[a::KD, spot] = 1.0
        rows[1, spot] = 1.0
        rows[2, spot] = 0.5
        rows[3, spot] = 1.0
        spot += 1
    rows[0:4, spot] = 1.0
    return jnp.asarray(pick_a, BF16), jnp.asarray(pick_b, BF16), jnp.asarray(rows)


def dot(left, right):
    return jnp.dot(left, right, preferred_element_type=F32)


def dot_nt(left, right):
    return lax.dot_general(left, right, (((1,), (1,)), ((), ())), preferred_element_type=F32)


def dot_tn(left, right):
    return lax.dot_general(left, right, (((0,), (0,)), ((), ())), preferred_element_type=F32)


def tile_at(index):
    return pl.ds(pl.multiple_of(index * LANES, LANES), LANES)


def head_lanes(rows, spot):
    return lax.broadcasted_iota(jnp.int32, (rows, LANES), 1) // KD == spot


def half_lanes(rows, half):
    return lax.broadcasted_iota(jnp.int32, (rows, LANES), 1) // VD == half


def halves_of(masked, pick_a, pick_b, rows):
    first = dot(masked, pick_a) + rows[0:1, :]
    second = dot(masked, pick_b) + rows[1:2, :]
    return first, second


def features_of(masked, pick_a, pick_b, rows):
    first, second = halves_of(masked, pick_a, pick_b, rows)
    return (first * second * rows[2:3, :]).astype(BF16)


def only(mask, value):
    return jnp.where(mask, value, jnp.zeros_like(value))


def project_body(tok, gain, wq, wk, wv, normed, query, keys, values):
    x = tok[...].astype(F32)
    scale = lax.rsqrt(jnp.mean(x * x, axis=-1, keepdims=True) + EPS)
    normed[...] = (x * scale * gain[...]).astype(BF16)
    query[...] = dot(normed[...], wq[...]).astype(BF16)
    keys[...] = dot(normed[...], wk[...]).astype(BF16)
    values[...] = dot(normed[...], wv[...]).astype(BF16)


def state_body(keys, values, pick_a, pick_b, rows, state, total, between=None):
    pairs = values.shape[1] // LANES
    count = keys.shape[0]

    def step(pair, carry):
        turned = values[:, tile_at(pair)].T
        for half in range(2):
            head = pair * 2 + half
            masked = only(head_lanes(count, head % 8), keys[:, tile_at(head // 8)])
            feat = features_of(masked, pick_a[...], pick_b[...], rows[...])
            sums = dot(turned[half * VD : (half + 1) * VD, :], feat)
            state[head] = (sums * rows[3:4, :]).astype(BF16)
            total[head] = jnp.sum(feat.astype(F32), axis=0, keepdims=True) * rows[3:4, :]
        if between is not None:
            between(pair)
        return carry

    lax.fori_loop(0, pairs, step, 0)


def causal(rows, columns, row_start, column_start):
    row = lax.broadcasted_iota(jnp.int32, (rows, columns), 0) + row_start
    column = lax.broadcasted_iota(jnp.int32, (rows, columns), 1) + column_start
    return row >= column


def attend_body(query, keys, values, pick_a, pick_b, rows, state, total, mixed, inverse, between=None, block=256):
    pairs = values.shape[1] // LANES
    count = keys.shape[0]

    def step(pair, carry):
        vals = values[:, tile_at(pair)]
        for start in range(0, count, block):
            stop = start + block
            numer = None
            for half in range(2):
                head = pair * 2 + half
                masked = only(head_lanes(block, head % 8), query[start:stop, tile_at(head // 8)])
                score = dot_nt(masked, keys[0:stop, tile_at(head // 8)]) * 0.25
                weight = 1.0 + score + 0.5 * score * score
                weight = jnp.where(causal(block, stop, start, 0), weight, 0.0)
                feat = features_of(masked, pick_a[...], pick_b[...], rows[...])
                inter = feat.astype(F32) * total[head]
                denom = jnp.sum(weight, axis=1, keepdims=True) + jnp.sum(
                    inter, axis=1, keepdims=True
                )
                across = dot_nt(feat, state[head])
                both = dot(weight.astype(BF16), vals[0:stop, :])
                across = jnp.concatenate([across, across], axis=1)
                whole = (both + across) / denom
                flip = jnp.broadcast_to(1.0 / denom, (block, LANES))
                if half == 0:
                    numer, invs = whole, flip
                else:
                    mask = half_lanes(block, 0)
                    numer = jnp.where(mask, numer, whole)
                    invs = jnp.where(mask, invs, flip)
            mixed[start:stop, tile_at(pair)] = numer.astype(BF16)
            inverse[start:stop, tile_at(pair)] = invs
        if between is not None:
            between(pair)
        return carry

    lax.fori_loop(0, pairs, step, 0)


def spare_lane(rows, spot):
    lane = lax.broadcasted_iota(jnp.int32, (rows, LANES), 1)
    return lane == lax.rem(spot * KD + KD, LANES)


def query_side(value, spot):
    rows = value.shape[0]
    quarter = only(head_lanes(rows, spot), value * 0.25)
    return jnp.where(spare_lane(rows, spot), jnp.ones_like(value), quarter)


def key_side(value, spot):
    return jnp.where(spare_lane(value.shape[0], spot), jnp.ones_like(value), value)


def triangle(value, start, block, upper=False):
    row = lax.broadcasted_iota(jnp.int32, (block, block), 0)
    column = lax.broadcasted_iota(jnp.int32, (block, block), 1)
    keep = row <= column if upper else row >= column
    pieces = [value[:, 0:start]] if start > 0 else []
    pieces.append(only(keep, value[:, start : start + block]))
    if start + block < value.shape[1]:
        pieces.append(value[:, start + block :])
    return jnp.concatenate(pieces, axis=1) if len(pieces) > 1 else pieces[0]


def attend_inside(query, keys, values, numer, denoms, between, block=512):
    pairs = values.shape[1] // LANES
    count = keys.shape[0]

    def step(pair, carry):
        vals = values[:, tile_at(pair)]
        for start in range(0, count, block):
            stop = start + block
            for half in range(2):
                head = pair * 2 + half
                place = tile_at(head // 8)
                plus = dot_nt(
                    query_side(query[start:stop, place], head % 8), key_side(keys[0:stop, place], head % 8)
                )
                weight = triangle(0.5 * plus * plus + 0.5, start, block)
                flip = jnp.broadcast_to(jnp.sum(weight, axis=1, keepdims=True), (block, LANES))
                both = dot(weight.astype(BF16), vals[0:stop, :])
                if half == 0:
                    whole, wides = both, flip
                else:
                    mask = half_lanes(block, 0)
                    numer[start:stop, tile_at(pair)] = jnp.where(mask, whole, both)
                    denoms[start:stop, tile_at(pair)] = jnp.where(mask, wides, flip)
        between(pair)
        return carry

    lax.fori_loop(0, pairs, step, 0)


def attend_before(query, pick_a, pick_b, rows, state, total, numer, inverse, mixed, between):
    count = query.shape[0]
    pairs = mixed.shape[1] // LANES

    def step(pair, carry):
        spot = tile_at(pair)
        for half in range(2):
            head = pair * 2 + half
            masked = only(head_lanes(count, head % 8), query[:, tile_at(head // 8)])
            feat = features_of(masked, pick_a[...], pick_b[...], rows[...])
            inter = jnp.sum(feat.astype(F32) * total[head], axis=1, keepdims=True)
            inter = jnp.broadcast_to(inter, (count, LANES))
            across = dot_nt(feat, state[head])
            across = jnp.concatenate([across, across], axis=1)
            if half == 0:
                whole, wides = across, inter
            else:
                mask = half_lanes(count, 0)
                whole = jnp.where(mask, whole, across)
                wides = jnp.where(mask, wides, inter)
        flipped = 1.0 / (inverse[:, spot] + wides)
        inverse[:, spot] = flipped
        mixed[:, spot] = ((numer[:, spot] + whole) * flipped).astype(BF16)
        between(pair)
        return carry

    lax.fori_loop(0, pairs, step, 0)


def back_state_body(query, mixed, inverse, d_mixed, pick_a, pick_b, rows, d_state, d_total, between=None):
    pairs = mixed.shape[1] // LANES
    count = query.shape[0]

    def step(pair, carry):
        spot = tile_at(pair)
        d_numer = d_mixed[:, spot].astype(F32) * inverse[:, spot]
        lost = d_numer * mixed[:, spot].astype(F32)
        turned = d_numer.astype(BF16).T
        for half in range(2):
            head = pair * 2 + half
            masked = only(head_lanes(count, head % 8), query[:, tile_at(head // 8)])
            feat = features_of(masked, pick_a[...], pick_b[...], rows[...])
            d_denom = -jnp.sum(only(half_lanes(count, half), lost), axis=1, keepdims=True)
            sums = dot(turned[half * VD : (half + 1) * VD, :], feat)
            d_state[head] = (sums * rows[3:4, :]).astype(BF16)
            d_total[head] = (
                jnp.sum(feat.astype(F32) * d_denom, axis=0, keepdims=True) * rows[3:4, :]
            )
        if between is not None:
            between(pair)
        return carry

    lax.fori_loop(0, pairs, step, 0)


def feature_back(d_feat, first, second, pick_a, pick_b, rows):
    scaled = d_feat * rows[2:3, :]
    return dot_nt((scaled * second).astype(BF16), pick_a) + dot_nt(
        (scaled * first).astype(BF16), pick_b
    )


def attend_back_body(
    query,
    keys,
    values,
    mixed,
    inverse,
    d_mixed,
    pick_a,
    pick_b,
    rows,
    state,
    total,
    d_state,
    d_total,
    d_query,
    d_keys,
    d_values,
    q_sum,
    k_sum,
    v_sum,
    between=None,
    block=256,
):
    pairs = values.shape[1] // LANES
    count = keys.shape[0]
    q_sum[...] = jnp.zeros_like(q_sum)
    k_sum[...] = jnp.zeros_like(k_sum)

    def step(pair, carry):
        spot = tile_at(pair)
        d_numer = d_mixed[:, spot].astype(F32) * inverse[:, spot]
        lost = d_numer * mixed[:, spot].astype(F32)
        d_low = d_numer.astype(BF16)
        turned = pltpu.roll(lost, VD, 1)
        vals = values[:, spot]
        for half in range(2):
            head = pair * 2 + half
            place = tile_at(head // 8)
            mine = half_lanes(count, half)
            lanes = head_lanes(count, head % 8)
            d_denom = -jnp.sum(only(mine, lost), axis=1, keepdims=True)
            d_wide = jnp.where(mine, d_numer, -turned).astype(BF16)
            v_wide = jnp.where(mine, vals, jnp.ones_like(vals))
            q_mask = only(lanes, query[:, place])
            k_mask = only(lanes, keys[:, place])
            grads_q, grads_k, grads_v = [], [], []
            for start in range(0, count, block):
                stop = start + block
                score = dot_nt(q_mask[start:stop], k_mask[0:stop]) * 0.25
                d_weight = dot_nt(d_wide[start:stop], v_wide[0:stop])
                d_score = only(causal(block, stop, start, 0), d_weight * (1.0 + score))
                grads_q.append(dot(d_score.astype(BF16), k_mask[0:stop]))
                rest = count - start
                score = dot_nt(k_mask[start:stop], q_mask[start:count]) * 0.25
                mask = causal(rest, block, 0, 0)
                mask = (
                    lax.broadcasted_iota(jnp.int32, (block, rest), 0)
                    <= lax.broadcasted_iota(jnp.int32, (block, rest), 1)
                )
                weight = only(mask, 1.0 + score + 0.5 * score * score)
                d_weight = dot_nt(v_wide[start:stop], d_wide[start:count])
                d_score = only(mask, d_weight * (1.0 + score))
                grads_k.append(dot(d_score.astype(BF16), q_mask[start:count]))
                grads_v.append(dot(weight.astype(BF16), d_low[start:count]))
            first, second = halves_of(q_mask, pick_a[...], pick_b[...], rows[...])
            d_feat = dot(d_low[:, half * VD : (half + 1) * VD], state[head]) + d_denom * total[head]
            inter_q = feature_back(d_feat, first, second, pick_a[...], pick_b[...], rows[...])
            first, second = halves_of(k_mask, pick_a[...], pick_b[...], rows[...])
            feat = (first * second * rows[2:3, :]).astype(BF16)
            d_feat = dot(vals[:, half * VD : (half + 1) * VD], d_state[head]) + d_total[head]
            inter_k = feature_back(d_feat, first, second, pick_a[...], pick_b[...], rows[...])
            inter_v = dot_nt(feat, d_state[head])
            inter_v = jnp.concatenate([inter_v, inter_v], axis=1)
            whole_v = jnp.concatenate(grads_v, axis=0) + inter_v
            v_sum[...] = whole_v if half == 0 else jnp.where(mine, whole_v, v_sum[...])
            q_sum[:, place] += jnp.concatenate(grads_q, axis=0) * 0.25 + only(lanes, inter_q)
            k_sum[:, place] += jnp.concatenate(grads_k, axis=0) * 0.25 + only(lanes, inter_k)
        d_values[:, spot] = v_sum[...].astype(BF16)
        if between is not None:
            between(pair)
        return carry

    lax.fori_loop(0, pairs, step, 0)
    d_query[...] = q_sum[...].astype(BF16)
    d_keys[...] = k_sum[...].astype(BF16)


def attend_back_inside(
    query, keys, values, mixed, inverse, d_mixed, pick_a, pick_b, rows, state, total, q_sum, k_sum,
    v_part, between, block=512,
):
    pairs = values.shape[1] // LANES
    count = keys.shape[0]
    q_sum[...] = jnp.zeros_like(q_sum)
    k_sum[...] = jnp.zeros_like(k_sum)

    def step(pair, carry):
        spot = tile_at(pair)
        d_numer = d_mixed[:, spot].astype(F32) * inverse[:, spot]
        lost = d_numer * mixed[:, spot].astype(F32)
        d_low = d_numer.astype(BF16)
        turned = pltpu.roll(lost, VD, 1)
        vals = values[:, spot]
        for half in range(2):
            head = pair * 2 + half
            place = tile_at(head // 8)
            mine = half_lanes(count, half)
            lanes = head_lanes(count, head % 8)
            d_wide = jnp.where(mine, d_numer, -turned).astype(BF16)
            v_wide = jnp.where(mine, vals, jnp.ones_like(vals))
            q_tile, k_tile = query[:, place], keys[:, place]
            q_mask = only(lanes, q_tile)
            q_quarter, k_quarter = q_mask * 0.25, only(lanes, k_tile) * 0.25
            q_plus, k_plus = query_side(q_tile, head % 8), key_side(k_tile, head % 8)
            grads_q, grads_k, grads_v = [], [], []
            for start in range(0, count, block):
                stop = start + block
                plus = dot_nt(q_plus[start:stop], k_plus[0:stop])
                d_weight = dot_nt(d_wide[start:stop], v_wide[0:stop])
                d_score = triangle(d_weight * plus, start, block)
                grads_q.append(dot(d_score.astype(BF16), k_quarter[0:stop]))
                plus = dot_nt(k_plus[start:stop], q_plus[start:count])
                weight = triangle(0.5 * plus * plus + 0.5, 0, block, True)
                d_weight = dot_nt(v_wide[start:stop], d_wide[start:count])
                d_score = triangle(d_weight * plus, 0, block, True)
                grads_k.append(dot(d_score.astype(BF16), q_quarter[start:count]))
                grads_v.append(dot(weight.astype(BF16), d_low[start:count]))
            first, second = halves_of(q_mask, pick_a[...], pick_b[...], rows[...])
            high = total[head].astype(BF16)
            rest = (total[head] - high.astype(F32)).astype(BF16)
            sums = [jnp.broadcast_to(part, (VD, FEATS)) for part in (high, rest)]
            zero = jnp.zeros((VD, FEATS), BF16)
            own = [state[head], sums[0]], [zero, sums[1]]
            order = [part for group in own for part in (group if half == 0 else group[::-1])]
            d_feat = dot(
                jnp.concatenate([d_wide, d_wide], axis=1), jnp.concatenate(order, axis=0)
            )
            inter_q = feature_back(d_feat, first, second, pick_a[...], pick_b[...], rows[...])
            whole_v = jnp.concatenate(grads_v, axis=0)
            v_part[:, spot] = whole_v if half == 0 else jnp.where(mine, whole_v, v_part[:, spot])
            q_sum[:, place] += jnp.concatenate(grads_q, axis=0) + only(lanes, inter_q)
            k_sum[:, place] += jnp.concatenate(grads_k, axis=0)
        between(pair)
        return carry

    lax.fori_loop(0, pairs, step, 0)


def attend_back_after(
    keys, values, pick_a, pick_b, rows, d_state, d_total, k_sum, v_part, d_values, between, ended
):
    pairs = values.shape[1] // LANES
    count = keys.shape[0]

    def step(pair, carry):
        spot = tile_at(pair)
        vals = values[:, spot]
        for half in range(2):
            head = pair * 2 + half
            place = tile_at(head // 8)
            lanes = head_lanes(count, head % 8)
            k_mask = only(lanes, keys[:, place])
            first, second = halves_of(k_mask, pick_a[...], pick_b[...], rows[...])
            feat = (first * second * rows[2:3, :]).astype(BF16)
            d_feat = dot(vals[:, half * VD : (half + 1) * VD], d_state[head]) + d_total[head]
            inter_k = feature_back(d_feat, first, second, pick_a[...], pick_b[...], rows[...])
            inter_v = dot_nt(feat, d_state[head])
            inter_v = jnp.concatenate([inter_v, inter_v], axis=1)
            k_sum[:, place] += only(lanes, inter_k)
            whole_v = v_part[:, spot] + inter_v
            mask = half_lanes(count, half)
            whole_v = whole_v if half == 0 else jnp.where(mask, whole_v, v_part[:, spot])
            if half == 0:
                v_part[:, spot] = jnp.where(mask, whole_v, v_part[:, spot])
            else:
                d_values[:, spot] = whole_v.astype(BF16)
        between(pair)
        ended(pair)
        return carry

    lax.fori_loop(0, pairs, step, 0)


def call(body, shapes, *operands, scratch=()):
    return pl.pallas_call(
        body,
        out_shape=[jax.ShapeDtypeStruct(shape, kind) for shape, kind in shapes],
        scratch_shapes=list(scratch),
        compiler_params=pltpu.CompilerParams(vmem_limit_bytes=VMEM_LIMIT),
    )(*operands)


def rms_norm(inputs, gain):
    return inputs * lax.rsqrt(jnp.mean(inputs * inputs, axis=-1, keepdims=True) + EPS) * gain


def gated(gate_in, up_in):
    return jax.nn.silu(gate_in) * up_in


def before(parts, axis, reverse=False):
    place = lax.axis_index(axis)
    order = jnp.arange(parts.shape[0])
    chosen = order > place if reverse else order < place
    chosen = chosen.reshape((-1,) + (1,) * (parts.ndim - 1))
    return jnp.sum(jnp.where(chosen, parts.astype(F32), 0.0), axis=0)


MESH_ID = pl.DeviceIdType.MESH


class Place:
    def __init__(self):
        self.dp, self.seq = lax.axis_index("dp"), lax.axis_index("seq")
        self.z, self.y = self.dp // 2, self.dp % 2
        self.x, self.core = self.seq // 2, self.seq % 2
        self.zh, self.zl = self.z // 2, self.z % 2

    def at(self, z=None, y=None, x=None, core=None):
        z = self.z if z is None else z
        y = self.y if y is None else y
        x = self.x if x is None else x
        core = self.core if core is None else core
        return (z * 2 + y, x * 2 + core)

    def mate(self):
        return self.at(core=1 - self.core)

    def across(self, axis):
        return self.at(y=1 - self.y) if axis == "y" else self.at(x=1 - self.x)

    def own(self, axis):
        return self.y if axis == "y" else self.x


def remote(source, target, sent, landed, device):
    return pltpu.make_async_remote_copy(
        src_ref=source,
        dst_ref=target,
        send_sem=sent,
        recv_sem=landed,
        device_id=device,
        device_id_type=MESH_ID,
    )


def enter(place):
    barrier = pltpu.get_barrier_semaphore()
    others = [(place.dp, jnp.bitwise_xor(place.seq, other)) for other in range(1, 4)]
    others += [(jnp.bitwise_xor(place.dp, other), place.seq) for other in range(1, 8)]
    for device in others:
        pl.semaphore_signal(barrier, inc=1, device_id=device, device_id_type=MESH_ID)
    pl.semaphore_wait(barrier, len(others))


class Gather:
    def __init__(self, shard, whole, rows, columns, first, sems, place):
        self.shard, self.whole, self.rows, self.columns = shard, whole, rows, columns
        self.first, self.third = first, "x" if first == "y" else "y"
        self.sems, self.place = sems, place

    def block(self, high, low, one, three, core=None):
        core = self.place.core if core is None else core
        grid = (one, three) if self.first == "y" else (three, one)
        return self.whole.at[(high, low) + grid + (core, self.rows, self.columns)]

    def move(self, ref, spot, device, source=None):
        sent, landed, _ = self.sems
        source = ref if source is None else source
        return remote(source, ref, sent.at[spot], landed.at[spot], device)

    def copies(self):
        place, every = self.place, slice(None)
        own1, own3 = place.own(self.first), place.own(self.third)
        mine = self.shard.at[self.rows, self.columns]
        block = self.block
        zh, zl = place.zh, place.zl

        def keep():
            return pltpu.make_async_copy(mine, block(zh, zl, own1, own3), self.sems[2])

        def far(high):
            device = place.at(z=jnp.bitwise_xor(place.z, 2))
            return self.move(block(high, zl, own1, own3), 0, device, mine)

        def cross(three):
            return self.move(block(every, zl, own1, three), 1, place.across(self.third))

        def near(low):
            device = place.at(z=jnp.bitwise_xor(place.z, 1))
            return self.move(block(every, low, own1, every), 2, device)

        def over(one):
            return self.move(block(every, every, one, every), 3, place.across(self.first))

        def mate(core):
            return self.move(block(every, every, every, every, core), 4, place.mate())

        return keep, [
            (far, zh, 1 - zh),
            (cross, own3, 1 - own3),
            (near, zl, 1 - zl),
            (over, own1, 1 - own1),
            (mate, place.core, 1 - place.core),
        ]

    def step(self, index):
        keep, stages = self.copies()
        if index == 0:
            keep().start()
        if index == 1:
            keep().wait()
        if index > 0:
            act, _, theirs = stages[index - 1]
            act(theirs).wait_recv()
        if index < 5:
            act, own, _ = stages[index]
            act(own).start()
        else:
            for act, own, _ in stages:
                act(own).wait_send()


class Pool:
    def __init__(self, refs, sems, free, place, chunks):
        self.refs, self.sems, self.free, self.place, self.chunks = refs, sems, free, place, chunks
        self.kept, self.landing = refs[0].shape[0], refs[1].shape[0]


class Chunk:
    def __init__(self, pool, order, source, rows, columns, first, put):
        self.pool, self.place, self.put = pool, pool.place, put
        self.order = order
        self.source, self.rows, self.columns, self.first = source, rows, columns, first
        self.third = "x" if first == "y" else "y"
        self.width = columns.size

    def ref(self, kind):
        spot = self.order
        if kind == 0:
            spot = spot % self.pool.kept
        if kind == 1:
            spot = spot % self.pool.landing
        return self.pool.refs[kind].at[spot]

    def cut(self, ref):
        return ref.at[(slice(None),) * (len(ref.shape) - 1) + (pl.ds(0, self.width),)]

    def share(self, core):
        every = slice(None)
        return self.source.at[every, every, every, every, core, self.rows, self.columns]

    def pick(self, which):
        mine = self.ref(0)
        return mine.at[:, :, which] if self.first == "y" else mine.at[:, :, :, which]

    def fetch(self):
        return pltpu.make_async_copy(
            self.share(self.place.core), self.cut(self.ref(0)), self.pool.sems[2].at[self.order]
        )

    def send(self, ref, target, spot, device):
        sent, landed = self.pool.sems[0].at[self.order, spot], self.pool.sems[1].at[self.order, spot]
        return remote(ref, self.cut(target), sent, landed, device)

    def to_mate(self):
        return self.send(self.share(1 - self.place.core), self.ref(1), 0, self.place.mate())

    def to_over(self):
        own = self.place.own(self.first)
        return self.send(
            self.cut(self.pick(1 - own)), self.ref(2), 1, self.place.across(self.first)
        )

    def to_near(self):
        place = self.place
        source = self.cut(self.ref(2).at[:, 1 - place.zl])
        return self.send(source, self.ref(3), 2, place.at(z=jnp.bitwise_xor(place.z, 1)))

    def to_cross(self):
        own = self.place.own(self.third)
        source = self.cut(self.ref(3).at[:, 1 - own])
        return self.send(source, self.ref(4), 3, self.place.across(self.third))

    def to_far(self):
        place = self.place
        source = self.cut(self.ref(4).at[1 - place.zh])
        return self.send(source, self.ref(5), 4, place.at(z=jnp.bitwise_xor(place.z, 2)))

    def view(self, ref):
        return self.cut(ref)

    def step(self, index):
        pool, place, order = self.pool, self.place, self.order
        if index == 0:
            if order >= pool.landing:
                pl.semaphore_wait(pool.free, 1)
            self.fetch().start()
            self.to_mate().start()
        elif index == 1:
            self.fetch().wait()
            self.to_mate().wait_recv()
            mine = self.cut(self.ref(0))
            mine[...] = mine[...] + self.cut(self.ref(1))[...]
            if order + pool.landing < pool.chunks:
                pl.semaphore_signal(
                    pool.free, inc=1, device_id=place.mate(), device_id_type=MESH_ID
                )
            self.to_over().start()
        elif index == 2:
            self.to_over().wait()
            over = self.cut(self.ref(2))
            over[...] = over[...] + self.cut(self.pick(place.own(self.first)))[...]
            self.to_near().start()
        elif index == 3:
            self.to_near().wait_recv()
            near = self.cut(self.ref(3))
            near[...] = near[...] + self.cut(self.ref(2).at[:, place.zl])[...]
            self.to_cross().start()
        elif index == 4:
            self.to_cross().wait_recv()
            cross = self.cut(self.ref(4))
            cross[...] = cross[...] + self.cut(self.ref(3).at[:, place.own(self.third)])[...]
            self.to_far().start()
        else:
            self.to_far().wait_recv()
            final = self.cut(self.ref(4).at[place.zh])[...].astype(F32)
            self.put(final + self.cut(self.ref(5))[...].astype(F32))
            self.to_mate().wait_send()
            self.to_near().wait_send()
            self.to_cross().wait_send()
            self.to_far().wait_send()


class Gains:
    def __init__(self, mine, slots, sent, landed, place):
        self.mine, self.slots, self.sent, self.landed, self.place = mine, slots, sent, landed, place

    def swaps(self, index):
        place = self.place
        if index == 0:
            partners = [(place.dp, jnp.bitwise_xor(place.seq, k)) for k in range(1, 4)]
        else:
            partners = [(jnp.bitwise_xor(place.dp, k), place.seq) for k in range(1, 8)]
        for spot, partner in enumerate(partners):
            spot += 3 * index
            yield spot, remote(
                self.mine.at[index], self.slots.at[spot], self.sent.at[spot], self.landed.at[spot],
                partner,
            )

    def step(self, index):
        if index > 0:
            value = self.mine[index - 1]
            for spot, swap in self.swaps(index - 1):
                swap.wait()
                value = value + self.slots[spot]
            self.mine[index] = value
        if index < 2:
            for _, swap in self.swaps(index):
                swap.start()


class Exchange:
    def __init__(self, state, total, near, far, sent, landed, place, reverse):
        self.state, self.total, self.near, self.far = state, total, near, far
        self.sent, self.landed, self.place, self.reverse = sent, landed, place, reverse
        self.half = state.shape[0] // 2

    def move(self, source, target, spot, device):
        return remote(source, target, self.sent.at[spot], self.landed.at[spot], device)

    def to_mate(self):
        pairs = zip((self.state, self.total), self.near)
        return [self.move(a, b, i, self.place.mate()) for i, (a, b) in enumerate(pairs)]

    def part(self, spot, core, device):
        part = pl.ds(core * self.half, self.half)
        return [
            self.move(ref.at[part], ref.at[part], spot + i, device) for i, ref in enumerate(self.far)
        ]

    def over(self):
        return self.part(2, self.place.core, self.place.across("x"))

    def share(self, core):
        return self.part(4, core, self.place.mate())

    def step(self, index):
        place, reverse = self.place, self.reverse
        giving = place.x == (1 if reverse else 0)
        taking = place.x == (0 if reverse else 1)
        second = place.core == (0 if reverse else 1)
        state, total = self.state, self.total
        (near_state, near_total), (far_state, far_total) = self.near, self.far
        if index == 0:
            for copy in self.to_mate():
                copy.start()
        elif index == 1:
            for copy in self.to_mate():
                copy.wait_recv()

            @pl.when(giving)
            def _():
                part = pl.ds(place.core * self.half, self.half)
                far_state[part] = state[part] + near_state[part]
                far_total[part] = total[part] + near_total[part]
                for copy in self.over():
                    copy.start()

        elif index == 2:

            @pl.when(taking)
            def _():
                for copy in self.over():
                    copy.wait_recv()
                for copy in self.share(place.core):
                    copy.start()

        else:

            @pl.when(taking)
            def _():
                for copy in self.share(1 - place.core):
                    copy.wait_recv()
                for copy in self.share(place.core):
                    copy.wait_send()

            for copy in self.to_mate():
                copy.wait_send()

            @pl.when(giving)
            def _():
                for copy in self.over():
                    copy.wait_send()

            @pl.when(jnp.logical_and(giving, second))
            def _():
                state[...] = near_state[...]
                total[...] = near_total[...]

            @pl.when(jnp.logical_and(giving, jnp.logical_not(second)))
            def _():
                state[...] = jnp.zeros_like(state)
                total[...] = jnp.zeros_like(total)

            @pl.when(jnp.logical_and(taking, second))
            def _():
                state[...] = far_state[...] + near_state[...]
                total[...] = far_total[...] + near_total[...]

            @pl.when(jnp.logical_and(taking, jnp.logical_not(second)))
            def _():
                state[...] = far_state[...]
                total[...] = far_total[...]


class Work:
    def __init__(self):
        self.kinds = ([], [], [], [])

    def pause(self, name):
        for code in PLAN.get(name, ()):
            self.kinds[code // 1000][code % 1000 // 10].step(code % 10)

    def between(self, prefix, count, halves=False):
        def hook(index, half=""):
            for spot in range(count):
                name = f"{prefix}{spot}{half}"
                if name in PLAN:

                    @pl.when(index == spot)
                    def _():
                        self.pause(name)

        return hook


PLAN = {
    's': (0, 10,),
    'qk': (20,),
    'v': (30,),
    'st0': (1, 40,),
    'st2': (11, 50,),
    'st4': (21, 60,),
    'st6': (2, 31,),
    'e0': (2000,),
    'a0': (41,),
    'a1': (51,),
    'a2': (2001, 12, 61,),
    'a4': (22,),
    'a7': (32,),
    'e0w': (3, 13, 2002, 42, 2003,),
    'b0': (23, 52,),
    'b4': (4, 14, 43, 62,),
    'b7': (33, 70,),
    'po': (5, 15, 80,),
    'nm': (90,),
    'p0': (24, 63, 100, 110, 53, 44, 120, 25, 130, 34, 140, 45, 71, 150, 91, 81, 160, 35, 111, 170, 64, 101, 131, 72, 121, 54, 151, 141, 65, 161, 82, 171, 55,),
    't0': (73, 92,),
    't1': (83, 102,),
    't2': (93, 112,),
    'm3': (122, 74, 103, 132, 84, 113, 75, 142, 123, 94, 85, 152, 133, 162, 104, 95, 143, 172, 114, 105, 153, 124, 163, 115,),
    't3': (125, 134,),
    'm4': (144, 173, 1000, 1010, 1020, 1030,),
    't4': (135,),
    'm5': (145, 154,),
    't5': (164, 1001, 1011, 1040,),
    'm6': (1021,),
    't6': (174, 1031,),
    'm7': (155, 165, 1041, 175,),
    't7': (1002, 1012, 1050,),
    'm8': (1060,),
    't8': (1051,),
    'm9': (1003, 1061, 1022, 1070,),
    't9': (1032, 1080,),
    'm10': (1013, 1071,),
    't10': (1023, 1081,),
    'ft': (1042, 1052, 1090, 1100,),
    'dm': (1004, 1033,),
    'c0': (1091,),
    'c1': (1101,),
    'c2': (1043, 1062, 1110,),
    'c4': (1014, 1072, 1120,),
    'c5': (1053, 1024, 1111,),
    'c6': (1005,),
    'c7': (1121,),
    'e1': (2010,),
    'og': (2011, 1015, 1063, 1082, 1130,),
    'd0': (1025, 1034, 1044, 1092, 1131, 1140,),
    'd1': (1035, 1073, 1083, 1102, 1054, 1112, 1045, 1141, 1150, 1160,),
    'd2': (1064, 1093, 1151, 1161, 1122, 1170,),
    'd3': (1055, 1084, 1103, 1132, 1171, 1180,),
    'd4': (2012, 1065, 1074, 1113, 1123, 1152, 1181,),
    'd5': (2013, 1075, 1085, 1104, 1133, 1142, 1190, 1200,),
    'd6': (1105, 1094, 1124, 1153, 1172, 1191, 1201, 1143,),
    'd7': (1095, 1125, 1114, 1134, 1162, 1182, 1210,),
    'lq': (1154, 1192, 1220, 1230,),
    'f0': (1173, 1211,),
    'f1': (1115, 1202, 1135, 1221, 1231,),
    'f2': (1144, 1174, 1163,),
    'f3': (1183, 1222, 1212,),
    'l1': (1155, 1240, 1250, 1232,),
    'f4': (1164, 1184, 1193, 1203,),
    'f5': (1145, 1241, 1251,),
    'f6': (1175, 1194, 1204, 1223,),
    'l2': (1213, 1260, 1270,),
    'f7': (1233, 1165,),
    'l3': (1185, 1261, 1280, 1271, 1242, 1252, 1290,),
    'dn': (1195, 1205, 1214, 1224, 1234, 1243, 1262, 1272, 1281, 1291,),
    'z': (1215, 1225, 1244, 1253, 1235, 3000, 1282, 1263, 1292, 1273, 1254, 3001, 1245, 1264, 1283, 1293, 1274, 1255, 1284, 3002, 1294, 1265, 1275, 1285, 1295,),
}


def normalize(value, gain):
    return value * lax.rsqrt(jnp.mean(value * value, axis=-1, keepdims=True) + EPS) * gain


GRID = (2, 2, 2, 2, 2)
PARTS = (4, 8, 11)
GATHER_PARTS = (4, 8, 11)
TURNED = ((0, 1),)
BAND = 128
TILE = 256


def shape(dims, kind):
    return jax.ShapeDtypeStruct(dims, kind)


def padded(columns):
    return -(-columns // TILE) * TILE


def bands(count, act, size=BAND):
    def step(index, carry):
        act(pl.ds(pl.multiple_of(index * size, size), size))
        return carry

    lax.fori_loop(0, count // size, step, 0)


def rms_back(value, gain, grad):
    scale = lax.rsqrt(jnp.mean(value * value, axis=-1, keepdims=True) + EPS)
    unit = value * scale
    inner = grad * gain
    back = scale * (inner - unit * jnp.mean(inner * unit, axis=-1, keepdims=True))
    return back, jnp.sum(grad * unit, axis=0, keepdims=True)


def front_phase(work, r):
    r.ready("tok")

    def norm(band):
        r.normed[band, :] = normalize(r.tok[band, :].astype(F32), r.gain_row[...]).astype(BF16)

    bands(r.count, norm)
    r.ready("wq", "wk", "wv", "og", "wo")
    r.query[...] = dot(r.normed[...], r.wq[...]).astype(BF16)
    r.keys[...] = dot(r.normed[...], r.wk[...]).astype(BF16)
    work.pause("qk")

    def project(band):
        r.values[:, band] = dot(r.normed[...], r.wv[:, band]).astype(BF16)

    bands(r.heads * VD, project, TILE)
    work.pause("v")
    pairs = r.heads // 2
    tables = r.pick_a, r.pick_b, r.table
    state_body(r.keys, r.values, *tables, r.state, r.total, work.between("st", pairs))
    work.pause("e0")
    attend_inside(r.query, r.keys, r.values, r.middle, r.inverse, work.between("a", pairs))
    work.pause("e0w")
    attend_before(
        r.query, *tables, r.state, r.total, r.middle, r.inverse, r.mixed, work.between("b", pairs)
    )

    def project_out(band):
        r.middle[:, band] = r.tok[:, band].astype(F32) + dot(r.mixed[...], r.wo[:, band])

    bands(r.width, project_out, TILE)
    work.pause("po")

    def norm_again(band):
        r.low[band, :] = normalize(r.middle[band, :], r.gain2_row[...]).astype(BF16)

    bands(r.count, norm_again)
    work.pause("nm")


def feed_phase(work, r, tiles, made, low_t, og_t, acc_out, acc_back, in_sem, out_sem):
    steps = PARTS[-1]

    def columns(step):
        return pl.ds(pl.multiple_of(step * TILE, TILE), TILE)

    def load(step, slot):
        return [
            pltpu.make_async_copy(ref.at[:, columns(step)], tiles.at[slot, i], in_sem.at[slot, i])
            for i, ref in enumerate(r.wholes_flat)
        ]

    def save(step, slot):
        return [
            pltpu.make_async_copy(made.at[slot, i], ref.at[:, columns(step)], out_sem.at[slot, i])
            for i, ref in enumerate(r.grads_flat)
        ]

    low_t[...] = r.low[...].T
    og_t[...] = r.og[...].T
    acc_out[...] = r.middle[...]
    acc_back[...] = jnp.zeros_like(acc_back)
    work.pause("p0")
    for copy in load(0, 0):
        copy.start()
    in_tile, after_tile = work.between("m", steps), work.between("t", steps)

    def step(index, carry):
        slot = index % 2
        for copy in load(index, slot):
            copy.wait()

        crossing = functools.reduce(jnp.logical_or, [index + 1 == edge for edge in GATHER_PARTS])

        @pl.when(jnp.logical_not(crossing))
        def _():
            for copy in load(index + 1, 1 - slot):
                copy.start()

        gate_w, up_w, down_w = (tiles.at[slot, i] for i in range(3))
        gate = dot(r.low[...], gate_w[...])
        upward = dot(r.low[...], up_w[...])
        d_hidden = dot(r.og[...], down_w[...])
        sig = 1.0 / (1.0 + jnp.exp(-gate))
        silu = gate * sig
        hidden = (silu * upward).astype(BF16)
        d_gate = (d_hidden * upward * (sig * (1.0 + gate * (1.0 - sig)))).astype(BF16)
        d_up = (d_hidden * silu).astype(BF16)
        acc_out[...] += dot_nt(hidden, down_w[...])

        @pl.when(index >= 1)
        def _():
            for copy in save(index - 1, 1 - slot):
                copy.wait()

        in_tile(index)

        @pl.when(jnp.logical_and(crossing, index + 1 < steps))
        def _():
            for copy in load(index + 1, 1 - slot):
                copy.start()

        acc_back[...] += dot_nt(d_gate, gate_w[...]) + dot_nt(d_up, up_w[...])
        made[slot, 0] = dot(low_t[...], d_gate).astype(BF16)
        made[slot, 1] = dot(low_t[...], d_up).astype(BF16)
        made[slot, 2] = dot(og_t[...], hidden).astype(BF16)
        for copy in save(index, slot):
            copy.start()
        after_tile(index)
        return carry

    lax.fori_loop(0, steps, step, 0)

    def store_out(band):
        r.out[band, :] = acc_out[band, :].astype(BF16)

    bands(r.count, store_out)
    r.ends[0]().start()
    r.gain_sum[...] = jnp.zeros(r.gain_sum.shape, F32)

    def middle_back(band):
        value, part = rms_back(r.middle[band, :], r.gain2_row[...], acc_back[band, :])
        r.gain_sum[1:2, :] += part
        value = r.og[band, :].astype(F32) + value
        r.middle[band, :] = value
        r.low[band, :] = value.astype(BF16)

    bands(r.count, middle_back)
    for copy in save(steps - 1, (steps - 1) % 2):
        copy.wait()
    work.pause("ft")

    def mixed_back(band):
        r.d_mixed[:, band] = dot_nt(r.low[...], r.wo[band, :]).astype(BF16)

    bands(r.heads * VD, mixed_back, TILE)
    work.pause("dm")


def back_phase(work, r, d_query, d_keys, d_values, q_sum, k_sum, turned, v_part):
    heads_wide, narrow = r.heads * VD, r.heads * KD
    pairs = r.heads // 2
    tables = r.pick_a, r.pick_b, r.table
    back_state_body(
        r.query, r.mixed, r.inverse, r.d_mixed, *tables, r.d_state, r.d_total,
        work.between("c", pairs),
    )
    work.pause("e1")
    turned[...] = r.mixed[...].T

    def out_grads(band):
        r.out_g[:, band] = dot(turned[...], r.low[:, band]).astype(BF16)

    bands(r.width, out_grads, TILE)
    work.pause("og")
    turned[...] = r.normed[...].T
    attend_back_inside(
        r.query, r.keys, r.values, r.mixed, r.inverse, r.d_mixed, *tables, r.state, r.total,
        q_sum, k_sum, v_part, work.between("d", pairs),
    )
    work.pause("e1w")
    grid = GRID + (r.rows,)
    late_refs = dict(q=(d_query, q_sum), k=(d_keys, k_sum), v=(d_values, None))

    def late(index):
        spot = sum(high - low for group in r.late_groups[:index] for _, low, high in group)
        for name, low, high in r.late_groups[index]:
            ref, wide = late_refs[name]
            if wide is not None:
                ref[:, low:high] = wide[:, low:high].astype(BF16)
            for start in range(low, high, TILE):
                stop = min(start + TILE, high)
                value = dot(turned[...], ref[:, start:stop]).astype(BF16)
                size = stop - start
                r.late_g[:, :, :, :, :, :, spot : spot + size] = value.reshape(grid + (size,))
                spot += size

    late(0)
    work.pause("lq")

    def ended(pair):
        for spot, index in ((pairs // 2 - 1, 1), (pairs - 2, 2)):

            @pl.when(pair == spot)
            def _(index=index):
                late(index)
                work.pause(f"l{index}")

    attend_back_after(
        r.keys, r.values, *tables, r.d_state, r.d_total, k_sum, v_part, d_values,
        work.between("f", pairs), ended,
    )
    late(3)
    work.pause("l3")

    def back_norm(band):
        v_part[:, band] = (
            dot_nt(d_query[...], r.wq[band, :])
            + dot_nt(d_keys[...], r.wk[band, :])
            + dot_nt(d_values[...], r.wv[band, :])
        )

    bands(r.width, back_norm, TILE)
    work.pause("dn")

    def tokens_back(band):
        value, part = rms_back(r.tok[band, :].astype(F32), r.gain_row[...], v_part[band, :])
        r.gain_sum[0:1, :] += part
        r.middle[band, :] = r.middle[band, :] + value

    bands(r.count, tokens_back)
    quarter = r.width // 4
    for which in range(2):
        for part in range(4):
            spot = 4 * which + part
            r.gain_mine[0, spot : spot + 1, :] = r.gain_sum[
                which : which + 1, part * quarter : (part + 1) * quarter
            ]


class Refs:
    pass


def layer(tokens, gain, wq, wk, wv, wo, gain2, tables, shards3, out_grad):
    count, width = tokens.shape
    heads = wq.shape[1] // KD
    rows, columns = shards3[0].shape
    full = padded(columns)
    tall = rows // 2
    heads_wide, narrow = heads * VD, heads * KD
    last = heads_wide - 2 * VD
    late_groups = (
        (("q", 0, narrow),),
        (("v", 0, heads_wide // 2), ("k", 0, narrow // 2)),
        (("v", heads_wide // 2, last),),
        (("v", last, heads_wide), ("k", narrow // 2, narrow)),
    )
    late_sizes = [sum(high - low for _, low, high in group) for group in late_groups]
    edges = [0] + [part * TILE for part in PARTS]
    widest = max(*late_sizes, width // 2, *[high - low for low, high in zip(edges, edges[1:])])
    chunks = 6 * len(PARTS) + 4 + 2 * len(late_groups)
    gather_edges = [0] + [part * TILE for part in GATHER_PARTS]
    gathers = 6 * len(GATHER_PARTS)
    states = ((heads, VD, FEATS), BF16), ((heads, 1, FEATS), F32)
    sem = pltpu.SemaphoreType.DMA

    loads = dict(
        shard0=shards3[0], shard1=shards3[1], shard2=shards3[2], tok=tokens, wq=wq, wk=wk, wv=wv,
        og=out_grad, wo=wo,
    )
    inputs = {name + "_in": value for name, value in loads.items()}
    inputs |= dict(
        gain=gain, gain2=gain2, pick_a=tables[0], pick_b=tables[1], table=tables[2]
    )
    free_outs = dict(
        whole0=shape((width, full), BF16), whole1=shape((width, full), BF16),
        whole2=shape((width, full), BF16), grad0=shape((width, full), BF16),
        grad1=shape((width, full), BF16), grad2=shape((width, full), BF16),
        out_end=shape((count, width), BF16), tok_end=shape((count, width), F32),
    )
    outs = dict(
        g0=shape((rows, columns), F32), g1=shape((rows, columns), F32),
        g2=shape((rows, columns), F32), g_out=shape((rows, width), F32),
        g_value=shape((rows, heads_wide), F32), g_query=shape((rows, narrow), F32),
        g_keys=shape((rows, narrow), F32), g_gain=shape((8, width // 4), F32),
    )
    scratch = {name: pltpu.VMEM(value.shape, value.dtype) for name, value in loads.items()}
    scratch |= dict(
        out=pltpu.VMEM((count, width), BF16),
        middle=pltpu.VMEM((count, width), F32),
        load_sem=sem((len(loads),)), end_sem=sem((2,)),
        gain_row=pltpu.VMEM((1, width), F32), gain2_row=pltpu.VMEM((1, width), F32),
        normed=pltpu.VMEM((count, width), BF16),
        query=pltpu.VMEM((count, narrow), BF16),
        keys=pltpu.VMEM((count, narrow), BF16),
        values=pltpu.VMEM((count, heads_wide), BF16),
        mixed=pltpu.VMEM((count, heads_wide), BF16),
        inverse=pltpu.VMEM((count, heads_wide), F32),
        state=pltpu.VMEM(*states[0]), total=pltpu.VMEM(*states[1]),
        d_state=pltpu.VMEM(*states[0]), d_total=pltpu.VMEM(*states[1]),
        near_state=pltpu.VMEM(*states[0]), near_total=pltpu.VMEM(*states[1]),
        far_state=pltpu.VMEM(*states[0]), far_total=pltpu.VMEM(*states[1]),
        ex_sent=sem((6,)), ex_landed=sem((6,)),
        low=pltpu.VMEM((count, width), BF16),
        d_mixed=pltpu.VMEM((count, heads_wide), BF16),
        out_g=pltpu.VMEM((width, width), BF16),
        late_g=pltpu.VMEM(GRID + (rows, sum(late_sizes)), BF16),
        wide=pltpu.VMEM((3, rows, full), BF16),
        ag_sent=sem((gathers, 5)), ag_landed=sem((gathers, 5)), ag_local=sem((gathers,)),
        gain_sum=pltpu.VMEM((8, width), F32),
        gain_mine=pltpu.VMEM((3, 8, width // 4), F32),
        gain_slots=pltpu.VMEM((10, 8, width // 4), F32),
        gain_sent=sem((10,)), gain_landed=sem((10,)),
        p0=pltpu.VMEM((5, 2, 2, 2, 2, tall, widest), BF16),
        p1=pltpu.VMEM((4, 2, 2, 2, 2, tall, widest), BF16),
        p2=pltpu.VMEM((chunks, 2, 2, 2, tall, widest), BF16),
        p3=pltpu.VMEM((chunks, 2, 2, tall, widest), BF16),
        p4=pltpu.VMEM((chunks, 2, tall, widest), BF16),
        p5=pltpu.VMEM((chunks, tall, widest), BF16),
        rs_sent=sem((chunks, 5)), rs_landed=sem((chunks, 5)), rs_local=sem((chunks,)),
        credit=pltpu.SemaphoreType.REGULAR,
    )
    names = list(inputs) + list(free_outs) + list(outs) + list(scratch)

    def body(*refs):
        r = Refs()
        for name, ref in zip(names, refs):
            setattr(r, name, ref)
        r.count, r.width, r.heads, r.rows = count, width, heads, rows
        r.late_groups = late_groups
        r.place = place = Place()
        r.wholes_flat = [r.whole0, r.whole1, r.whole2]
        r.grads_flat = [r.grad0, r.grad1, r.grad2]
        grid = GRID + (rows,)
        wholes = [ref.reshape(grid + (full,)) for ref in r.wholes_flat]
        grads = [ref.reshape(grid + (full,)) for ref in r.grads_flat]
        def load(name):
            spot = list(loads).index(name)
            source = getattr(r, name + "_in")
            return pltpu.make_async_copy(source, getattr(r, name), r.load_sem.at[spot])

        r.ready = lambda *wanted: [load(name).wait() for name in wanted]
        r.ends = [
            lambda: pltpu.make_async_copy(r.out, r.out_end, r.end_sem.at[0]),
            lambda: pltpu.make_async_copy(r.middle, r.tok_end, r.end_sem.at[1]),
        ]
        for name in loads:
            load(name).start()
        enter(place)
        work = Work()
        r.gain_row[...] = r.gain[...].astype(F32).reshape(1, width)
        r.gain2_row[...] = r.gain2[...].astype(F32).reshape(1, width)
        r.ready("shard0", "shard1", "shard2")
        gather_list, sum_list, exchange_list, gain_list = work.kinds
        for spot, shard in enumerate((r.shard0, r.shard1, r.shard2)):
            r.wide[spot, :, columns:full] = jnp.zeros((rows, full - columns), BF16)
            r.wide[spot, :, 0:columns] = shard[...]
        for part, (low, high) in enumerate(zip(gather_edges, gather_edges[1:])):
            for weight in range(3):
                for kind, first in enumerate("yy" if (part, weight) in TURNED else "xy"):
                    order = len(gather_list)
                    gather_list.append(
                        Gather(
                            r.wide.at[weight], wholes[weight], pl.ds(kind * tall, tall),
                            pl.ds(low, high - low), first,
                            (r.ag_sent.at[order], r.ag_landed.at[order], r.ag_local.at[order]), place,
                        )
                    )
        pool = Pool(
            [r.p0, r.p1, r.p2, r.p3, r.p4, r.p5], (r.rs_sent, r.rs_landed, r.rs_local), r.credit,
            place, chunks,
        )

        def sums(source, low, high, target, firsts="xy"):
            for kind, first in enumerate(firsts):

                def put(value, kind=kind):
                    target(slice(kind * tall, (kind + 1) * tall), value)

                chunk_rows, chunk_columns = pl.ds(kind * tall, tall), pl.ds(low, high - low)
                sum_list.append(
                    Chunk(pool, len(sum_list), source, chunk_rows, chunk_columns, first, put)
                )

        def into(ref, low, high):
            def put(where, value):
                ref[where, low:high] = value[:, 0 : high - low]

            return put

        for low, high in zip(edges, edges[1:]):
            for source, target in zip(grads, (r.g0, r.g1, r.g2)):
                sums(source, low, high, into(target, low, min(high, columns)))
        half = width // 2
        for low in (0, half):
            target = into(r.g_out, low, low + half)
            sums(r.out_g.reshape(grid + (width,)), low, low + half, target, "yy")
        late_ends = dict(q=r.g_query, k=r.g_keys, v=r.g_value)
        spot = 0
        for group, size in zip(late_groups, late_sizes):

            def put_late(where, value, group=group):
                at = 0
                for name, low, high in group:
                    late_ends[name][where, low:high] = value[:, at : at + high - low]
                    at += high - low

            sums(r.late_g, spot, spot + size, put_late)
            spot += size
        for state, total, reverse in ((r.state, r.total, False), (r.d_state, r.d_total, True)):
            exchange_list.append(
                Exchange(
                    state, total, (r.near_state, r.near_total), (r.far_state, r.far_total),
                    r.ex_sent, r.ex_landed, place, reverse,
                )
            )
        gain_list.append(Gains(r.gain_mine, r.gain_slots, r.gain_sent, r.gain_landed, place))
        work.pause("s")
        front_phase(work, r)
        pl.run_scoped(
            lambda *buffers: feed_phase(work, r, *buffers),
            pltpu.VMEM((2, 3, width, TILE), BF16),
            pltpu.VMEM((2, 3, width, TILE), BF16),
            pltpu.VMEM((width, count), BF16),
            pltpu.VMEM((width, count), BF16),
            pltpu.VMEM((count, width), F32),
            pltpu.VMEM((count, width), F32),
            sem((2, 3)),
            sem((2, 3)),
        )
        pl.run_scoped(
            lambda *buffers: back_phase(work, r, *buffers),
            pltpu.VMEM((count, narrow), BF16),
            pltpu.VMEM((count, narrow), BF16),
            pltpu.VMEM((count, heads_wide), BF16),
            pltpu.VMEM((count, narrow), F32),
            pltpu.VMEM((count, narrow), F32),
            pltpu.VMEM((width, count), BF16),
            pltpu.VMEM((count, width), F32),
        )
        r.ends[1]().start()
        work.pause("z")
        r.ends[0]().wait()
        r.ends[1]().wait()
        r.g_gain[...] = r.gain_mine[2]

    vmem = pl.BlockSpec(memory_space=pltpu.VMEM)
    free = pl.BlockSpec(memory_space=pl.ANY)
    results = pl.pallas_call(
        body,
        out_shape=list(free_outs.values()) + list(outs.values()),
        in_specs=[free] * len(loads) + [vmem] * 5,
        out_specs=[free] * len(free_outs) + [vmem] * len(outs),
        scratch_shapes=list(scratch.values()),
        compiler_params=pltpu.CompilerParams(
            collective_id=0, has_side_effects=True, vmem_limit_bytes=VMEM_LIMIT
        ),
    )(*inputs.values())
    return results[6:]


def hand_over(results, gains):
    quarter = gains.shape[1]
    share = quarter // 8
    count = len(results)

    def body(*refs):
        sources, gain, targets = refs[:count], refs[count], refs[count + 1 : 2 * count + 1]
        first, second, sems = refs[2 * count + 1 :]
        copies = [
            pltpu.make_async_copy(a, b, sems.at[i]) for i, (a, b) in enumerate(zip(sources, targets))
        ]
        for copy in copies:
            copy.start()
        own = lax.axis_index("dp") * 4 + lax.axis_index("seq")
        turned = pltpu.roll(gain[...], lax.rem(quarter - own % 8 * share, quarter), 1)[:, 0:share]
        row = lax.broadcasted_iota(jnp.int32, turned.shape, 0)
        for ref, start in ((first, 0), (second, 4)):
            ref[...] = jnp.sum(only(row == start + own // 8, turned), axis=0, keepdims=True)
        for copy in copies:
            copy.wait()

    vmem = pl.BlockSpec(memory_space=pltpu.VMEM)
    free = pl.BlockSpec(memory_space=pl.ANY)
    return pl.pallas_call(
        body,
        out_shape=[shape(value.shape, value.dtype) for value in results] + [shape((1, share), F32)] * 2,
        in_specs=[vmem] * (count + 1),
        out_specs=[free] * count + [vmem] * 2,
        scratch_shapes=[pltpu.SemaphoreType.DMA((count,))],
    )(*results, gains)


def general(
    tokens, attn_gain, w_query, w_key, w_value, w_output, mlp_gain, w_gate, w_up, w_down, out_grad
):
    count, width = tokens.shape
    heads = w_query.shape[1] // KD
    all_values = heads * VD
    tables = feature_tables()
    inputs = tokens.astype(F32)
    gain = attn_gain.astype(F32).reshape(1, width)
    gate_full, up_full, down_full = (
        lax.all_gather(w, ("dp", "seq"), axis=0, tiled=True) for w in (w_gate, w_up, w_down)
    )
    normed, query, keys, values = call(
        project_body,
        [
            ((count, width), BF16),
            ((count, heads * KD), BF16),
            ((count, heads * KD), BF16),
            ((count, all_values), BF16),
        ],
        tokens,
        gain,
        w_query,
        w_key,
        w_value,
    )
    state_shapes = [((heads, VD, FEATS), BF16), ((heads, 1, FEATS), F32)]
    state, total = call(state_body, state_shapes, keys, values, *tables)
    state = before(lax.all_gather(state, "seq"), "seq").astype(BF16)
    total = before(lax.all_gather(total, "seq"), "seq")
    mixed, inverse = call(
        attend_body,
        [((count, all_values), BF16), ((count, all_values), F32)],
        query,
        keys,
        values,
        *tables,
        state,
        total,
    )
    middle = inputs + dot(mixed, w_output)
    normed_mlp, second_back = jax.vjp(rms_norm, middle, mlp_gain.astype(F32))
    mlp_low = normed_mlp.astype(BF16)
    gate = dot(mlp_low, gate_full)
    upward = dot(mlp_low, up_full)
    hidden_val, gated_back = jax.vjp(gated, gate, upward)
    hidden = hidden_val.astype(BF16)
    layer_out = (middle + dot_nt(hidden, down_full)).astype(BF16)
    d_hidden = dot(out_grad, down_full)
    down_grad = dot_tn(out_grad, hidden).astype(BF16)
    d_gate_f, d_up_f = gated_back(d_hidden)
    d_gate = d_gate_f.astype(BF16)
    d_up = d_up_f.astype(BF16)
    gate_grad = dot_tn(mlp_low, d_gate).astype(BF16)
    up_grad = dot_tn(mlp_low, d_up).astype(BF16)
    d_normed_mlp = dot_nt(d_gate, gate_full) + dot_nt(d_up, up_full)
    d_middle_norm, mlp_gain_part = second_back(d_normed_mlp)
    d_middle = out_grad.astype(F32) + d_middle_norm
    d_branch = d_middle.astype(BF16)
    output_grad = dot_tn(mixed, d_branch).astype(BF16)
    d_mixed = dot_nt(d_branch, w_output).astype(BF16)
    d_state, d_total = call(
        back_state_body, state_shapes, query, mixed, inverse, d_mixed, *tables
    )
    d_state = before(lax.all_gather(d_state, "seq"), "seq", True).astype(BF16)
    d_total = before(lax.all_gather(d_total, "seq"), "seq", True)
    d_query, d_keys, d_values = call(
        attend_back_body,
        [
            ((count, heads * KD), BF16),
            ((count, heads * KD), BF16),
            ((count, all_values), BF16),
        ],
        query,
        keys,
        values,
        mixed,
        inverse,
        d_mixed,
        *tables,
        state,
        total,
        d_state,
        d_total,
        scratch=[
            pltpu.VMEM((count, heads * KD), F32),
            pltpu.VMEM((count, heads * KD), F32),
            pltpu.VMEM((count, LANES), F32),
        ],
    )
    d_normed = dot_nt(d_query, w_query) + dot_nt(d_keys, w_key) + dot_nt(d_values, w_value)
    query_grad = dot_tn(normed, d_query).astype(BF16)
    key_grad = dot_tn(normed, d_keys).astype(BF16)
    value_grad = dot_tn(normed, d_values).astype(BF16)
    _, first_back = jax.vjp(rms_norm, inputs, attn_gain.astype(F32))
    d_inputs_norm, attn_gain_part = first_back(d_normed)
    tokens_grad = d_middle + d_inputs_norm
    parts = [query_grad, key_grad, value_grad, output_grad, gate_grad, up_grad, down_grad]
    joined = lax.psum_scatter(
        jnp.concatenate(parts, axis=1), ("dp", "seq"), scatter_dimension=0, tiled=True
    ).astype(F32)
    edges = np.cumsum([part.shape[1] for part in parts])[:-1]
    query_grad, key_grad, value_grad, output_grad, gate_grad, up_grad, down_grad = jnp.split(
        joined, edges, axis=1
    )
    gains = lax.psum_scatter(
        jnp.stack([attn_gain_part, mlp_gain_part], axis=1),
        ("dp", "seq"),
        scatter_dimension=0,
        tiled=True,
    )
    return (
        layer_out,
        tokens_grad,
        gains[:, 0],
        query_grad,
        key_grad,
        value_grad,
        output_grad,
        gains[:, 1],
        gate_grad,
        up_grad,
        down_grad,
    )


def shards(
    tokens, attn_gain, w_query, w_key, w_value, w_output, mlp_gain, w_gate, w_up, w_down, out_grad
):
    args = (
        tokens, attn_gain, w_query, w_key, w_value, w_output, mlp_gain, w_gate, w_up, w_down, out_grad
    )
    if (lax.axis_size("dp"), lax.axis_size("seq")) != (8, 4):
        return general(*args)
    *results, gains = layer(
        tokens, attn_gain, w_query, w_key, w_value, w_output, mlp_gain, feature_tables(),
        (w_gate, w_up, w_down), out_grad,
    )
    *results, gain_grad, gain2_grad = hand_over(results, gains)
    layer_out, tok_grad, gate_grad, up_grad, down_grad, output_grad, value_grad, query_grad, key_grad = results
    return (
        layer_out,
        tok_grad,
        gain_grad.reshape(-1),
        query_grad,
        key_grad,
        value_grad,
        output_grad,
        gain2_grad.reshape(-1),
        gate_grad,
        up_grad,
        down_grad,
    )


def solution(mesh):
    rows = P(("dp", "seq"), None)
    in_specs = (rows, P(), P(), P(), P(), P(), P(), rows, rows, rows, rows)
    out_specs = (
        rows,
        rows,
        P(("dp", "seq")),
        rows,
        rows,
        rows,
        rows,
        P(("dp", "seq")),
        rows,
        rows,
        rows,
    )
    return jax.shard_map(
        shards, mesh=mesh, in_specs=in_specs, out_specs=out_specs, check_vma=False
    )
```

```python
import functools
import math

import jax
import jax.numpy as jnp
import numpy as np
from jax import lax
from jax.experimental import pallas as pl
from jax.experimental.pallas import tpu as pltpu
from jax.sharding import PartitionSpec as P

KD = 16
VD = 64
LANES = 128
FEATS = 256
EPS = 1e-05
QUAD = 1.0 / (4.0 * math.sqrt(2.0))
F32 = jnp.float32
BF16 = jnp.bfloat16
VMEM_LIMIT = 62 << 20


def feature_tables():
    pick_a = np.zeros((LANES, FEATS), np.float32)
    pick_b = np.zeros((LANES, FEATS), np.float32)
    rows = np.zeros((8, FEATS), np.float32)
    spot = 0
    for a in range(KD):
        for b in range(a, KD):
            pick_a[a::KD, spot] = 1.0
            pick_b[b::KD, spot] = 1.0
            rows[2, spot] = QUAD
            rows[3, spot] = 1.0 if a == b else 2.0
            spot += 1
    for a in range(KD):
        pick_a[a::KD, spot] = 1.0
        rows[1, spot] = 1.0
        rows[2, spot] = 0.5
        rows[3, spot] = 1.0
        spot += 1
    rows[0:4, spot] = 1.0
    return jnp.asarray(pick_a, BF16), jnp.asarray(pick_b, BF16), jnp.asarray(rows)


def dot(left, right):
    return jnp.dot(left, right, preferred_element_type=F32)


def dot_nt(left, right):
    return lax.dot_general(left, right, (((1,), (1,)), ((), ())), preferred_element_type=F32)


def dot_tn(left, right):
    return lax.dot_general(left, right, (((0,), (0,)), ((), ())), preferred_element_type=F32)


def tile_at(index):
    return pl.ds(pl.multiple_of(index * LANES, LANES), LANES)


def head_lanes(rows, spot):
    return lax.broadcasted_iota(jnp.int32, (rows, LANES), 1) // KD == spot


def half_lanes(rows, half):
    return lax.broadcasted_iota(jnp.int32, (rows, LANES), 1) // VD == half


def halves_of(masked, pick_a, pick_b, rows):
    first = dot(masked, pick_a) + rows[0:1, :]
    second = dot(masked, pick_b) + rows[1:2, :]
    return first, second


def features_of(masked, pick_a, pick_b, rows):
    first, second = halves_of(masked, pick_a, pick_b, rows)
    return (first * second * rows[2:3, :]).astype(BF16)


def only(mask, value):
    return jnp.where(mask, value, jnp.zeros_like(value))


def project_body(tok, gain, wq, wk, wv, normed, query, keys, values):
    x = tok[...].astype(F32)
    scale = lax.rsqrt(jnp.mean(x * x, axis=-1, keepdims=True) + EPS)
    normed[...] = (x * scale * gain[...]).astype(BF16)
    query[...] = dot(normed[...], wq[...]).astype(BF16)
    keys[...] = dot(normed[...], wk[...]).astype(BF16)
    values[...] = dot(normed[...], wv[...]).astype(BF16)


def state_body(keys, values, pick_a, pick_b, rows, state, total, between=None):
    pairs = values.shape[1] // LANES
    count = keys.shape[0]

    def step(pair, carry):
        turned = values[:, tile_at(pair)].T
        for half in range(2):
            head = pair * 2 + half
            masked = only(head_lanes(count, head % 8), keys[:, tile_at(head // 8)])
            feat = features_of(masked, pick_a[...], pick_b[...], rows[...])
            sums = dot(turned[half * VD : (half + 1) * VD, :], feat)
            state[head] = (sums * rows[3:4, :]).astype(BF16)
            total[head] = jnp.sum(feat.astype(F32), axis=0, keepdims=True) * rows[3:4, :]
        if between is not None:
            between(pair)
        return carry

    lax.fori_loop(0, pairs, step, 0)


def causal(rows, columns, row_start, column_start):
    row = lax.broadcasted_iota(jnp.int32, (rows, columns), 0) + row_start
    column = lax.broadcasted_iota(jnp.int32, (rows, columns), 1) + column_start
    return row >= column


def attend_body(query, keys, values, pick_a, pick_b, rows, state, total, mixed, inverse, between=None, block=256):
    pairs = values.shape[1] // LANES
    count = keys.shape[0]

    def step(pair, carry):
        vals = values[:, tile_at(pair)]
        for start in range(0, count, block):
            stop = start + block
            numer = None
            for half in range(2):
                head = pair * 2 + half
                masked = only(head_lanes(block, head % 8), query[start:stop, tile_at(head // 8)])
                score = dot_nt(masked, keys[0:stop, tile_at(head // 8)]) * 0.25
                weight = 1.0 + score + 0.5 * score * score
                weight = jnp.where(causal(block, stop, start, 0), weight, 0.0)
                feat = features_of(masked, pick_a[...], pick_b[...], rows[...])
                inter = feat.astype(F32) * total[head]
                denom = jnp.sum(weight, axis=1, keepdims=True) + jnp.sum(
                    inter, axis=1, keepdims=True
                )
                across = dot_nt(feat, state[head])
                both = dot(weight.astype(BF16), vals[0:stop, :])
                across = jnp.concatenate([across, across], axis=1)
                whole = (both + across) / denom
                flip = jnp.broadcast_to(1.0 / denom, (block, LANES))
                if half == 0:
                    numer, invs = whole, flip
                else:
                    mask = half_lanes(block, 0)
                    numer = jnp.where(mask, numer, whole)
                    invs = jnp.where(mask, invs, flip)
            mixed[start:stop, tile_at(pair)] = numer.astype(BF16)
            inverse[start:stop, tile_at(pair)] = invs
        if between is not None:
            between(pair)
        return carry

    lax.fori_loop(0, pairs, step, 0)


def spare_lane(rows, spot):
    lane = lax.broadcasted_iota(jnp.int32, (rows, LANES), 1)
    return lane == lax.rem(spot * KD + KD, LANES)


def query_side(value, spot):
    rows = value.shape[0]
    quarter = only(head_lanes(rows, spot), value * 0.25)
    return jnp.where(spare_lane(rows, spot), jnp.ones_like(value), quarter)


def key_side(value, spot):
    return jnp.where(spare_lane(value.shape[0], spot), jnp.ones_like(value), value)


def triangle(value, start, block, upper=False):
    row = lax.broadcasted_iota(jnp.int32, (block, block), 0)
    column = lax.broadcasted_iota(jnp.int32, (block, block), 1)
    keep = row <= column if upper else row >= column
    pieces = [value[:, 0:start]] if start > 0 else []
    pieces.append(only(keep, value[:, start : start + block]))
    if start + block < value.shape[1]:
        pieces.append(value[:, start + block :])
    return jnp.concatenate(pieces, axis=1) if len(pieces) > 1 else pieces[0]


def attend_inside(query, keys, values, numer, denoms, between, block=512):
    pairs = values.shape[1] // LANES
    count = keys.shape[0]

    def step(pair, carry):
        vals = values[:, tile_at(pair)]
        for start in range(0, count, block):
            stop = start + block
            for half in range(2):
                head = pair * 2 + half
                place = tile_at(head // 8)
                plus = dot_nt(
                    query_side(query[start:stop, place], head % 8), key_side(keys[0:stop, place], head % 8)
                )
                weight = triangle(0.5 * plus * plus + 0.5, start, block)
                flip = jnp.broadcast_to(jnp.sum(weight, axis=1, keepdims=True), (block, LANES))
                both = dot(weight.astype(BF16), vals[0:stop, :])
                if half == 0:
                    whole, wides = both, flip
                else:
                    mask = half_lanes(block, 0)
                    numer[start:stop, tile_at(pair)] = jnp.where(mask, whole, both)
                    denoms[start:stop, tile_at(pair)] = jnp.where(mask, wides, flip)
        between(pair)
        return carry

    lax.fori_loop(0, pairs, step, 0)


def attend_before(query, pick_a, pick_b, rows, state, total, numer, inverse, mixed, between):
    count = query.shape[0]
    pairs = mixed.shape[1] // LANES

    def step(pair, carry):
        spot = tile_at(pair)
        for half in range(2):
            head = pair * 2 + half
            masked = only(head_lanes(count, head % 8), query[:, tile_at(head // 8)])
            feat = features_of(masked, pick_a[...], pick_b[...], rows[...])
            inter = jnp.sum(feat.astype(F32) * total[head], axis=1, keepdims=True)
            inter = jnp.broadcast_to(inter, (count, LANES))
            across = dot_nt(feat, state[head])
            across = jnp.concatenate([across, across], axis=1)
            if half == 0:
                whole, wides = across, inter
            else:
                mask = half_lanes(count, 0)
                whole = jnp.where(mask, whole, across)
                wides = jnp.where(mask, wides, inter)
        flipped = 1.0 / (inverse[:, spot] + wides)
        inverse[:, spot] = flipped
        mixed[:, spot] = ((numer[:, spot] + whole) * flipped).astype(BF16)
        between(pair)
        return carry

    lax.fori_loop(0, pairs, step, 0)


def back_state_body(query, mixed, inverse, d_mixed, pick_a, pick_b, rows, d_state, d_total, between=None):
    pairs = mixed.shape[1] // LANES
    count = query.shape[0]

    def step(pair, carry):
        spot = tile_at(pair)
        d_numer = d_mixed[:, spot].astype(F32) * inverse[:, spot]
        lost = d_numer * mixed[:, spot].astype(F32)
        turned = d_numer.astype(BF16).T
        for half in range(2):
            head = pair * 2 + half
            masked = only(head_lanes(count, head % 8), query[:, tile_at(head // 8)])
            feat = features_of(masked, pick_a[...], pick_b[...], rows[...])
            d_denom = -jnp.sum(only(half_lanes(count, half), lost), axis=1, keepdims=True)
            sums = dot(turned[half * VD : (half + 1) * VD, :], feat)
            d_state[head] = (sums * rows[3:4, :]).astype(BF16)
            d_total[head] = (
                jnp.sum(feat.astype(F32) * d_denom, axis=0, keepdims=True) * rows[3:4, :]
            )
        if between is not None:
            between(pair)
        return carry

    lax.fori_loop(0, pairs, step, 0)


def feature_back(d_feat, first, second, pick_a, pick_b, rows):
    scaled = d_feat * rows[2:3, :]
    return dot_nt((scaled * second).astype(BF16), pick_a) + dot_nt(
        (scaled * first).astype(BF16), pick_b
    )


def attend_back_body(
    query,
    keys,
    values,
    mixed,
    inverse,
    d_mixed,
    pick_a,
    pick_b,
    rows,
    state,
    total,
    d_state,
    d_total,
    d_query,
    d_keys,
    d_values,
    q_sum,
    k_sum,
    v_sum,
    between=None,
    block=256,
):
    pairs = values.shape[1] // LANES
    count = keys.shape[0]
    q_sum[...] = jnp.zeros_like(q_sum)
    k_sum[...] = jnp.zeros_like(k_sum)

    def step(pair, carry):
        spot = tile_at(pair)
        d_numer = d_mixed[:, spot].astype(F32) * inverse[:, spot]
        lost = d_numer * mixed[:, spot].astype(F32)
        d_low = d_numer.astype(BF16)
        turned = pltpu.roll(lost, VD, 1)
        vals = values[:, spot]
        for half in range(2):
            head = pair * 2 + half
            place = tile_at(head // 8)
            mine = half_lanes(count, half)
            lanes = head_lanes(count, head % 8)
            d_denom = -jnp.sum(only(mine, lost), axis=1, keepdims=True)
            d_wide = jnp.where(mine, d_numer, -turned).astype(BF16)
            v_wide = jnp.where(mine, vals, jnp.ones_like(vals))
            q_mask = only(lanes, query[:, place])
            k_mask = only(lanes, keys[:, place])
            grads_q, grads_k, grads_v = [], [], []
            for start in range(0, count, block):
                stop = start + block
                score = dot_nt(q_mask[start:stop], k_mask[0:stop]) * 0.25
                d_weight = dot_nt(d_wide[start:stop], v_wide[0:stop])
                d_score = only(causal(block, stop, start, 0), d_weight * (1.0 + score))
                grads_q.append(dot(d_score.astype(BF16), k_mask[0:stop]))
                rest = count - start
                score = dot_nt(k_mask[start:stop], q_mask[start:count]) * 0.25
                mask = causal(rest, block, 0, 0)
                mask = (
                    lax.broadcasted_iota(jnp.int32, (block, rest), 0)
                    <= lax.broadcasted_iota(jnp.int32, (block, rest), 1)
                )
                weight = only(mask, 1.0 + score + 0.5 * score * score)
                d_weight = dot_nt(v_wide[start:stop], d_wide[start:count])
                d_score = only(mask, d_weight * (1.0 + score))
                grads_k.append(dot(d_score.astype(BF16), q_mask[start:count]))
                grads_v.append(dot(weight.astype(BF16), d_low[start:count]))
            first, second = halves_of(q_mask, pick_a[...], pick_b[...], rows[...])
            d_feat = dot(d_low[:, half * VD : (half + 1) * VD], state[head]) + d_denom * total[head]
            inter_q = feature_back(d_feat, first, second, pick_a[...], pick_b[...], rows[...])
            first, second = halves_of(k_mask, pick_a[...], pick_b[...], rows[...])
            feat = (first * second * rows[2:3, :]).astype(BF16)
            d_feat = dot(vals[:, half * VD : (half + 1) * VD], d_state[head]) + d_total[head]
            inter_k = feature_back(d_feat, first, second, pick_a[...], pick_b[...], rows[...])
            inter_v = dot_nt(feat, d_state[head])
            inter_v = jnp.concatenate([inter_v, inter_v], axis=1)
            whole_v = jnp.concatenate(grads_v, axis=0) + inter_v
            v_sum[...] = whole_v if half == 0 else jnp.where(mine, whole_v, v_sum[...])
            q_sum[:, place] += jnp.concatenate(grads_q, axis=0) * 0.25 + only(lanes, inter_q)
            k_sum[:, place] += jnp.concatenate(grads_k, axis=0) * 0.25 + only(lanes, inter_k)
        d_values[:, spot] = v_sum[...].astype(BF16)
        if between is not None:
            between(pair)
        return carry

    lax.fori_loop(0, pairs, step, 0)
    d_query[...] = q_sum[...].astype(BF16)
    d_keys[...] = k_sum[...].astype(BF16)


def attend_back_inside(
    query, keys, values, mixed, inverse, d_mixed, pick_a, pick_b, rows, state, total, q_sum, k_sum,
    v_part, between, block=512,
):
    pairs = values.shape[1] // LANES
    count = keys.shape[0]
    q_sum[...] = jnp.zeros_like(q_sum)
    k_sum[...] = jnp.zeros_like(k_sum)

    def step(pair, carry):
        spot = tile_at(pair)
        d_numer = d_mixed[:, spot].astype(F32) * inverse[:, spot]
        lost = d_numer * mixed[:, spot].astype(F32)
        d_low = d_numer.astype(BF16)
        turned = pltpu.roll(lost, VD, 1)
        vals = values[:, spot]
        for half in range(2):
            head = pair * 2 + half
            place = tile_at(head // 8)
            mine = half_lanes(count, half)
            lanes = head_lanes(count, head % 8)
            d_wide = jnp.where(mine, d_numer, -turned).astype(BF16)
            v_wide = jnp.where(mine, vals, jnp.ones_like(vals))
            q_tile, k_tile = query[:, place], keys[:, place]
            q_mask = only(lanes, q_tile)
            q_quarter, k_quarter = q_mask * 0.25, only(lanes, k_tile) * 0.25
            q_plus, k_plus = query_side(q_tile, head % 8), key_side(k_tile, head % 8)
            grads_q, grads_k, grads_v = [], [], []
            for start in range(0, count, block):
                stop = start + block
                plus = dot_nt(q_plus[start:stop], k_plus[0:stop])
                d_weight = dot_nt(d_wide[start:stop], v_wide[0:stop])
                d_score = triangle(d_weight * plus, start, block)
                grads_q.append(dot(d_score.astype(BF16), k_quarter[0:stop]))
                plus = dot_nt(k_plus[start:stop], q_plus[start:count])
                weight = triangle(0.5 * plus * plus + 0.5, 0, block, True)
                d_weight = dot_nt(v_wide[start:stop], d_wide[start:count])
                d_score = triangle(d_weight * plus, 0, block, True)
                grads_k.append(dot(d_score.astype(BF16), q_quarter[start:count]))
                grads_v.append(dot(weight.astype(BF16), d_low[start:count]))
            first, second = halves_of(q_mask, pick_a[...], pick_b[...], rows[...])
            high = total[head].astype(BF16)
            rest = (total[head] - high.astype(F32)).astype(BF16)
            sums = [jnp.broadcast_to(part, (VD, FEATS)) for part in (high, rest)]
            zero = jnp.zeros((VD, FEATS), BF16)
            own = [state[head], sums[0]], [zero, sums[1]]
            order = [part for group in own for part in (group if half == 0 else group[::-1])]
            d_feat = dot(
                jnp.concatenate([d_wide, d_wide], axis=1), jnp.concatenate(order, axis=0)
            )
            inter_q = feature_back(d_feat, first, second, pick_a[...], pick_b[...], rows[...])
            whole_v = jnp.concatenate(grads_v, axis=0)
            v_part[:, spot] = whole_v if half == 0 else jnp.where(mine, whole_v, v_part[:, spot])
            q_sum[:, place] += jnp.concatenate(grads_q, axis=0) + only(lanes, inter_q)
            k_sum[:, place] += jnp.concatenate(grads_k, axis=0)
        between(pair)
        return carry

    lax.fori_loop(0, pairs, step, 0)


def attend_back_after(
    keys, values, pick_a, pick_b, rows, d_state, d_total, k_sum, v_part, d_values, between, ended
):
    pairs = values.shape[1] // LANES
    count = keys.shape[0]

    def step(pair, carry):
        spot = tile_at(pair)
        vals = values[:, spot]
        for half in range(2):
            head = pair * 2 + half
            place = tile_at(head // 8)
            lanes = head_lanes(count, head % 8)
            k_mask = only(lanes, keys[:, place])
            first, second = halves_of(k_mask, pick_a[...], pick_b[...], rows[...])
            feat = (first * second * rows[2:3, :]).astype(BF16)
            d_feat = dot(vals[:, half * VD : (half + 1) * VD], d_state[head]) + d_total[head]
            inter_k = feature_back(d_feat, first, second, pick_a[...], pick_b[...], rows[...])
            inter_v = dot_nt(feat, d_state[head])
            inter_v = jnp.concatenate([inter_v, inter_v], axis=1)
            k_sum[:, place] += only(lanes, inter_k)
            whole_v = v_part[:, spot] + inter_v
            mask = half_lanes(count, half)
            whole_v = whole_v if half == 0 else jnp.where(mask, whole_v, v_part[:, spot])
            if half == 0:
                v_part[:, spot] = jnp.where(mask, whole_v, v_part[:, spot])
            else:
                d_values[:, spot] = whole_v.astype(BF16)
        between(pair)
        ended(pair)
        return carry

    lax.fori_loop(0, pairs, step, 0)


def call(body, shapes, *operands, scratch=()):
    return pl.pallas_call(
        body,
        out_shape=[jax.ShapeDtypeStruct(shape, kind) for shape, kind in shapes],
        scratch_shapes=list(scratch),
        compiler_params=pltpu.CompilerParams(vmem_limit_bytes=VMEM_LIMIT),
    )(*operands)


def rms_norm(inputs, gain):
    return inputs * lax.rsqrt(jnp.mean(inputs * inputs, axis=-1, keepdims=True) + EPS) * gain


def gated(gate_in, up_in):
    return jax.nn.silu(gate_in) * up_in


def before(parts, axis, reverse=False):
    place = lax.axis_index(axis)
    order = jnp.arange(parts.shape[0])
    chosen = order > place if reverse else order < place
    chosen = chosen.reshape((-1,) + (1,) * (parts.ndim - 1))
    return jnp.sum(jnp.where(chosen, parts.astype(F32), 0.0), axis=0)


MESH_ID = pl.DeviceIdType.MESH


class Place:
    def __init__(self):
        self.dp, self.seq = lax.axis_index("dp"), lax.axis_index("seq")
        self.z, self.y = self.dp // 2, self.dp % 2
        self.x, self.core = self.seq // 2, self.seq % 2
        self.zh, self.zl = self.z // 2, self.z % 2

    def at(self, z=None, y=None, x=None, core=None):
        z = self.z if z is None else z
        y = self.y if y is None else y
        x = self.x if x is None else x
        core = self.core if core is None else core
        return (z * 2 + y, x * 2 + core)

    def mate(self):
        return self.at(core=1 - self.core)

    def across(self, axis):
        return self.at(y=1 - self.y) if axis == "y" else self.at(x=1 - self.x)

    def own(self, axis):
        return self.y if axis == "y" else self.x


def remote(source, target, sent, landed, device):
    return pltpu.make_async_remote_copy(
        src_ref=source,
        dst_ref=target,
        send_sem=sent,
        recv_sem=landed,
        device_id=device,
        device_id_type=MESH_ID,
    )


def enter(place):
    barrier = pltpu.get_barrier_semaphore()
    others = [(place.dp, jnp.bitwise_xor(place.seq, other)) for other in range(1, 4)]
    others += [(jnp.bitwise_xor(place.dp, other), place.seq) for other in range(1, 8)]
    for device in others:
        pl.semaphore_signal(barrier, inc=1, device_id=device, device_id_type=MESH_ID)
    pl.semaphore_wait(barrier, len(others))


class Gather:
    def __init__(self, shard, whole, rows, columns, first, sems, place):
        self.shard, self.whole, self.rows, self.columns = shard, whole, rows, columns
        self.first, self.third = first, "x" if first == "y" else "y"
        self.sems, self.place = sems, place

    def block(self, high, low, one, three, core=None):
        core = self.place.core if core is None else core
        grid = (one, three) if self.first == "y" else (three, one)
        return self.whole.at[(high, low) + grid + (core, self.rows, self.columns)]

    def move(self, ref, spot, device, source=None):
        sent, landed, _ = self.sems
        source = ref if source is None else source
        return remote(source, ref, sent.at[spot], landed.at[spot], device)

    def copies(self):
        place, every = self.place, slice(None)
        own1, own3 = place.own(self.first), place.own(self.third)
        mine = self.shard.at[self.rows, self.columns]
        block = self.block
        zh, zl = place.zh, place.zl

        def keep():
            return pltpu.make_async_copy(mine, block(zh, zl, own1, own3), self.sems[2])

        def far(high):
            device = place.at(z=jnp.bitwise_xor(place.z, 2))
            return self.move(block(high, zl, own1, own3), 0, device, mine)

        def cross(three):
            return self.move(block(every, zl, own1, three), 1, place.across(self.third))

        def near(low):
            device = place.at(z=jnp.bitwise_xor(place.z, 1))
            return self.move(block(every, low, own1, every), 2, device)

        def over(one):
            return self.move(block(every, every, one, every), 3, place.across(self.first))

        def mate(core):
            return self.move(block(every, every, every, every, core), 4, place.mate())

        return keep, [
            (far, zh, 1 - zh),
            (cross, own3, 1 - own3),
            (near, zl, 1 - zl),
            (over, own1, 1 - own1),
            (mate, place.core, 1 - place.core),
        ]

    def step(self, index):
        keep, stages = self.copies()
        if index == 0:
            keep().start()
        if index == 1:
            keep().wait()
        if index > 0:
            act, _, theirs = stages[index - 1]
            act(theirs).wait_recv()
        if index < 5:
            act, own, _ = stages[index]
            act(own).start()
        else:
            for act, own, _ in stages:
                act(own).wait_send()


class Pool:
    def __init__(self, refs, sems, free, place, chunks):
        self.refs, self.sems, self.free, self.place, self.chunks = refs, sems, free, place, chunks
        self.kept, self.landing = refs[0].shape[0], refs[1].shape[0]


class Chunk:
    def __init__(self, pool, order, source, rows, columns, first, put):
        self.pool, self.place, self.put = pool, pool.place, put
        self.order = order
        self.source, self.rows, self.columns, self.first = source, rows, columns, first
        self.third = "x" if first == "y" else "y"
        self.width = columns.size

    def ref(self, kind):
        spot = self.order
        if kind == 0:
            spot = spot % self.pool.kept
        if kind == 1:
            spot = spot % self.pool.landing
        return self.pool.refs[kind].at[spot]

    def cut(self, ref):
        return ref.at[(slice(None),) * (len(ref.shape) - 1) + (pl.ds(0, self.width),)]

    def share(self, core):
        every = slice(None)
        return self.source.at[every, every, every, every, core, self.rows, self.columns]

    def pick(self, which):
        mine = self.ref(0)
        return mine.at[:, :, which] if self.first == "y" else mine.at[:, :, :, which]

    def fetch(self):
        return pltpu.make_async_copy(
            self.share(self.place.core), self.cut(self.ref(0)), self.pool.sems[2].at[self.order]
        )

    def send(self, ref, target, spot, device):
        sent, landed = self.pool.sems[0].at[self.order, spot], self.pool.sems[1].at[self.order, spot]
        return remote(ref, self.cut(target), sent, landed, device)

    def to_mate(self):
        return self.send(self.share(1 - self.place.core), self.ref(1), 0, self.place.mate())

    def to_over(self):
        own = self.place.own(self.first)
        return self.send(
            self.cut(self.pick(1 - own)), self.ref(2), 1, self.place.across(self.first)
        )

    def to_near(self):
        place = self.place
        source = self.cut(self.ref(2).at[:, 1 - place.zl])
        return self.send(source, self.ref(3), 2, place.at(z=jnp.bitwise_xor(place.z, 1)))

    def to_cross(self):
        own = self.place.own(self.third)
        source = self.cut(self.ref(3).at[:, 1 - own])
        return self.send(source, self.ref(4), 3, self.place.across(self.third))

    def to_far(self):
        place = self.place
        source = self.cut(self.ref(4).at[1 - place.zh])
        return self.send(source, self.ref(5), 4, place.at(z=jnp.bitwise_xor(place.z, 2)))

    def view(self, ref):
        return self.cut(ref)

    def step(self, index):
        pool, place, order = self.pool, self.place, self.order
        if index == 0:
            if order >= pool.landing:
                pl.semaphore_wait(pool.free, 1)
            self.fetch().start()
            self.to_mate().start()
        elif index == 1:
            self.fetch().wait()
            self.to_mate().wait_recv()
            mine = self.cut(self.ref(0))
            mine[...] = mine[...] + self.cut(self.ref(1))[...]
            if order + pool.landing < pool.chunks:
                pl.semaphore_signal(
                    pool.free, inc=1, device_id=place.mate(), device_id_type=MESH_ID
                )
            self.to_over().start()
        elif index == 2:
            self.to_over().wait()
            over = self.cut(self.ref(2))
            over[...] = over[...] + self.cut(self.pick(place.own(self.first)))[...]
            self.to_near().start()
        elif index == 3:
            self.to_near().wait_recv()
            near = self.cut(self.ref(3))
            near[...] = near[...] + self.cut(self.ref(2).at[:, place.zl])[...]
            self.to_cross().start()
        elif index == 4:
            self.to_cross().wait_recv()
            cross = self.cut(self.ref(4))
            cross[...] = cross[...] + self.cut(self.ref(3).at[:, place.own(self.third)])[...]
            self.to_far().start()
        else:
            self.to_far().wait_recv()
            final = self.cut(self.ref(4).at[place.zh])[...].astype(F32)
            self.put(final + self.cut(self.ref(5))[...].astype(F32))
            self.to_mate().wait_send()
            self.to_near().wait_send()
            self.to_cross().wait_send()
            self.to_far().wait_send()


class Gains:
    def __init__(self, mine, slots, sent, landed, place):
        self.mine, self.slots, self.sent, self.landed, self.place = mine, slots, sent, landed, place

    def swaps(self, index):
        place = self.place
        if index == 0:
            partners = [(place.dp, jnp.bitwise_xor(place.seq, k)) for k in range(1, 4)]
        else:
            partners = [(jnp.bitwise_xor(place.dp, k), place.seq) for k in range(1, 8)]
        for spot, partner in enumerate(partners):
            spot += 3 * index
            yield spot, remote(
                self.mine.at[index], self.slots.at[spot], self.sent.at[spot], self.landed.at[spot],
                partner,
            )

    def step(self, index):
        if index > 0:
            value = self.mine[index - 1]
            for spot, swap in self.swaps(index - 1):
                swap.wait()
                value = value + self.slots[spot]
            self.mine[index] = value
        if index < 2:
            for _, swap in self.swaps(index):
                swap.start()


class Exchange:
    def __init__(self, state, total, near, far, sent, landed, place, reverse):
        self.state, self.total, self.near, self.far = state, total, near, far
        self.sent, self.landed, self.place, self.reverse = sent, landed, place, reverse
        self.half = state.shape[0] // 2

    def move(self, source, target, spot, device):
        return remote(source, target, self.sent.at[spot], self.landed.at[spot], device)

    def to_mate(self):
        pairs = zip((self.state, self.total), self.near)
        return [self.move(a, b, i, self.place.mate()) for i, (a, b) in enumerate(pairs)]

    def part(self, spot, core, device):
        part = pl.ds(core * self.half, self.half)
        return [
            self.move(ref.at[part], ref.at[part], spot + i, device) for i, ref in enumerate(self.far)
        ]

    def over(self):
        return self.part(2, self.place.core, self.place.across("x"))

    def share(self, core):
        return self.part(4, core, self.place.mate())

    def step(self, index):
        place, reverse = self.place, self.reverse
        giving = place.x == (1 if reverse else 0)
        taking = place.x == (0 if reverse else 1)
        second = place.core == (0 if reverse else 1)
        state, total = self.state, self.total
        (near_state, near_total), (far_state, far_total) = self.near, self.far
        if index == 0:
            for copy in self.to_mate():
                copy.start()
        elif index == 1:
            for copy in self.to_mate():
                copy.wait_recv()

            @pl.when(giving)
            def _():
                part = pl.ds(place.core * self.half, self.half)
                far_state[part] = state[part] + near_state[part]
                far_total[part] = total[part] + near_total[part]
                for copy in self.over():
                    copy.start()

        elif index == 2:

            @pl.when(taking)
            def _():
                for copy in self.over():
                    copy.wait_recv()
                for copy in self.share(place.core):
                    copy.start()

        else:

            @pl.when(taking)
            def _():
                for copy in self.share(1 - place.core):
                    copy.wait_recv()
                for copy in self.share(place.core):
                    copy.wait_send()

            for copy in self.to_mate():
                copy.wait_send()

            @pl.when(giving)
            def _():
                for copy in self.over():
                    copy.wait_send()

            @pl.when(jnp.logical_and(giving, second))
            def _():
                state[...] = near_state[...]
                total[...] = near_total[...]

            @pl.when(jnp.logical_and(giving, jnp.logical_not(second)))
            def _():
                state[...] = jnp.zeros_like(state)
                total[...] = jnp.zeros_like(total)

            @pl.when(jnp.logical_and(taking, second))
            def _():
                state[...] = far_state[...] + near_state[...]
                total[...] = far_total[...] + near_total[...]

            @pl.when(jnp.logical_and(taking, jnp.logical_not(second)))
            def _():
                state[...] = far_state[...]
                total[...] = far_total[...]


class Work:
    def __init__(self):
        self.kinds = ([], [], [], [])

    def pause(self, name):
        for code in PLAN.get(name, ()):
            self.kinds[code // 1000][code % 1000 // 10].step(code % 10)

    def between(self, prefix, count, halves=False):
        def hook(index, half=""):
            for spot in range(count):
                name = f"{prefix}{spot}{half}"
                if name in PLAN:

                    @pl.when(index == spot)
                    def _():
                        self.pause(name)

        return hook


PLAN = {
    's': (0, 10,),
    'qk': (20,),
    'v': (30,),
    'st0': (1, 40,),
    'st2': (11, 50,),
    'st4': (21, 60,),
    'st6': (2, 31,),
    'e0': (2000,),
    'a0': (41,),
    'a1': (51,),
    'a2': (2001, 12, 61,),
    'a4': (22,),
    'a7': (32,),
    'e0w': (3, 13, 2002, 42, 2003,),
    'b0': (23, 52,),
    'b4': (4, 14, 43, 62,),
    'b7': (33, 70,),
    'po': (5, 15, 80,),
    'nm': (90,),
    'p0': (24, 63, 100, 110, 53, 44, 120, 25, 130, 34, 140, 45, 71, 150, 91, 81, 160, 35, 111, 170, 64, 101, 131, 72, 121, 54, 151, 141, 65, 161, 82, 171, 55,),
    't0': (73, 92,),
    't1': (83, 102,),
    't2': (93, 112,),
    'm3': (122, 74, 103, 132, 84, 113, 75, 142, 123, 94, 85, 152, 133, 162, 104, 95, 143, 172, 114, 105, 153, 124, 163, 115,),
    't3': (125, 134,),
    'm4': (144, 173, 1000, 1010, 1020, 1030,),
    't4': (135,),
    'm5': (145, 154,),
    't5': (164, 1001, 1011, 1040,),
    'm6': (1021,),
    't6': (174, 1031,),
    'm7': (155, 165, 1041, 175,),
    't7': (1002, 1012, 1050,),
    'm8': (1060,),
    't8': (1051,),
    'm9': (1003, 1061, 1022, 1070,),
    't9': (1032, 1080,),
    'm10': (1013, 1071,),
    't10': (1023, 1081,),
    'ft': (1042, 1052, 1090, 1100,),
    'dm': (1004, 1033,),
    'c0': (1091,),
    'c1': (1101,),
    'c2': (1043, 1062, 1110,),
    'c4': (1014, 1072, 1120,),
    'c5': (1053, 1024, 1111,),
    'c6': (1005,),
    'c7': (1121,),
    'e1': (2010,),
    'og': (2011, 1015, 1063, 1082, 1130,),
    'd0': (1025, 1034, 1044, 1092, 1131, 1140,),
    'd1': (1035, 1073, 1083, 1102, 1054, 1112, 1045, 1141, 1150, 1160,),
    'd2': (1064, 1093, 1151, 1161, 1122, 1170,),
    'd3': (1055, 1084, 1103, 1132, 1171, 1180,),
    'd4': (2012, 1065, 1074, 1113, 1123, 1152, 1181,),
    'd5': (2013, 1075, 1085, 1104, 1133, 1142, 1190, 1200,),
    'd6': (1105, 1094, 1124, 1153, 1172, 1191, 1201, 1143,),
    'd7': (1095, 1125, 1114, 1134, 1162, 1182, 1210,),
    'lq': (1154, 1192, 1220, 1230,),
    'f0': (1173, 1211,),
    'f1': (1115, 1202, 1135, 1221, 1231,),
    'f2': (1144, 1174, 1163,),
    'f3': (1183, 1222, 1212,),
    'l1': (1155, 1240, 1250, 1232,),
    'f4': (1164, 1184, 1193, 1203,),
    'f5': (1145, 1241, 1251,),
    'f6': (1175, 1194, 1204, 1223,),
    'l2': (1213, 1260, 1270,),
    'f7': (1233, 1165,),
    'l3': (1185, 1261, 1280, 1271, 1242, 1252, 1290,),
    'dn': (1195, 1205, 1214, 1224, 1234, 1243, 1262, 1272, 1281, 1291,),
    'z': (1215, 1225, 1244, 1253, 1235, 3000, 1282, 1263, 1292, 1273, 1254, 3001, 1245, 1264, 1283, 1293, 1274, 1255, 1284, 3002, 1294, 1265, 1275, 1285, 1295,),
}


def normalize(value, gain):
    return value * lax.rsqrt(jnp.mean(value * value, axis=-1, keepdims=True) + EPS) * gain


GRID = (2, 2, 2, 2, 2)
PARTS = (4, 8, 11)
GATHER_PARTS = (4, 8, 11)
TURNED = ((0, 1),)
BAND = 128
TILE = 256


def shape(dims, kind):
    return jax.ShapeDtypeStruct(dims, kind)


def padded(columns):
    return -(-columns // TILE) * TILE


def bands(count, act, size=BAND):
    def step(index, carry):
        act(pl.ds(pl.multiple_of(index * size, size), size))
        return carry

    lax.fori_loop(0, count // size, step, 0)


def rms_back(value, gain, grad):
    scale = lax.rsqrt(jnp.mean(value * value, axis=-1, keepdims=True) + EPS)
    unit = value * scale
    inner = grad * gain
    back = scale * (inner - unit * jnp.mean(inner * unit, axis=-1, keepdims=True))
    return back, jnp.sum(grad * unit, axis=0, keepdims=True)


def front_phase(work, r):
    r.ready("tok")

    def norm(band):
        r.normed[band, :] = normalize(r.tok[band, :].astype(F32), r.gain_row[...]).astype(BF16)

    bands(r.count, norm)
    r.ready("wq", "wk", "wv")
    r.query[...] = dot(r.normed[...], r.wq[...]).astype(BF16)
    r.keys[...] = dot(r.normed[...], r.wk[...]).astype(BF16)
    work.pause("qk")

    def project(band):
        r.values[:, band] = dot(r.normed[...], r.wv[:, band]).astype(BF16)

    bands(r.heads * VD, project, TILE)
    work.pause("v")
    pairs = r.heads // 2
    tables = r.pick_a, r.pick_b, r.table
    state_body(r.keys, r.values, *tables, r.state, r.total, work.between("st", pairs))
    work.pause("e0")
    attend_inside(r.query, r.keys, r.values, r.middle, r.inverse, work.between("a", pairs))
    work.pause("e0w")
    attend_before(
        r.query, *tables, r.state, r.total, r.middle, r.inverse, r.mixed, work.between("b", pairs)
    )

    r.ready("wo")

    def project_out(band):
        r.middle[:, band] = r.tok[:, band].astype(F32) + dot(r.mixed[...], r.wo[:, band])

    bands(r.width, project_out, TILE)
    work.pause("po")

    def norm_again(band):
        r.low[band, :] = normalize(r.middle[band, :], r.gain2_row[...]).astype(BF16)

    bands(r.count, norm_again)
    work.pause("nm")


def feed_phase(work, r, tiles, made, low_t, og_t, acc_out, acc_back, in_sem, out_sem):
    steps = PARTS[-1]

    def columns(step):
        return pl.ds(pl.multiple_of(step * TILE, TILE), TILE)

    def load(step, slot):
        return [
            pltpu.make_async_copy(ref.at[:, columns(step)], tiles.at[slot, i], in_sem.at[slot, i])
            for i, ref in enumerate(r.wholes_flat)
        ]

    def save(step, slot):
        return [
            pltpu.make_async_copy(made.at[slot, i], ref.at[:, columns(step)], out_sem.at[slot, i])
            for i, ref in enumerate(r.grads_flat)
        ]

    r.ready("og")
    low_t[...] = r.low[...].T
    og_t[...] = r.og[...].T
    acc_out[...] = r.middle[...]
    acc_back[...] = jnp.zeros_like(acc_back)
    work.pause("p0")
    for copy in load(0, 0):
        copy.start()
    in_tile, after_tile = work.between("m", steps), work.between("t", steps)

    def step(index, carry):
        slot = index % 2
        for copy in load(index, slot):
            copy.wait()

        crossing = functools.reduce(jnp.logical_or, [index + 1 == edge for edge in GATHER_PARTS])

        @pl.when(jnp.logical_not(crossing))
        def _():
            for copy in load(index + 1, 1 - slot):
                copy.start()

        gate_w, up_w, down_w = (tiles.at[slot, i] for i in range(3))
        gate = dot(r.low[...], gate_w[...])
        upward = dot(r.low[...], up_w[...])
        d_hidden = dot(r.og[...], down_w[...])
        sig = 1.0 / (1.0 + jnp.exp(-gate))
        silu = gate * sig
        hidden = (silu * upward).astype(BF16)
        d_gate = (d_hidden * upward * (sig * (1.0 + gate * (1.0 - sig)))).astype(BF16)
        d_up = (d_hidden * silu).astype(BF16)
        acc_out[...] += dot_nt(hidden, down_w[...])

        @pl.when(index >= 1)
        def _():
            for copy in save(index - 1, 1 - slot):
                copy.wait()

        in_tile(index)

        @pl.when(jnp.logical_and(crossing, index + 1 < steps))
        def _():
            for copy in load(index + 1, 1 - slot):
                copy.start()

        acc_back[...] += dot_nt(d_gate, gate_w[...]) + dot_nt(d_up, up_w[...])
        made[slot, 0] = dot(low_t[...], d_gate).astype(BF16)
        made[slot, 1] = dot(low_t[...], d_up).astype(BF16)
        made[slot, 2] = dot(og_t[...], hidden).astype(BF16)
        for copy in save(index, slot):
            copy.start()
        after_tile(index)
        return carry

    lax.fori_loop(0, steps, step, 0)

    def store_out(band):
        r.out[band, :] = acc_out[band, :].astype(BF16)

    bands(r.count, store_out)
    r.ends[0]().start()
    r.gain_sum[...] = jnp.zeros(r.gain_sum.shape, F32)

    def middle_back(band):
        value, part = rms_back(r.middle[band, :], r.gain2_row[...], acc_back[band, :])
        r.gain_sum[1:2, :] += part
        value = r.og[band, :].astype(F32) + value
        r.middle[band, :] = value
        r.low[band, :] = value.astype(BF16)

    bands(r.count, middle_back)
    for copy in save(steps - 1, (steps - 1) % 2):
        copy.wait()
    work.pause("ft")

    def mixed_back(band):
        r.d_mixed[:, band] = dot_nt(r.low[...], r.wo[band, :]).astype(BF16)

    bands(r.heads * VD, mixed_back, TILE)
    work.pause("dm")


def back_phase(work, r, d_query, d_keys, d_values, q_sum, k_sum, turned, v_part):
    heads_wide, narrow = r.heads * VD, r.heads * KD
    pairs = r.heads // 2
    tables = r.pick_a, r.pick_b, r.table
    back_state_body(
        r.query, r.mixed, r.inverse, r.d_mixed, *tables, r.d_state, r.d_total,
        work.between("c", pairs),
    )
    work.pause("e1")
    turned[...] = r.mixed[...].T

    def out_grads(band):
        r.out_g[:, band] = dot(turned[...], r.low[:, band]).astype(BF16)

    bands(r.width, out_grads, TILE)
    work.pause("og")
    turned[...] = r.normed[...].T
    attend_back_inside(
        r.query, r.keys, r.values, r.mixed, r.inverse, r.d_mixed, *tables, r.state, r.total,
        q_sum, k_sum, v_part, work.between("d", pairs),
    )
    work.pause("e1w")
    grid = GRID + (r.rows,)
    late_refs = dict(q=(d_query, q_sum), k=(d_keys, k_sum), v=(d_values, None))

    def late(index):
        spot = sum(high - low for group in r.late_groups[:index] for _, low, high in group)
        for name, low, high in r.late_groups[index]:
            ref, wide = late_refs[name]
            if wide is not None:
                ref[:, low:high] = wide[:, low:high].astype(BF16)
            for start in range(low, high, TILE):
                stop = min(start + TILE, high)
                value = dot(turned[...], ref[:, start:stop]).astype(BF16)
                size = stop - start
                r.late_g[:, :, :, :, :, :, spot : spot + size] = value.reshape(grid + (size,))
                spot += size

    late(0)
    work.pause("lq")

    def ended(pair):
        for spot, index in ((pairs // 2 - 1, 1), (pairs - 2, 2)):

            @pl.when(pair == spot)
            def _(index=index):
                late(index)
                work.pause(f"l{index}")

    attend_back_after(
        r.keys, r.values, *tables, r.d_state, r.d_total, k_sum, v_part, d_values,
        work.between("f", pairs), ended,
    )
    late(3)
    work.pause("l3")

    def back_norm(band):
        v_part[:, band] = (
            dot_nt(d_query[...], r.wq[band, :])
            + dot_nt(d_keys[...], r.wk[band, :])
            + dot_nt(d_values[...], r.wv[band, :])
        )

    bands(r.width, back_norm, TILE)
    work.pause("dn")

    def tokens_back(band):
        value, part = rms_back(r.tok[band, :].astype(F32), r.gain_row[...], v_part[band, :])
        r.gain_sum[0:1, :] += part
        r.middle[band, :] = r.middle[band, :] + value

    bands(r.count, tokens_back)
    quarter = r.width // 4
    for which in range(2):
        for part in range(4):
            spot = 4 * which + part
            r.gain_mine[0, spot : spot + 1, :] = r.gain_sum[
                which : which + 1, part * quarter : (part + 1) * quarter
            ]


class Refs:
    pass


def layer(tokens, gain, wq, wk, wv, wo, gain2, tables, shards3, out_grad):
    count, width = tokens.shape
    heads = wq.shape[1] // KD
    rows, columns = shards3[0].shape
    full = padded(columns)
    tall = rows // 2
    heads_wide, narrow = heads * VD, heads * KD
    last = heads_wide - 2 * VD
    late_groups = (
        (("q", 0, narrow),),
        (("v", 0, heads_wide // 2), ("k", 0, narrow // 2)),
        (("v", heads_wide // 2, last),),
        (("v", last, heads_wide), ("k", narrow // 2, narrow)),
    )
    late_sizes = [sum(high - low for _, low, high in group) for group in late_groups]
    edges = [0] + [part * TILE for part in PARTS]
    widest = max(*late_sizes, width // 2, *[high - low for low, high in zip(edges, edges[1:])])
    chunks = 6 * len(PARTS) + 4 + 2 * len(late_groups)
    gather_edges = [0] + [part * TILE for part in GATHER_PARTS]
    gathers = 6 * len(GATHER_PARTS)
    states = ((heads, VD, FEATS), BF16), ((heads, 1, FEATS), F32)
    sem = pltpu.SemaphoreType.DMA

    loads = dict(
        shard0=shards3[0], shard1=shards3[1], shard2=shards3[2], tok=tokens, wq=wq, wk=wk, wv=wv,
        og=out_grad, wo=wo,
    )
    inputs = {name + "_in": value for name, value in loads.items()}
    inputs |= dict(
        gain=gain, gain2=gain2, pick_a=tables[0], pick_b=tables[1], table=tables[2]
    )
    free_outs = dict(
        whole0=shape((width, full), BF16), whole1=shape((width, full), BF16),
        whole2=shape((width, full), BF16), grad0=shape((width, full), BF16),
        grad1=shape((width, full), BF16), grad2=shape((width, full), BF16),
        out_end=shape((count, width), BF16), tok_end=shape((count, width), F32),
    )
    outs = dict(
        g0=shape((rows, columns), F32), g1=shape((rows, columns), F32),
        g2=shape((rows, columns), F32), g_out=shape((rows, width), F32),
        g_value=shape((rows, heads_wide), F32), g_query=shape((rows, narrow), F32),
        g_keys=shape((rows, narrow), F32), g_gain=shape((8, width // 4), F32),
    )
    scratch = {name: pltpu.VMEM(value.shape, value.dtype) for name, value in loads.items()}
    scratch |= dict(
        out=pltpu.VMEM((count, width), BF16),
        middle=pltpu.VMEM((count, width), F32),
        load_sem=sem((len(loads),)), end_sem=sem((2,)),
        gain_row=pltpu.VMEM((1, width), F32), gain2_row=pltpu.VMEM((1, width), F32),
        normed=pltpu.VMEM((count, width), BF16),
        query=pltpu.VMEM((count, narrow), BF16),
        keys=pltpu.VMEM((count, narrow), BF16),
        values=pltpu.VMEM((count, heads_wide), BF16),
        mixed=pltpu.VMEM((count, heads_wide), BF16),
        inverse=pltpu.VMEM((count, heads_wide), F32),
        state=pltpu.VMEM(*states[0]), total=pltpu.VMEM(*states[1]),
        d_state=pltpu.VMEM(*states[0]), d_total=pltpu.VMEM(*states[1]),
        near_state=pltpu.VMEM(*states[0]), near_total=pltpu.VMEM(*states[1]),
        far_state=pltpu.VMEM(*states[0]), far_total=pltpu.VMEM(*states[1]),
        ex_sent=sem((6,)), ex_landed=sem((6,)),
        low=pltpu.VMEM((count, width), BF16),
        d_mixed=pltpu.VMEM((count, heads_wide), BF16),
        out_g=pltpu.VMEM((width, width), BF16),
        late_g=pltpu.VMEM(GRID + (rows, sum(late_sizes)), BF16),
        wide=pltpu.VMEM((3, rows, full), BF16),
        ag_sent=sem((gathers, 5)), ag_landed=sem((gathers, 5)), ag_local=sem((gathers,)),
        gain_sum=pltpu.VMEM((8, width), F32),
        gain_mine=pltpu.VMEM((3, 8, width // 4), F32),
        gain_slots=pltpu.VMEM((10, 8, width // 4), F32),
        gain_sent=sem((10,)), gain_landed=sem((10,)),
        p0=pltpu.VMEM((5, 2, 2, 2, 2, tall, widest), BF16),
        p1=pltpu.VMEM((4, 2, 2, 2, 2, tall, widest), BF16),
        p2=pltpu.VMEM((chunks, 2, 2, 2, tall, widest), BF16),
        p3=pltpu.VMEM((chunks, 2, 2, tall, widest), BF16),
        p4=pltpu.VMEM((chunks, 2, tall, widest), BF16),
        p5=pltpu.VMEM((chunks, tall, widest), BF16),
        rs_sent=sem((chunks, 5)), rs_landed=sem((chunks, 5)), rs_local=sem((chunks,)),
        credit=pltpu.SemaphoreType.REGULAR,
    )
    names = list(inputs) + list(free_outs) + list(outs) + list(scratch)

    def body(*refs):
        r = Refs()
        for name, ref in zip(names, refs):
            setattr(r, name, ref)
        r.count, r.width, r.heads, r.rows = count, width, heads, rows
        r.late_groups = late_groups
        r.place = place = Place()
        r.wholes_flat = [r.whole0, r.whole1, r.whole2]
        r.grads_flat = [r.grad0, r.grad1, r.grad2]
        grid = GRID + (rows,)
        wholes = [ref.reshape(grid + (full,)) for ref in r.wholes_flat]
        grads = [ref.reshape(grid + (full,)) for ref in r.grads_flat]
        def load(name):
            spot = list(loads).index(name)
            source = getattr(r, name + "_in")
            return pltpu.make_async_copy(source, getattr(r, name), r.load_sem.at[spot])

        r.ready = lambda *wanted: [load(name).wait() for name in wanted]
        r.ends = [
            lambda: pltpu.make_async_copy(r.out, r.out_end, r.end_sem.at[0]),
            lambda: pltpu.make_async_copy(r.middle, r.tok_end, r.end_sem.at[1]),
        ]
        for name in loads:
            load(name).start()
        enter(place)
        work = Work()
        r.gain_row[...] = r.gain[...].astype(F32).reshape(1, width)
        r.gain2_row[...] = r.gain2[...].astype(F32).reshape(1, width)
        r.ready("shard0", "shard1", "shard2")
        gather_list, sum_list, exchange_list, gain_list = work.kinds
        for spot, shard in enumerate((r.shard0, r.shard1, r.shard2)):
            r.wide[spot, :, columns:full] = jnp.zeros((rows, full - columns), BF16)
            r.wide[spot, :, 0:columns] = shard[...]
        for part, (low, high) in enumerate(zip(gather_edges, gather_edges[1:])):
            for weight in range(3):
                for kind, first in enumerate("yy" if (part, weight) in TURNED else "xy"):
                    order = len(gather_list)
                    gather_list.append(
                        Gather(
                            r.wide.at[weight], wholes[weight], pl.ds(kind * tall, tall),
                            pl.ds(low, high - low), first,
                            (r.ag_sent.at[order], r.ag_landed.at[order], r.ag_local.at[order]), place,
                        )
                    )
        pool = Pool(
            [r.p0, r.p1, r.p2, r.p3, r.p4, r.p5], (r.rs_sent, r.rs_landed, r.rs_local), r.credit,
            place, chunks,
        )

        def sums(source, low, high, target, firsts="xy"):
            for kind, first in enumerate(firsts):

                def put(value, kind=kind):
                    target(slice(kind * tall, (kind + 1) * tall), value)

                chunk_rows, chunk_columns = pl.ds(kind * tall, tall), pl.ds(low, high - low)
                sum_list.append(
                    Chunk(pool, len(sum_list), source, chunk_rows, chunk_columns, first, put)
                )

        def into(ref, low, high):
            def put(where, value):
                ref[where, low:high] = value[:, 0 : high - low]

            return put

        for low, high in zip(edges, edges[1:]):
            for source, target in zip(grads, (r.g0, r.g1, r.g2)):
                sums(source, low, high, into(target, low, min(high, columns)))
        half = width // 2
        for low in (0, half):
            target = into(r.g_out, low, low + half)
            sums(r.out_g.reshape(grid + (width,)), low, low + half, target, "yy")
        late_ends = dict(q=r.g_query, k=r.g_keys, v=r.g_value)
        spot = 0
        for group, size in zip(late_groups, late_sizes):

            def put_late(where, value, group=group):
                at = 0
                for name, low, high in group:
                    late_ends[name][where, low:high] = value[:, at : at + high - low]
                    at += high - low

            sums(r.late_g, spot, spot + size, put_late)
            spot += size
        for state, total, reverse in ((r.state, r.total, False), (r.d_state, r.d_total, True)):
            exchange_list.append(
                Exchange(
                    state, total, (r.near_state, r.near_total), (r.far_state, r.far_total),
                    r.ex_sent, r.ex_landed, place, reverse,
                )
            )
        gain_list.append(Gains(r.gain_mine, r.gain_slots, r.gain_sent, r.gain_landed, place))
        work.pause("s")
        front_phase(work, r)
        pl.run_scoped(
            lambda *buffers: feed_phase(work, r, *buffers),
            pltpu.VMEM((2, 3, width, TILE), BF16),
            pltpu.VMEM((2, 3, width, TILE), BF16),
            pltpu.VMEM((width, count), BF16),
            pltpu.VMEM((width, count), BF16),
            pltpu.VMEM((count, width), F32),
            pltpu.VMEM((count, width), F32),
            sem((2, 3)),
            sem((2, 3)),
        )
        pl.run_scoped(
            lambda *buffers: back_phase(work, r, *buffers),
            pltpu.VMEM((count, narrow), BF16),
            pltpu.VMEM((count, narrow), BF16),
            pltpu.VMEM((count, heads_wide), BF16),
            pltpu.VMEM((count, narrow), F32),
            pltpu.VMEM((count, narrow), F32),
            pltpu.VMEM((width, count), BF16),
            pltpu.VMEM((count, width), F32),
        )
        r.ends[1]().start()
        work.pause("z")
        r.ends[0]().wait()
        r.ends[1]().wait()
        r.g_gain[...] = r.gain_mine[2]

    vmem = pl.BlockSpec(memory_space=pltpu.VMEM)
    free = pl.BlockSpec(memory_space=pl.ANY)
    results = pl.pallas_call(
        body,
        out_shape=list(free_outs.values()) + list(outs.values()),
        in_specs=[free] * len(loads) + [vmem] * 5,
        out_specs=[free] * len(free_outs) + [vmem] * len(outs),
        scratch_shapes=list(scratch.values()),
        compiler_params=pltpu.CompilerParams(
            collective_id=0, has_side_effects=True, vmem_limit_bytes=VMEM_LIMIT
        ),
    )(*inputs.values())
    return results[6:]


def hand_over(results, gains):
    quarter = gains.shape[1]
    share = quarter // 8
    count = len(results)

    def body(*refs):
        sources, gain, targets = refs[:count], refs[count], refs[count + 1 : 2 * count + 1]
        first, second, sems = refs[2 * count + 1 :]
        copies = [
            pltpu.make_async_copy(a, b, sems.at[i]) for i, (a, b) in enumerate(zip(sources, targets))
        ]
        for copy in copies:
            copy.start()
        own = lax.axis_index("dp") * 4 + lax.axis_index("seq")
        turned = pltpu.roll(gain[...], lax.rem(quarter - own % 8 * share, quarter), 1)[:, 0:share]
        row = lax.broadcasted_iota(jnp.int32, turned.shape, 0)
        for ref, start in ((first, 0), (second, 4)):
            ref[...] = jnp.sum(only(row == start + own // 8, turned), axis=0, keepdims=True)
        for copy in copies:
            copy.wait()

    vmem = pl.BlockSpec(memory_space=pltpu.VMEM)
    free = pl.BlockSpec(memory_space=pl.ANY)
    return pl.pallas_call(
        body,
        out_shape=[shape(value.shape, value.dtype) for value in results] + [shape((1, share), F32)] * 2,
        in_specs=[vmem] * (count + 1),
        out_specs=[free] * count + [vmem] * 2,
        scratch_shapes=[pltpu.SemaphoreType.DMA((count,))],
    )(*results, gains)


def general(
    tokens, attn_gain, w_query, w_key, w_value, w_output, mlp_gain, w_gate, w_up, w_down, out_grad
):
    count, width = tokens.shape
    heads = w_query.shape[1] // KD
    all_values = heads * VD
    tables = feature_tables()
    inputs = tokens.astype(F32)
    gain = attn_gain.astype(F32).reshape(1, width)
    gate_full, up_full, down_full = (
        lax.all_gather(w, ("dp", "seq"), axis=0, tiled=True) for w in (w_gate, w_up, w_down)
    )
    normed, query, keys, values = call(
        project_body,
        [
            ((count, width), BF16),
            ((count, heads * KD), BF16),
            ((count, heads * KD), BF16),
            ((count, all_values), BF16),
        ],
        tokens,
        gain,
        w_query,
        w_key,
        w_value,
    )
    state_shapes = [((heads, VD, FEATS), BF16), ((heads, 1, FEATS), F32)]
    state, total = call(state_body, state_shapes, keys, values, *tables)
    state = before(lax.all_gather(state, "seq"), "seq").astype(BF16)
    total = before(lax.all_gather(total, "seq"), "seq")
    mixed, inverse = call(
        attend_body,
        [((count, all_values), BF16), ((count, all_values), F32)],
        query,
        keys,
        values,
        *tables,
        state,
        total,
    )
    middle = inputs + dot(mixed, w_output)
    normed_mlp, second_back = jax.vjp(rms_norm, middle, mlp_gain.astype(F32))
    mlp_low = normed_mlp.astype(BF16)
    gate = dot(mlp_low, gate_full)
    upward = dot(mlp_low, up_full)
    hidden_val, gated_back = jax.vjp(gated, gate, upward)
    hidden = hidden_val.astype(BF16)
    layer_out = (middle + dot_nt(hidden, down_full)).astype(BF16)
    d_hidden = dot(out_grad, down_full)
    down_grad = dot_tn(out_grad, hidden).astype(BF16)
    d_gate_f, d_up_f = gated_back(d_hidden)
    d_gate = d_gate_f.astype(BF16)
    d_up = d_up_f.astype(BF16)
    gate_grad = dot_tn(mlp_low, d_gate).astype(BF16)
    up_grad = dot_tn(mlp_low, d_up).astype(BF16)
    d_normed_mlp = dot_nt(d_gate, gate_full) + dot_nt(d_up, up_full)
    d_middle_norm, mlp_gain_part = second_back(d_normed_mlp)
    d_middle = out_grad.astype(F32) + d_middle_norm
    d_branch = d_middle.astype(BF16)
    output_grad = dot_tn(mixed, d_branch).astype(BF16)
    d_mixed = dot_nt(d_branch, w_output).astype(BF16)
    d_state, d_total = call(
        back_state_body, state_shapes, query, mixed, inverse, d_mixed, *tables
    )
    d_state = before(lax.all_gather(d_state, "seq"), "seq", True).astype(BF16)
    d_total = before(lax.all_gather(d_total, "seq"), "seq", True)
    d_query, d_keys, d_values = call(
        attend_back_body,
        [
            ((count, heads * KD), BF16),
            ((count, heads * KD), BF16),
            ((count, all_values), BF16),
        ],
        query,
        keys,
        values,
        mixed,
        inverse,
        d_mixed,
        *tables,
        state,
        total,
        d_state,
        d_total,
        scratch=[
            pltpu.VMEM((count, heads * KD), F32),
            pltpu.VMEM((count, heads * KD), F32),
            pltpu.VMEM((count, LANES), F32),
        ],
    )
    d_normed = dot_nt(d_query, w_query) + dot_nt(d_keys, w_key) + dot_nt(d_values, w_value)
    query_grad = dot_tn(normed, d_query).astype(BF16)
    key_grad = dot_tn(normed, d_keys).astype(BF16)
    value_grad = dot_tn(normed, d_values).astype(BF16)
    _, first_back = jax.vjp(rms_norm, inputs, attn_gain.astype(F32))
    d_inputs_norm, attn_gain_part = first_back(d_normed)
    tokens_grad = d_middle + d_inputs_norm
    parts = [query_grad, key_grad, value_grad, output_grad, gate_grad, up_grad, down_grad]
    joined = lax.psum_scatter(
        jnp.concatenate(parts, axis=1), ("dp", "seq"), scatter_dimension=0, tiled=True
    ).astype(F32)
    edges = np.cumsum([part.shape[1] for part in parts])[:-1]
    query_grad, key_grad, value_grad, output_grad, gate_grad, up_grad, down_grad = jnp.split(
        joined, edges, axis=1
    )
    gains = lax.psum_scatter(
        jnp.stack([attn_gain_part, mlp_gain_part], axis=1),
        ("dp", "seq"),
        scatter_dimension=0,
        tiled=True,
    )
    return (
        layer_out,
        tokens_grad,
        gains[:, 0],
        query_grad,
        key_grad,
        value_grad,
        output_grad,
        gains[:, 1],
        gate_grad,
        up_grad,
        down_grad,
    )


def shards(
    tokens, attn_gain, w_query, w_key, w_value, w_output, mlp_gain, w_gate, w_up, w_down, out_grad
):
    args = (
        tokens, attn_gain, w_query, w_key, w_value, w_output, mlp_gain, w_gate, w_up, w_down, out_grad
    )
    if (lax.axis_size("dp"), lax.axis_size("seq")) != (8, 4):
        return general(*args)
    *results, gains = layer(
        tokens, attn_gain, w_query, w_key, w_value, w_output, mlp_gain, feature_tables(),
        (w_gate, w_up, w_down), out_grad,
    )
    *results, gain_grad, gain2_grad = hand_over(results, gains)
    layer_out, tok_grad, gate_grad, up_grad, down_grad, output_grad, value_grad, query_grad, key_grad = results
    return (
        layer_out,
        tok_grad,
        gain_grad.reshape(-1),
        query_grad,
        key_grad,
        value_grad,
        output_grad,
        gain2_grad.reshape(-1),
        gate_grad,
        up_grad,
        down_grad,
    )


def solution(mesh):
    rows = P(("dp", "seq"), None)
    in_specs = (rows, P(), P(), P(), P(), P(), P(), rows, rows, rows, rows)
    out_specs = (
        rows,
        rows,
        P(("dp", "seq")),
        rows,
        rows,
        rows,
        rows,
        P(("dp", "seq")),
        rows,
        rows,
        rows,
    )
    return jax.shard_map(
        shards, mesh=mesh, in_specs=in_specs, out_specs=out_specs, check_vma=False
    )
```

```python
import functools
import math

import jax
import jax.numpy as jnp
import numpy as np
from jax import lax
from jax.experimental import pallas as pl
from jax.experimental.pallas import tpu as pltpu
from jax.sharding import PartitionSpec as P

KD = 16
VD = 64
LANES = 128
FEATS = 256
EPS = 1e-05
QUAD = 1.0 / (4.0 * math.sqrt(2.0))
F32 = jnp.float32
BF16 = jnp.bfloat16
VMEM_LIMIT = 62 << 20


def feature_tables():
    pick_a = np.zeros((LANES, FEATS), np.float32)
    pick_b = np.zeros((LANES, FEATS), np.float32)
    rows = np.zeros((8, FEATS), np.float32)
    spot = 0
    for a in range(KD):
        for b in range(a, KD):
            pick_a[a::KD, spot] = 1.0
            pick_b[b::KD, spot] = 1.0
            rows[2, spot] = QUAD
            rows[3, spot] = 1.0 if a == b else 2.0
            spot += 1
    for a in range(KD):
        pick_a[a::KD, spot] = 1.0
        rows[1, spot] = 1.0
        rows[2, spot] = 0.5
        rows[3, spot] = 1.0
        spot += 1
    rows[0:4, spot] = 1.0
    return jnp.asarray(pick_a, BF16), jnp.asarray(pick_b, BF16), jnp.asarray(rows)


def dot(left, right):
    return jnp.dot(left, right, preferred_element_type=F32)


def dot_nt(left, right):
    return lax.dot_general(left, right, (((1,), (1,)), ((), ())), preferred_element_type=F32)


def dot_tn(left, right):
    return lax.dot_general(left, right, (((0,), (0,)), ((), ())), preferred_element_type=F32)


def tile_at(index):
    return pl.ds(pl.multiple_of(index * LANES, LANES), LANES)


def head_lanes(rows, spot):
    return lax.broadcasted_iota(jnp.int32, (rows, LANES), 1) // KD == spot


def half_lanes(rows, half):
    return lax.broadcasted_iota(jnp.int32, (rows, LANES), 1) // VD == half


def halves_of(masked, pick_a, pick_b, rows):
    first = dot(masked, pick_a) + rows[0:1, :]
    second = dot(masked, pick_b) + rows[1:2, :]
    return first, second


def features_of(masked, pick_a, pick_b, rows):
    first, second = halves_of(masked, pick_a, pick_b, rows)
    return (first * second * rows[2:3, :]).astype(BF16)


def only(mask, value):
    return jnp.where(mask, value, jnp.zeros_like(value))


def project_body(tok, gain, wq, wk, wv, normed, query, keys, values):
    x = tok[...].astype(F32)
    scale = lax.rsqrt(jnp.mean(x * x, axis=-1, keepdims=True) + EPS)
    normed[...] = (x * scale * gain[...]).astype(BF16)
    query[...] = dot(normed[...], wq[...]).astype(BF16)
    keys[...] = dot(normed[...], wk[...]).astype(BF16)
    values[...] = dot(normed[...], wv[...]).astype(BF16)


def state_body(keys, values, pick_a, pick_b, rows, state, total, between=None):
    pairs = values.shape[1] // LANES
    count = keys.shape[0]

    def step(pair, carry):
        turned = values[:, tile_at(pair)].T
        for half in range(2):
            head = pair * 2 + half
            masked = only(head_lanes(count, head % 8), keys[:, tile_at(head // 8)])
            feat = features_of(masked, pick_a[...], pick_b[...], rows[...])
            sums = dot(turned[half * VD : (half + 1) * VD, :], feat)
            state[head] = (sums * rows[3:4, :]).astype(BF16)
            total[head] = jnp.sum(feat.astype(F32), axis=0, keepdims=True) * rows[3:4, :]
        if between is not None:
            between(pair)
        return carry

    lax.fori_loop(0, pairs, step, 0)


def causal(rows, columns, row_start, column_start):
    row = lax.broadcasted_iota(jnp.int32, (rows, columns), 0) + row_start
    column = lax.broadcasted_iota(jnp.int32, (rows, columns), 1) + column_start
    return row >= column


def attend_body(query, keys, values, pick_a, pick_b, rows, state, total, mixed, inverse, between=None, block=256):
    pairs = values.shape[1] // LANES
    count = keys.shape[0]

    def step(pair, carry):
        vals = values[:, tile_at(pair)]
        for start in range(0, count, block):
            stop = start + block
            numer = None
            for half in range(2):
                head = pair * 2 + half
                masked = only(head_lanes(block, head % 8), query[start:stop, tile_at(head // 8)])
                score = dot_nt(masked, keys[0:stop, tile_at(head // 8)]) * 0.25
                weight = 1.0 + score + 0.5 * score * score
                weight = jnp.where(causal(block, stop, start, 0), weight, 0.0)
                feat = features_of(masked, pick_a[...], pick_b[...], rows[...])
                inter = feat.astype(F32) * total[head]
                denom = jnp.sum(weight, axis=1, keepdims=True) + jnp.sum(
                    inter, axis=1, keepdims=True
                )
                across = dot_nt(feat, state[head])
                both = dot(weight.astype(BF16), vals[0:stop, :])
                across = jnp.concatenate([across, across], axis=1)
                whole = (both + across) / denom
                flip = jnp.broadcast_to(1.0 / denom, (block, LANES))
                if half == 0:
                    numer, invs = whole, flip
                else:
                    mask = half_lanes(block, 0)
                    numer = jnp.where(mask, numer, whole)
                    invs = jnp.where(mask, invs, flip)
            mixed[start:stop, tile_at(pair)] = numer.astype(BF16)
            inverse[start:stop, tile_at(pair)] = invs
        if between is not None:
            between(pair)
        return carry

    lax.fori_loop(0, pairs, step, 0)


def spare_lane(rows, spot):
    lane = lax.broadcasted_iota(jnp.int32, (rows, LANES), 1)
    return lane == lax.rem(spot * KD + KD, LANES)


def query_side(value, spot):
    rows = value.shape[0]
    quarter = only(head_lanes(rows, spot), value * 0.25)
    return jnp.where(spare_lane(rows, spot), jnp.ones_like(value), quarter)


def key_side(value, spot):
    return jnp.where(spare_lane(value.shape[0], spot), jnp.ones_like(value), value)


def triangle(value, start, block, upper=False):
    row = lax.broadcasted_iota(jnp.int32, (block, block), 0)
    column = lax.broadcasted_iota(jnp.int32, (block, block), 1)
    keep = row <= column if upper else row >= column
    pieces = [value[:, 0:start]] if start > 0 else []
    pieces.append(only(keep, value[:, start : start + block]))
    if start + block < value.shape[1]:
        pieces.append(value[:, start + block :])
    return jnp.concatenate(pieces, axis=1) if len(pieces) > 1 else pieces[0]


def attend_inside(query, keys, values, numer, denoms, between, block=512):
    pairs = values.shape[1] // LANES
    count = keys.shape[0]

    def step(pair, carry):
        vals = values[:, tile_at(pair)]
        for start in range(0, count, block):
            stop = start + block
            for half in range(2):
                head = pair * 2 + half
                place = tile_at(head // 8)
                plus = dot_nt(
                    query_side(query[start:stop, place], head % 8), key_side(keys[0:stop, place], head % 8)
                )
                weight = triangle(0.5 * plus * plus + 0.5, start, block)
                flip = jnp.broadcast_to(jnp.sum(weight, axis=1, keepdims=True), (block, LANES))
                both = dot(weight.astype(BF16), vals[0:stop, :])
                if half == 0:
                    whole, wides = both, flip
                else:
                    mask = half_lanes(block, 0)
                    numer[start:stop, tile_at(pair)] = jnp.where(mask, whole, both)
                    denoms[start:stop, tile_at(pair)] = jnp.where(mask, wides, flip)
        between(pair)
        return carry

    lax.fori_loop(0, pairs, step, 0)


def attend_before(query, pick_a, pick_b, rows, state, total, numer, inverse, mixed, between):
    count = query.shape[0]
    pairs = mixed.shape[1] // LANES

    def step(pair, carry):
        spot = tile_at(pair)
        for half in range(2):
            head = pair * 2 + half
            masked = only(head_lanes(count, head % 8), query[:, tile_at(head // 8)])
            feat = features_of(masked, pick_a[...], pick_b[...], rows[...])
            inter = jnp.sum(feat.astype(F32) * total[head], axis=1, keepdims=True)
            inter = jnp.broadcast_to(inter, (count, LANES))
            across = dot_nt(feat, state[head])
            across = jnp.concatenate([across, across], axis=1)
            if half == 0:
                whole, wides = across, inter
            else:
                mask = half_lanes(count, 0)
                whole = jnp.where(mask, whole, across)
                wides = jnp.where(mask, wides, inter)
        flipped = 1.0 / (inverse[:, spot] + wides)
        inverse[:, spot] = flipped
        mixed[:, spot] = ((numer[:, spot] + whole) * flipped).astype(BF16)
        between(pair)
        return carry

    lax.fori_loop(0, pairs, step, 0)


def back_state_body(query, mixed, inverse, d_mixed, pick_a, pick_b, rows, d_state, d_total, between=None):
    pairs = mixed.shape[1] // LANES
    count = query.shape[0]

    def step(pair, carry):
        spot = tile_at(pair)
        d_numer = d_mixed[:, spot].astype(F32) * inverse[:, spot]
        lost = d_numer * mixed[:, spot].astype(F32)
        turned = d_numer.astype(BF16).T
        for half in range(2):
            head = pair * 2 + half
            masked = only(head_lanes(count, head % 8), query[:, tile_at(head // 8)])
            feat = features_of(masked, pick_a[...], pick_b[...], rows[...])
            d_denom = -jnp.sum(only(half_lanes(count, half), lost), axis=1, keepdims=True)
            sums = dot(turned[half * VD : (half + 1) * VD, :], feat)
            d_state[head] = (sums * rows[3:4, :]).astype(BF16)
            d_total[head] = (
                jnp.sum(feat.astype(F32) * d_denom, axis=0, keepdims=True) * rows[3:4, :]
            )
        if between is not None:
            between(pair)
        return carry

    lax.fori_loop(0, pairs, step, 0)


def feature_back(d_feat, first, second, pick_a, pick_b, rows):
    scaled = d_feat * rows[2:3, :]
    return dot_nt((scaled * second).astype(BF16), pick_a) + dot_nt(
        (scaled * first).astype(BF16), pick_b
    )


def attend_back_body(
    query,
    keys,
    values,
    mixed,
    inverse,
    d_mixed,
    pick_a,
    pick_b,
    rows,
    state,
    total,
    d_state,
    d_total,
    d_query,
    d_keys,
    d_values,
    q_sum,
    k_sum,
    v_sum,
    between=None,
    block=256,
):
    pairs = values.shape[1] // LANES
    count = keys.shape[0]
    q_sum[...] = jnp.zeros_like(q_sum)
    k_sum[...] = jnp.zeros_like(k_sum)

    def step(pair, carry):
        spot = tile_at(pair)
        d_numer = d_mixed[:, spot].astype(F32) * inverse[:, spot]
        lost = d_numer * mixed[:, spot].astype(F32)
        d_low = d_numer.astype(BF16)
        turned = pltpu.roll(lost, VD, 1)
        vals = values[:, spot]
        for half in range(2):
            head = pair * 2 + half
            place = tile_at(head // 8)
            mine = half_lanes(count, half)
            lanes = head_lanes(count, head % 8)
            d_denom = -jnp.sum(only(mine, lost), axis=1, keepdims=True)
            d_wide = jnp.where(mine, d_numer, -turned).astype(BF16)
            v_wide = jnp.where(mine, vals, jnp.ones_like(vals))
            q_mask = only(lanes, query[:, place])
            k_mask = only(lanes, keys[:, place])
            grads_q, grads_k, grads_v = [], [], []
            for start in range(0, count, block):
                stop = start + block
                score = dot_nt(q_mask[start:stop], k_mask[0:stop]) * 0.25
                d_weight = dot_nt(d_wide[start:stop], v_wide[0:stop])
                d_score = only(causal(block, stop, start, 0), d_weight * (1.0 + score))
                grads_q.append(dot(d_score.astype(BF16), k_mask[0:stop]))
                rest = count - start
                score = dot_nt(k_mask[start:stop], q_mask[start:count]) * 0.25
                mask = causal(rest, block, 0, 0)
                mask = (
                    lax.broadcasted_iota(jnp.int32, (block, rest), 0)
                    <= lax.broadcasted_iota(jnp.int32, (block, rest), 1)
                )
                weight = only(mask, 1.0 + score + 0.5 * score * score)
                d_weight = dot_nt(v_wide[start:stop], d_wide[start:count])
                d_score = only(mask, d_weight * (1.0 + score))
                grads_k.append(dot(d_score.astype(BF16), q_mask[start:count]))
                grads_v.append(dot(weight.astype(BF16), d_low[start:count]))
            first, second = halves_of(q_mask, pick_a[...], pick_b[...], rows[...])
            d_feat = dot(d_low[:, half * VD : (half + 1) * VD], state[head]) + d_denom * total[head]
            inter_q = feature_back(d_feat, first, second, pick_a[...], pick_b[...], rows[...])
            first, second = halves_of(k_mask, pick_a[...], pick_b[...], rows[...])
            feat = (first * second * rows[2:3, :]).astype(BF16)
            d_feat = dot(vals[:, half * VD : (half + 1) * VD], d_state[head]) + d_total[head]
            inter_k = feature_back(d_feat, first, second, pick_a[...], pick_b[...], rows[...])
            inter_v = dot_nt(feat, d_state[head])
            inter_v = jnp.concatenate([inter_v, inter_v], axis=1)
            whole_v = jnp.concatenate(grads_v, axis=0) + inter_v
            v_sum[...] = whole_v if half == 0 else jnp.where(mine, whole_v, v_sum[...])
            q_sum[:, place] += jnp.concatenate(grads_q, axis=0) * 0.25 + only(lanes, inter_q)
            k_sum[:, place] += jnp.concatenate(grads_k, axis=0) * 0.25 + only(lanes, inter_k)
        d_values[:, spot] = v_sum[...].astype(BF16)
        if between is not None:
            between(pair)
        return carry

    lax.fori_loop(0, pairs, step, 0)
    d_query[...] = q_sum[...].astype(BF16)
    d_keys[...] = k_sum[...].astype(BF16)


def attend_back_inside(
    query, keys, values, mixed, inverse, d_mixed, pick_a, pick_b, rows, state, total, q_sum, k_sum,
    v_part, between, block=512,
):
    pairs = values.shape[1] // LANES
    count = keys.shape[0]
    q_sum[...] = jnp.zeros_like(q_sum)
    k_sum[...] = jnp.zeros_like(k_sum)

    def step(pair, carry):
        spot = tile_at(pair)
        d_numer = d_mixed[:, spot].astype(F32) * inverse[:, spot]
        lost = d_numer * mixed[:, spot].astype(F32)
        d_low = d_numer.astype(BF16)
        turned = pltpu.roll(lost, VD, 1)
        vals = values[:, spot]
        for half in range(2):
            head = pair * 2 + half
            place = tile_at(head // 8)
            mine = half_lanes(count, half)
            lanes = head_lanes(count, head % 8)
            d_wide = jnp.where(mine, d_numer, -turned).astype(BF16)
            v_wide = jnp.where(mine, vals, jnp.ones_like(vals))
            q_tile, k_tile = query[:, place], keys[:, place]
            q_mask = only(lanes, q_tile)
            q_quarter, k_quarter = q_mask * 0.25, only(lanes, k_tile) * 0.25
            q_plus, k_plus = query_side(q_tile, head % 8), key_side(k_tile, head % 8)
            grads_q, grads_k, grads_v = [], [], []
            for start in range(0, count, block):
                stop = start + block
                plus = dot_nt(q_plus[start:stop], k_plus[0:stop])
                d_weight = dot_nt(d_wide[start:stop], v_wide[0:stop])
                d_score = triangle(d_weight * plus, start, block)
                grads_q.append(dot(d_score.astype(BF16), k_quarter[0:stop]))
                plus = dot_nt(k_plus[start:stop], q_plus[start:count])
                weight = triangle(0.5 * plus * plus + 0.5, 0, block, True)
                d_weight = dot_nt(v_wide[start:stop], d_wide[start:count])
                d_score = triangle(d_weight * plus, 0, block, True)
                grads_k.append(dot(d_score.astype(BF16), q_quarter[start:count]))
                grads_v.append(dot(weight.astype(BF16), d_low[start:count]))
            first, second = halves_of(q_mask, pick_a[...], pick_b[...], rows[...])
            high = total[head].astype(BF16)
            rest = (total[head] - high.astype(F32)).astype(BF16)
            sums = [jnp.broadcast_to(part, (VD, FEATS)) for part in (high, rest)]
            zero = jnp.zeros((VD, FEATS), BF16)
            own = [state[head], sums[0]], [zero, sums[1]]
            order = [part for group in own for part in (group if half == 0 else group[::-1])]
            d_feat = dot(
                jnp.concatenate([d_wide, d_wide], axis=1), jnp.concatenate(order, axis=0)
            )
            inter_q = feature_back(d_feat, first, second, pick_a[...], pick_b[...], rows[...])
            whole_v = jnp.concatenate(grads_v, axis=0)
            v_part[:, spot] = whole_v if half == 0 else jnp.where(mine, whole_v, v_part[:, spot])
            q_sum[:, place] += jnp.concatenate(grads_q, axis=0) + only(lanes, inter_q)
            k_sum[:, place] += jnp.concatenate(grads_k, axis=0)
        between(pair)
        return carry

    lax.fori_loop(0, pairs, step, 0)


def attend_back_after(
    keys, values, pick_a, pick_b, rows, d_state, d_total, k_sum, v_part, d_values, between, ended
):
    pairs = values.shape[1] // LANES
    count = keys.shape[0]

    def step(pair, carry):
        spot = tile_at(pair)
        vals = values[:, spot]
        for half in range(2):
            head = pair * 2 + half
            place = tile_at(head // 8)
            lanes = head_lanes(count, head % 8)
            k_mask = only(lanes, keys[:, place])
            first, second = halves_of(k_mask, pick_a[...], pick_b[...], rows[...])
            feat = (first * second * rows[2:3, :]).astype(BF16)
            d_feat = dot(vals[:, half * VD : (half + 1) * VD], d_state[head]) + d_total[head]
            inter_k = feature_back(d_feat, first, second, pick_a[...], pick_b[...], rows[...])
            inter_v = dot_nt(feat, d_state[head])
            inter_v = jnp.concatenate([inter_v, inter_v], axis=1)
            k_sum[:, place] += only(lanes, inter_k)
            whole_v = v_part[:, spot] + inter_v
            mask = half_lanes(count, half)
            whole_v = whole_v if half == 0 else jnp.where(mask, whole_v, v_part[:, spot])
            if half == 0:
                v_part[:, spot] = jnp.where(mask, whole_v, v_part[:, spot])
            else:
                d_values[:, spot] = whole_v.astype(BF16)
        between(pair)
        ended(pair)
        return carry

    lax.fori_loop(0, pairs, step, 0)


def call(body, shapes, *operands, scratch=()):
    return pl.pallas_call(
        body,
        out_shape=[jax.ShapeDtypeStruct(shape, kind) for shape, kind in shapes],
        scratch_shapes=list(scratch),
        compiler_params=pltpu.CompilerParams(vmem_limit_bytes=VMEM_LIMIT),
    )(*operands)


def rms_norm(inputs, gain):
    return inputs * lax.rsqrt(jnp.mean(inputs * inputs, axis=-1, keepdims=True) + EPS) * gain


def gated(gate_in, up_in):
    return jax.nn.silu(gate_in) * up_in


def before(parts, axis, reverse=False):
    place = lax.axis_index(axis)
    order = jnp.arange(parts.shape[0])
    chosen = order > place if reverse else order < place
    chosen = chosen.reshape((-1,) + (1,) * (parts.ndim - 1))
    return jnp.sum(jnp.where(chosen, parts.astype(F32), 0.0), axis=0)


MESH_ID = pl.DeviceIdType.MESH


class Place:
    def __init__(self):
        self.dp, self.seq = lax.axis_index("dp"), lax.axis_index("seq")
        self.z, self.y = self.dp // 2, self.dp % 2
        self.x, self.core = self.seq // 2, self.seq % 2
        self.zh, self.zl = self.z // 2, self.z % 2

    def at(self, z=None, y=None, x=None, core=None):
        z = self.z if z is None else z
        y = self.y if y is None else y
        x = self.x if x is None else x
        core = self.core if core is None else core
        return (z * 2 + y, x * 2 + core)

    def mate(self):
        return self.at(core=1 - self.core)

    def across(self, axis):
        return self.at(y=1 - self.y) if axis == "y" else self.at(x=1 - self.x)

    def own(self, axis):
        return self.y if axis == "y" else self.x


def remote(source, target, sent, landed, device):
    return pltpu.make_async_remote_copy(
        src_ref=source,
        dst_ref=target,
        send_sem=sent,
        recv_sem=landed,
        device_id=device,
        device_id_type=MESH_ID,
    )


def enter(place):
    barrier = pltpu.get_barrier_semaphore()
    others = [(place.dp, jnp.bitwise_xor(place.seq, other)) for other in range(1, 4)]
    others += [(jnp.bitwise_xor(place.dp, other), place.seq) for other in range(1, 8)]
    for device in others:
        pl.semaphore_signal(barrier, inc=1, device_id=device, device_id_type=MESH_ID)
    pl.semaphore_wait(barrier, len(others))


class Gather:
    def __init__(self, shard, whole, rows, columns, first, sems, place):
        self.shard, self.whole, self.rows, self.columns = shard, whole, rows, columns
        self.first, self.third = first, "x" if first == "y" else "y"
        self.sems, self.place = sems, place

    def block(self, high, low, one, three, core=None):
        core = self.place.core if core is None else core
        grid = (one, three) if self.first == "y" else (three, one)
        return self.whole.at[(high, low) + grid + (core, self.rows, self.columns)]

    def move(self, ref, spot, device, source=None):
        sent, landed, _ = self.sems
        source = ref if source is None else source
        return remote(source, ref, sent.at[spot], landed.at[spot], device)

    def copies(self):
        place, every = self.place, slice(None)
        own1, own3 = place.own(self.first), place.own(self.third)
        mine = self.shard.at[self.rows, self.columns]
        block = self.block
        zh, zl = place.zh, place.zl

        def keep():
            return pltpu.make_async_copy(mine, block(zh, zl, own1, own3), self.sems[2])

        def far(high):
            device = place.at(z=jnp.bitwise_xor(place.z, 2))
            return self.move(block(high, zl, own1, own3), 0, device, mine)

        def cross(three):
            return self.move(block(every, zl, own1, three), 1, place.across(self.third))

        def near(low):
            device = place.at(z=jnp.bitwise_xor(place.z, 1))
            return self.move(block(every, low, own1, every), 2, device)

        def over(one):
            return self.move(block(every, every, one, every), 3, place.across(self.first))

        def mate(core):
            return self.move(block(every, every, every, every, core), 4, place.mate())

        return keep, [
            (far, zh, 1 - zh),
            (cross, own3, 1 - own3),
            (near, zl, 1 - zl),
            (over, own1, 1 - own1),
            (mate, place.core, 1 - place.core),
        ]

    def step(self, index):
        keep, stages = self.copies()
        if index == 0:
            keep().start()
        if index == 1:
            keep().wait()
        if index > 0:
            act, _, theirs = stages[index - 1]
            act(theirs).wait_recv()
        if index < 5:
            act, own, _ = stages[index]
            act(own).start()
        else:
            for act, own, _ in stages:
                act(own).wait_send()


class Pool:
    def __init__(self, refs, sems, free, place, chunks):
        self.refs, self.sems, self.free, self.place, self.chunks = refs, sems, free, place, chunks
        self.kept, self.landing = refs[0].shape[0], refs[1].shape[0]


class Chunk:
    def __init__(self, pool, order, source, rows, columns, first, put):
        self.pool, self.place, self.put = pool, pool.place, put
        self.order = order
        self.source, self.rows, self.columns, self.first = source, rows, columns, first
        self.third = "x" if first == "y" else "y"
        self.width = columns.size

    def ref(self, kind):
        spot = self.order
        if kind == 0:
            spot = spot % self.pool.kept
        if kind == 1:
            spot = spot % self.pool.landing
        return self.pool.refs[kind].at[spot]

    def cut(self, ref):
        return ref.at[(slice(None),) * (len(ref.shape) - 1) + (pl.ds(0, self.width),)]

    def share(self, core):
        every = slice(None)
        return self.source.at[every, every, every, every, core, self.rows, self.columns]

    def pick(self, which):
        mine = self.ref(0)
        return mine.at[:, :, which] if self.first == "y" else mine.at[:, :, :, which]

    def fetch(self):
        return pltpu.make_async_copy(
            self.share(self.place.core), self.cut(self.ref(0)), self.pool.sems[2].at[self.order]
        )

    def send(self, ref, target, spot, device):
        sent, landed = self.pool.sems[0].at[self.order, spot], self.pool.sems[1].at[self.order, spot]
        return remote(ref, self.cut(target), sent, landed, device)

    def to_mate(self):
        return self.send(self.share(1 - self.place.core), self.ref(1), 0, self.place.mate())

    def to_over(self):
        own = self.place.own(self.first)
        return self.send(
            self.cut(self.pick(1 - own)), self.ref(2), 1, self.place.across(self.first)
        )

    def to_near(self):
        place = self.place
        source = self.cut(self.ref(2).at[:, 1 - place.zl])
        return self.send(source, self.ref(3), 2, place.at(z=jnp.bitwise_xor(place.z, 1)))

    def to_cross(self):
        own = self.place.own(self.third)
        source = self.cut(self.ref(3).at[:, 1 - own])
        return self.send(source, self.ref(4), 3, self.place.across(self.third))

    def to_far(self):
        place = self.place
        source = self.cut(self.ref(4).at[1 - place.zh])
        return self.send(source, self.ref(5), 4, place.at(z=jnp.bitwise_xor(place.z, 2)))

    def view(self, ref):
        return self.cut(ref)

    def step(self, index):
        pool, place, order = self.pool, self.place, self.order
        if index == 0:
            if order >= pool.landing:
                pl.semaphore_wait(pool.free, 1)
            self.fetch().start()
            self.to_mate().start()
        elif index == 1:
            self.fetch().wait()
            self.to_mate().wait_recv()
            mine = self.cut(self.ref(0))
            mine[...] = mine[...] + self.cut(self.ref(1))[...]
            if order + pool.landing < pool.chunks:
                pl.semaphore_signal(
                    pool.free, inc=1, device_id=place.mate(), device_id_type=MESH_ID
                )
            self.to_over().start()
        elif index == 2:
            self.to_over().wait()
            over = self.cut(self.ref(2))
            over[...] = over[...] + self.cut(self.pick(place.own(self.first)))[...]
            self.to_near().start()
        elif index == 3:
            self.to_near().wait_recv()
            near = self.cut(self.ref(3))
            near[...] = near[...] + self.cut(self.ref(2).at[:, place.zl])[...]
            self.to_cross().start()
        elif index == 4:
            self.to_cross().wait_recv()
            cross = self.cut(self.ref(4))
            cross[...] = cross[...] + self.cut(self.ref(3).at[:, place.own(self.third)])[...]
            self.to_far().start()
        else:
            self.to_far().wait_recv()
            final = self.cut(self.ref(4).at[place.zh])[...].astype(F32)
            self.put(final + self.cut(self.ref(5))[...].astype(F32))
            self.to_mate().wait_send()
            self.to_near().wait_send()
            self.to_cross().wait_send()
            self.to_far().wait_send()


class Gains:
    def __init__(self, mine, slots, sent, landed, place):
        self.mine, self.slots, self.sent, self.landed, self.place = mine, slots, sent, landed, place

    def swaps(self, index):
        place = self.place
        if index == 0:
            partners = [(place.dp, jnp.bitwise_xor(place.seq, k)) for k in range(1, 4)]
        else:
            partners = [(jnp.bitwise_xor(place.dp, k), place.seq) for k in range(1, 8)]
        for spot, partner in enumerate(partners):
            spot += 3 * index
            yield spot, remote(
                self.mine.at[index], self.slots.at[spot], self.sent.at[spot], self.landed.at[spot],
                partner,
            )

    def step(self, index):
        if index > 0:
            value = self.mine[index - 1]
            for spot, swap in self.swaps(index - 1):
                swap.wait()
                value = value + self.slots[spot]
            self.mine[index] = value
        if index < 2:
            for _, swap in self.swaps(index):
                swap.start()


class Exchange:
    def __init__(self, state, total, near, far, sent, landed, place, reverse):
        self.state, self.total, self.near, self.far = state, total, near, far
        self.sent, self.landed, self.place, self.reverse = sent, landed, place, reverse
        self.half = state.shape[0] // 2

    def move(self, source, target, spot, device):
        return remote(source, target, self.sent.at[spot], self.landed.at[spot], device)

    def to_mate(self):
        pairs = zip((self.state, self.total), self.near)
        return [self.move(a, b, i, self.place.mate()) for i, (a, b) in enumerate(pairs)]

    def part(self, spot, core, device):
        part = pl.ds(core * self.half, self.half)
        return [
            self.move(ref.at[part], ref.at[part], spot + i, device) for i, ref in enumerate(self.far)
        ]

    def over(self):
        return self.part(2, self.place.core, self.place.across("x"))

    def share(self, core):
        return self.part(4, core, self.place.mate())

    def step(self, index):
        place, reverse = self.place, self.reverse
        giving = place.x == (1 if reverse else 0)
        taking = place.x == (0 if reverse else 1)
        second = place.core == (0 if reverse else 1)
        state, total = self.state, self.total
        (near_state, near_total), (far_state, far_total) = self.near, self.far
        if index == 0:
            for copy in self.to_mate():
                copy.start()
        elif index == 1:
            for copy in self.to_mate():
                copy.wait_recv()

            @pl.when(giving)
            def _():
                part = pl.ds(place.core * self.half, self.half)
                far_state[part] = state[part] + near_state[part]
                far_total[part] = total[part] + near_total[part]
                for copy in self.over():
                    copy.start()

        elif index == 2:

            @pl.when(taking)
            def _():
                for copy in self.over():
                    copy.wait_recv()
                for copy in self.share(place.core):
                    copy.start()

        else:

            @pl.when(taking)
            def _():
                for copy in self.share(1 - place.core):
                    copy.wait_recv()
                for copy in self.share(place.core):
                    copy.wait_send()

            for copy in self.to_mate():
                copy.wait_send()

            @pl.when(giving)
            def _():
                for copy in self.over():
                    copy.wait_send()

            @pl.when(jnp.logical_and(giving, second))
            def _():
                state[...] = near_state[...]
                total[...] = near_total[...]

            @pl.when(jnp.logical_and(giving, jnp.logical_not(second)))
            def _():
                state[...] = jnp.zeros_like(state)
                total[...] = jnp.zeros_like(total)

            @pl.when(jnp.logical_and(taking, second))
            def _():
                state[...] = far_state[...] + near_state[...]
                total[...] = far_total[...] + near_total[...]

            @pl.when(jnp.logical_and(taking, jnp.logical_not(second)))
            def _():
                state[...] = far_state[...]
                total[...] = far_total[...]


class Work:
    def __init__(self):
        self.kinds = ([], [], [], [])

    def pause(self, name):
        for code in PLAN.get(name, ()):
            self.kinds[code // 1000][code % 1000 // 10].step(code % 10)

    def between(self, prefix, count, halves=False):
        def hook(index, half=""):
            for spot in range(count):
                name = f"{prefix}{spot}{half}"
                if name in PLAN:

                    @pl.when(index == spot)
                    def _():
                        self.pause(name)

        return hook


PLAN = {
    's': (0, 10,),
    'qk': (20, 30,),
    'v': (40, 1,),
    'st1': (50,),
    'st2': (11,),
    'st3': (60,),
    'st4': (21,),
    'st5': (2,),
    'st6': (31,),
    'e0': (2000,),
    'a0': (41,),
    'a1': (12, 51,),
    'a2': (2001, 61,),
    'a3': (22,),
    'a6': (32,),
    'a7': (3,),
    'e0w': (13, 42, 2002, 23, 2003, 52,),
    'b2': (62,),
    'b3': (14,),
    'b4': (4, 43,),
    'b5': (33,),
    'b6': (70,),
    'b7': (15, 80,),
    'po': (5, 90,),
    'nm': (24, 100,),
    'p0': (53, 63, 110, 120, 44, 25, 130, 140, 71, 34, 150, 45, 91, 81, 160, 170, 111, 101, 35, 64, 131, 121, 141, 72, 54, 151, 92, 65, 161, 171, 55,),
    'm0': (82,),
    't0': (73,),
    'm1': (102,),
    'm2': (93, 112,),
    't2': (83,),
    'm3': (122, 74, 132, 103, 113, 142, 75, 152, 94, 84, 162, 133, 123, 95, 172, 85, 114, 153, 104, 143, 115, 105,),
    't3': (124, 134, 163, 173,),
    'm4': (1000, 1010, 1020, 1030,),
    't4': (125,),
    'm5': (135, 144, 154, 1001, 1040,),
    't5': (1011, 1021,),
    'm6': (164, 174, 1031,),
    't6': (145,),
    'm7': (155, 1041, 165, 175,),
    't7': (1002, 1012, 1050,),
    'm8': (1060,),
    't8': (1051,),
    'm9': (1003, 1022, 1061, 1070,),
    't9': (1032, 1080,),
    'm10': (1071,),
    't10': (1013,),
    'ft': (1023, 1042, 1052, 1081, 1090, 1100,),
    'dm': (1004,),
    'c0': (1091,),
    'c2': (1033, 1062, 1110,),
    'c3': (1101, 1014,),
    'c4': (1043, 1072, 1120,),
    'c6': (1005, 1024, 1111,),
    'e1': (2010,),
    'og': (2011, 1015, 1082, 1130,),
    'd0': (1025, 1034, 1044, 1063, 1092, 1140,),
    'd1': (1035, 1053, 1073, 1083, 1102, 1121, 1045, 1131, 1150,),
    'd2': (1064, 1084, 1112, 2012, 1093, 1160,),
    'd3': (2013, 1065, 1085, 1054, 1074, 1103, 1132, 1141, 1151,),
    'd4': (1055, 1104, 1113, 1094, 1122, 1161, 1170, 1180,),
    'd5': (1075, 1105, 1133, 1152, 1171, 1181, 1142, 1190, 1200,),
    'd6': (1095, 1114, 1123, 1191,),
    'd7': (1134, 1143, 1153, 1162, 1172, 1201, 1115, 1210,),
    'lq': (1220,),
    'f0': (1124, 1135, 1182, 1154, 1211, 1221, 1230,),
    'f2': (1163, 1192,),
    'f3': (1144, 1173, 1222, 1125, 1231,),
    'l1': (1183, 1240,),
    'f4': (1155, 1174, 1193, 1202, 1250,),
    'f5': (1145, 1184, 1223, 1241, 1212,),
    'f6': (1175, 1164, 1194, 1203, 1251,),
    'l2': (1185, 1224, 1232, 1260, 1270,),
    'f7': (1213, 1165,),
    'l3': (1195, 1242, 1261, 1225, 1271, 1280, 1290,),
    'dn': (1204, 1214, 1233, 1243, 1252, 1262, 1272, 1281, 1291,),
    'z': (1205, 1215, 1234, 1244, 3000, 1282, 1292, 1253, 3001, 1263, 1273, 1254, 1235, 1264, 1245, 1283, 1274, 1293, 3002, 1284, 1294, 1255, 1265, 1275, 1285, 1295,),
}


def normalize(value, gain):
    return value * lax.rsqrt(jnp.mean(value * value, axis=-1, keepdims=True) + EPS) * gain


GRID = (2, 2, 2, 2, 2)
PARTS = (4, 8, 11)
GATHER_PARTS = (4, 8, 11)
TURNED = ((0, 1),)
BAND = 128
TILE = 256


def shape(dims, kind):
    return jax.ShapeDtypeStruct(dims, kind)


def padded(columns):
    return -(-columns // TILE) * TILE


def bands(count, act, size=BAND):
    def step(index, carry):
        act(pl.ds(pl.multiple_of(index * size, size), size))
        return carry

    lax.fori_loop(0, count // size, step, 0)


def rms_back(value, gain, grad):
    scale = lax.rsqrt(jnp.mean(value * value, axis=-1, keepdims=True) + EPS)
    unit = value * scale
    inner = grad * gain
    back = scale * (inner - unit * jnp.mean(inner * unit, axis=-1, keepdims=True))
    return back, jnp.sum(grad * unit, axis=0, keepdims=True)


def front_phase(work, r):
    r.ready("tok")

    def norm(band):
        r.normed[band, :] = normalize(r.tok[band, :].astype(F32), r.gain_row[...]).astype(BF16)

    bands(r.count, norm)
    r.ready("wq", "wk", "wv")
    r.query[...] = dot(r.normed[...], r.wq[...]).astype(BF16)
    r.keys[...] = dot(r.normed[...], r.wk[...]).astype(BF16)
    work.pause("qk")

    def project(band):
        r.values[:, band] = dot(r.normed[...], r.wv[:, band]).astype(BF16)

    bands(r.heads * VD, project, TILE)
    work.pause("v")
    pairs = r.heads // 2
    tables = r.pick_a, r.pick_b, r.table
    state_body(r.keys, r.values, *tables, r.state, r.total, work.between("st", pairs))
    work.pause("e0")
    attend_inside(r.query, r.keys, r.values, r.middle, r.inverse, work.between("a", pairs))
    work.pause("e0w")
    attend_before(
        r.query, *tables, r.state, r.total, r.middle, r.inverse, r.mixed, work.between("b", pairs)
    )

    r.ready("wo")

    def project_out(band):
        r.middle[:, band] = r.tok[:, band].astype(F32) + dot(r.mixed[...], r.wo[:, band])

    bands(r.width, project_out, TILE)
    work.pause("po")

    def norm_again(band):
        r.low[band, :] = normalize(r.middle[band, :], r.gain2_row[...]).astype(BF16)

    bands(r.count, norm_again)
    work.pause("nm")


def feed_phase(work, r, tiles, made, low_t, og_t, acc_out, acc_back, in_sem, out_sem):
    steps = PARTS[-1]

    def columns(step):
        return pl.ds(pl.multiple_of(step * TILE, TILE), TILE)

    def load(step, slot):
        return [
            pltpu.make_async_copy(ref.at[:, columns(step)], tiles.at[slot, i], in_sem.at[slot, i])
            for i, ref in enumerate(r.wholes_flat)
        ]

    def save(step, slot):
        return [
            pltpu.make_async_copy(made.at[slot, i], ref.at[:, columns(step)], out_sem.at[slot, i])
            for i, ref in enumerate(r.grads_flat)
        ]

    r.ready("og")
    low_t[...] = r.low[...].T
    og_t[...] = r.og[...].T
    acc_out[...] = r.middle[...]
    acc_back[...] = jnp.zeros_like(acc_back)
    work.pause("p0")
    for copy in load(0, 0):
        copy.start()
    in_tile, after_tile = work.between("m", steps), work.between("t", steps)

    def step(index, carry):
        slot = index % 2
        for copy in load(index, slot):
            copy.wait()

        crossing = functools.reduce(jnp.logical_or, [index + 1 == edge for edge in GATHER_PARTS])

        @pl.when(jnp.logical_not(crossing))
        def _():
            for copy in load(index + 1, 1 - slot):
                copy.start()

        gate_w, up_w, down_w = (tiles.at[slot, i] for i in range(3))
        gate = dot(r.low[...], gate_w[...])
        upward = dot(r.low[...], up_w[...])
        d_hidden = dot(r.og[...], down_w[...])
        sig = 1.0 / (1.0 + jnp.exp(-gate))
        silu = gate * sig
        hidden = (silu * upward).astype(BF16)
        d_gate = (d_hidden * upward * (sig * (1.0 + gate * (1.0 - sig)))).astype(BF16)
        d_up = (d_hidden * silu).astype(BF16)
        acc_out[...] += dot_nt(hidden, down_w[...])

        @pl.when(index >= 1)
        def _():
            for copy in save(index - 1, 1 - slot):
                copy.wait()

        in_tile(index)

        @pl.when(jnp.logical_and(crossing, index + 1 < steps))
        def _():
            for copy in load(index + 1, 1 - slot):
                copy.start()

        acc_back[...] += dot_nt(d_gate, gate_w[...]) + dot_nt(d_up, up_w[...])
        made[slot, 0] = dot(low_t[...], d_gate).astype(BF16)
        made[slot, 1] = dot(low_t[...], d_up).astype(BF16)
        made[slot, 2] = dot(og_t[...], hidden).astype(BF16)
        for copy in save(index, slot):
            copy.start()
        after_tile(index)
        return carry

    lax.fori_loop(0, steps, step, 0)

    def store_out(band):
        r.out[band, :] = acc_out[band, :].astype(BF16)

    bands(r.count, store_out)
    r.ends[0]().start()
    r.gain_sum[...] = jnp.zeros(r.gain_sum.shape, F32)

    def middle_back(band):
        value, part = rms_back(r.middle[band, :], r.gain2_row[...], acc_back[band, :])
        r.gain_sum[1:2, :] += part
        value = r.og[band, :].astype(F32) + value
        r.middle[band, :] = value
        r.low[band, :] = value.astype(BF16)

    bands(r.count, middle_back)
    for copy in save(steps - 1, (steps - 1) % 2):
        copy.wait()
    work.pause("ft")

    def mixed_back(band):
        r.d_mixed[:, band] = dot_nt(r.low[...], r.wo[band, :]).astype(BF16)

    bands(r.heads * VD, mixed_back, TILE)
    work.pause("dm")


def back_phase(work, r, d_query, d_keys, d_values, q_sum, k_sum, turned, v_part):
    heads_wide, narrow = r.heads * VD, r.heads * KD
    pairs = r.heads // 2
    tables = r.pick_a, r.pick_b, r.table
    back_state_body(
        r.query, r.mixed, r.inverse, r.d_mixed, *tables, r.d_state, r.d_total,
        work.between("c", pairs),
    )
    work.pause("e1")
    turned[...] = r.mixed[...].T

    def out_grads(band):
        r.out_g[:, band] = dot(turned[...], r.low[:, band]).astype(BF16)

    bands(r.width, out_grads, TILE)
    work.pause("og")
    turned[...] = r.normed[...].T
    attend_back_inside(
        r.query, r.keys, r.values, r.mixed, r.inverse, r.d_mixed, *tables, r.state, r.total,
        q_sum, k_sum, v_part, work.between("d", pairs),
    )
    work.pause("e1w")
    grid = GRID + (r.rows,)
    late_refs = dict(q=(d_query, q_sum), k=(d_keys, k_sum), v=(d_values, None))

    def late(index):
        spot = sum(high - low for group in r.late_groups[:index] for _, low, high in group)
        for name, low, high in r.late_groups[index]:
            ref, wide = late_refs[name]
            if wide is not None:
                ref[:, low:high] = wide[:, low:high].astype(BF16)
            for start in range(low, high, TILE):
                stop = min(start + TILE, high)
                value = dot(turned[...], ref[:, start:stop]).astype(BF16)
                size = stop - start
                r.late_g[:, :, :, :, :, :, spot : spot + size] = value.reshape(grid + (size,))
                spot += size

    late(0)
    work.pause("lq")

    def ended(pair):
        for spot, index in ((pairs // 2 - 1, 1), (pairs - 2, 2)):

            @pl.when(pair == spot)
            def _(index=index):
                late(index)
                work.pause(f"l{index}")

    attend_back_after(
        r.keys, r.values, *tables, r.d_state, r.d_total, k_sum, v_part, d_values,
        work.between("f", pairs), ended,
    )
    late(3)
    work.pause("l3")

    def back_norm(band):
        v_part[:, band] = (
            dot_nt(d_query[...], r.wq[band, :])
            + dot_nt(d_keys[...], r.wk[band, :])
            + dot_nt(d_values[...], r.wv[band, :])
        )

    bands(r.width, back_norm, TILE)
    work.pause("dn")

    def tokens_back(band):
        value, part = rms_back(r.tok[band, :].astype(F32), r.gain_row[...], v_part[band, :])
        r.gain_sum[0:1, :] += part
        r.middle[band, :] = r.middle[band, :] + value

    bands(r.count, tokens_back)
    quarter = r.width // 4
    for which in range(2):
        for part in range(4):
            spot = 4 * which + part
            r.gain_mine[0, spot : spot + 1, :] = r.gain_sum[
                which : which + 1, part * quarter : (part + 1) * quarter
            ]


class Refs:
    pass


def layer(tokens, gain, wq, wk, wv, wo, gain2, tables, shards3, out_grad):
    count, width = tokens.shape
    heads = wq.shape[1] // KD
    rows, columns = shards3[0].shape
    full = padded(columns)
    tall = rows // 2
    heads_wide, narrow = heads * VD, heads * KD
    last = heads_wide - 2 * VD
    late_groups = (
        (("q", 0, narrow),),
        (("v", 0, heads_wide // 2), ("k", 0, narrow // 2)),
        (("v", heads_wide // 2, last),),
        (("v", last, heads_wide), ("k", narrow // 2, narrow)),
    )
    late_sizes = [sum(high - low for _, low, high in group) for group in late_groups]
    edges = [0] + [part * TILE for part in PARTS]
    widest = max(*late_sizes, width // 2, *[high - low for low, high in zip(edges, edges[1:])])
    chunks = 6 * len(PARTS) + 4 + 2 * len(late_groups)
    gather_edges = [0] + [part * TILE for part in GATHER_PARTS]
    gathers = 6 * len(GATHER_PARTS)
    states = ((heads, VD, FEATS), BF16), ((heads, 1, FEATS), F32)
    sem = pltpu.SemaphoreType.DMA

    loads = dict(
        shard0=shards3[0], shard1=shards3[1], shard2=shards3[2], tok=tokens, wq=wq, wk=wk, wv=wv,
        og=out_grad, wo=wo,
    )
    inputs = {name + "_in": value for name, value in loads.items()}
    inputs |= dict(
        gain=gain, gain2=gain2, pick_a=tables[0], pick_b=tables[1], table=tables[2]
    )
    free_outs = dict(
        whole0=shape((width, full), BF16), whole1=shape((width, full), BF16),
        whole2=shape((width, full), BF16), grad0=shape((width, full), BF16),
        grad1=shape((width, full), BF16), grad2=shape((width, full), BF16),
        out_end=shape((count, width), BF16), tok_end=shape((count, width), F32),
    )
    outs = dict(
        g0=shape((rows, columns), F32), g1=shape((rows, columns), F32),
        g2=shape((rows, columns), F32), g_out=shape((rows, width), F32),
        g_value=shape((rows, heads_wide), F32), g_query=shape((rows, narrow), F32),
        g_keys=shape((rows, narrow), F32), g_gain=shape((8, width // 4), F32),
    )
    scratch = {name: pltpu.VMEM(value.shape, value.dtype) for name, value in loads.items()}
    scratch |= dict(
        out=pltpu.VMEM((count, width), BF16),
        middle=pltpu.VMEM((count, width), F32),
        load_sem=sem((len(loads),)), end_sem=sem((2,)),
        gain_row=pltpu.VMEM((1, width), F32), gain2_row=pltpu.VMEM((1, width), F32),
        normed=pltpu.VMEM((count, width), BF16),
        query=pltpu.VMEM((count, narrow), BF16),
        keys=pltpu.VMEM((count, narrow), BF16),
        values=pltpu.VMEM((count, heads_wide), BF16),
        mixed=pltpu.VMEM((count, heads_wide), BF16),
        inverse=pltpu.VMEM((count, heads_wide), F32),
        state=pltpu.VMEM(*states[0]), total=pltpu.VMEM(*states[1]),
        d_state=pltpu.VMEM(*states[0]), d_total=pltpu.VMEM(*states[1]),
        near_state=pltpu.VMEM(*states[0]), near_total=pltpu.VMEM(*states[1]),
        far_state=pltpu.VMEM(*states[0]), far_total=pltpu.VMEM(*states[1]),
        ex_sent=sem((6,)), ex_landed=sem((6,)),
        low=pltpu.VMEM((count, width), BF16),
        d_mixed=pltpu.VMEM((count, heads_wide), BF16),
        out_g=pltpu.VMEM((width, width), BF16),
        late_g=pltpu.VMEM(GRID + (rows, sum(late_sizes)), BF16),
        wide=pltpu.VMEM((3, rows, full), BF16),
        ag_sent=sem((gathers, 5)), ag_landed=sem((gathers, 5)), ag_local=sem((gathers,)),
        gain_sum=pltpu.VMEM((8, width), F32),
        gain_mine=pltpu.VMEM((3, 8, width // 4), F32),
        gain_slots=pltpu.VMEM((10, 8, width // 4), F32),
        gain_sent=sem((10,)), gain_landed=sem((10,)),
        p0=pltpu.VMEM((5, 2, 2, 2, 2, tall, widest), BF16),
        p1=pltpu.VMEM((4, 2, 2, 2, 2, tall, widest), BF16),
        p2=pltpu.VMEM((chunks, 2, 2, 2, tall, widest), BF16),
        p3=pltpu.VMEM((chunks, 2, 2, tall, widest), BF16),
        p4=pltpu.VMEM((chunks, 2, tall, widest), BF16),
        p5=pltpu.VMEM((chunks, tall, widest), BF16),
        rs_sent=sem((chunks, 5)), rs_landed=sem((chunks, 5)), rs_local=sem((chunks,)),
        credit=pltpu.SemaphoreType.REGULAR,
    )
    names = list(inputs) + list(free_outs) + list(outs) + list(scratch)

    def body(*refs):
        r = Refs()
        for name, ref in zip(names, refs):
            setattr(r, name, ref)
        r.count, r.width, r.heads, r.rows = count, width, heads, rows
        r.late_groups = late_groups
        r.place = place = Place()
        r.wholes_flat = [r.whole0, r.whole1, r.whole2]
        r.grads_flat = [r.grad0, r.grad1, r.grad2]
        grid = GRID + (rows,)
        wholes = [ref.reshape(grid + (full,)) for ref in r.wholes_flat]
        grads = [ref.reshape(grid + (full,)) for ref in r.grads_flat]
        def load(name):
            spot = list(loads).index(name)
            source = getattr(r, name + "_in")
            return pltpu.make_async_copy(source, getattr(r, name), r.load_sem.at[spot])

        r.ready = lambda *wanted: [load(name).wait() for name in wanted]
        r.ends = [
            lambda: pltpu.make_async_copy(r.out, r.out_end, r.end_sem.at[0]),
            lambda: pltpu.make_async_copy(r.middle, r.tok_end, r.end_sem.at[1]),
        ]
        for name in loads:
            load(name).start()
        enter(place)
        work = Work()
        r.gain_row[...] = r.gain[...].astype(F32).reshape(1, width)
        r.gain2_row[...] = r.gain2[...].astype(F32).reshape(1, width)
        r.ready("shard0", "shard1", "shard2")
        gather_list, sum_list, exchange_list, gain_list = work.kinds
        for spot, shard in enumerate((r.shard0, r.shard1, r.shard2)):
            r.wide[spot, :, columns:full] = jnp.zeros((rows, full - columns), BF16)
            r.wide[spot, :, 0:columns] = shard[...]
        for part, (low, high) in enumerate(zip(gather_edges, gather_edges[1:])):
            for weight in range(3):
                for kind, first in enumerate("yy" if (part, weight) in TURNED else "xy"):
                    order = len(gather_list)
                    gather_list.append(
                        Gather(
                            r.wide.at[weight], wholes[weight], pl.ds(kind * tall, tall),
                            pl.ds(low, high - low), first,
                            (r.ag_sent.at[order], r.ag_landed.at[order], r.ag_local.at[order]), place,
                        )
                    )
        pool = Pool(
            [r.p0, r.p1, r.p2, r.p3, r.p4, r.p5], (r.rs_sent, r.rs_landed, r.rs_local), r.credit,
            place, chunks,
        )

        def sums(source, low, high, target, firsts="xy"):
            for kind, first in enumerate(firsts):

                def put(value, kind=kind):
                    target(slice(kind * tall, (kind + 1) * tall), value)

                chunk_rows, chunk_columns = pl.ds(kind * tall, tall), pl.ds(low, high - low)
                sum_list.append(
                    Chunk(pool, len(sum_list), source, chunk_rows, chunk_columns, first, put)
                )

        def into(ref, low, high):
            def put(where, value):
                ref[where, low:high] = value[:, 0 : high - low]

            return put

        for low, high in zip(edges, edges[1:]):
            for source, target in zip(grads, (r.g0, r.g1, r.g2)):
                sums(source, low, high, into(target, low, min(high, columns)))
        half = width // 2
        for low in (0, half):
            target = into(r.g_out, low, low + half)
            sums(r.out_g.reshape(grid + (width,)), low, low + half, target, "yy")
        late_ends = dict(q=r.g_query, k=r.g_keys, v=r.g_value)
        spot = 0
        for group, size in zip(late_groups, late_sizes):

            def put_late(where, value, group=group):
                at = 0
                for name, low, high in group:
                    late_ends[name][where, low:high] = value[:, at : at + high - low]
                    at += high - low

            sums(r.late_g, spot, spot + size, put_late)
            spot += size
        for state, total, reverse in ((r.state, r.total, False), (r.d_state, r.d_total, True)):
            exchange_list.append(
                Exchange(
                    state, total, (r.near_state, r.near_total), (r.far_state, r.far_total),
                    r.ex_sent, r.ex_landed, place, reverse,
                )
            )
        gain_list.append(Gains(r.gain_mine, r.gain_slots, r.gain_sent, r.gain_landed, place))
        work.pause("s")
        front_phase(work, r)
        pl.run_scoped(
            lambda *buffers: feed_phase(work, r, *buffers),
            pltpu.VMEM((2, 3, width, TILE), BF16),
            pltpu.VMEM((2, 3, width, TILE), BF16),
            pltpu.VMEM((width, count), BF16),
            pltpu.VMEM((width, count), BF16),
            pltpu.VMEM((count, width), F32),
            pltpu.VMEM((count, width), F32),
            sem((2, 3)),
            sem((2, 3)),
        )
        pl.run_scoped(
            lambda *buffers: back_phase(work, r, *buffers),
            pltpu.VMEM((count, narrow), BF16),
            pltpu.VMEM((count, narrow), BF16),
            pltpu.VMEM((count, heads_wide), BF16),
            pltpu.VMEM((count, narrow), F32),
            pltpu.VMEM((count, narrow), F32),
            pltpu.VMEM((width, count), BF16),
            pltpu.VMEM((count, width), F32),
        )
        r.ends[1]().start()
        work.pause("z")
        r.ends[0]().wait()
        r.ends[1]().wait()
        r.g_gain[...] = r.gain_mine[2]

    vmem = pl.BlockSpec(memory_space=pltpu.VMEM)
    free = pl.BlockSpec(memory_space=pl.ANY)
    results = pl.pallas_call(
        body,
        out_shape=list(free_outs.values()) + list(outs.values()),
        in_specs=[free] * len(loads) + [vmem] * 5,
        out_specs=[free] * len(free_outs) + [vmem] * len(outs),
        scratch_shapes=list(scratch.values()),
        compiler_params=pltpu.CompilerParams(
            collective_id=0, has_side_effects=True, vmem_limit_bytes=VMEM_LIMIT
        ),
    )(*inputs.values())
    return results[6:]


def hand_over(results, gains):
    quarter = gains.shape[1]
    share = quarter // 8
    count = len(results)

    def body(*refs):
        sources, gain, targets = refs[:count], refs[count], refs[count + 1 : 2 * count + 1]
        first, second, sems = refs[2 * count + 1 :]
        copies = [
            pltpu.make_async_copy(a, b, sems.at[i]) for i, (a, b) in enumerate(zip(sources, targets))
        ]
        for copy in copies:
            copy.start()
        own = lax.axis_index("dp") * 4 + lax.axis_index("seq")
        turned = pltpu.roll(gain[...], lax.rem(quarter - own % 8 * share, quarter), 1)[:, 0:share]
        row = lax.broadcasted_iota(jnp.int32, turned.shape, 0)
        for ref, start in ((first, 0), (second, 4)):
            ref[...] = jnp.sum(only(row == start + own // 8, turned), axis=0, keepdims=True)
        for copy in copies:
            copy.wait()

    vmem = pl.BlockSpec(memory_space=pltpu.VMEM)
    free = pl.BlockSpec(memory_space=pl.ANY)
    return pl.pallas_call(
        body,
        out_shape=[shape(value.shape, value.dtype) for value in results] + [shape((1, share), F32)] * 2,
        in_specs=[vmem] * (count + 1),
        out_specs=[free] * count + [vmem] * 2,
        scratch_shapes=[pltpu.SemaphoreType.DMA((count,))],
    )(*results, gains)


def general(
    tokens, attn_gain, w_query, w_key, w_value, w_output, mlp_gain, w_gate, w_up, w_down, out_grad
):
    count, width = tokens.shape
    heads = w_query.shape[1] // KD
    all_values = heads * VD
    tables = feature_tables()
    inputs = tokens.astype(F32)
    gain = attn_gain.astype(F32).reshape(1, width)
    gate_full, up_full, down_full = (
        lax.all_gather(w, ("dp", "seq"), axis=0, tiled=True) for w in (w_gate, w_up, w_down)
    )
    normed, query, keys, values = call(
        project_body,
        [
            ((count, width), BF16),
            ((count, heads * KD), BF16),
            ((count, heads * KD), BF16),
            ((count, all_values), BF16),
        ],
        tokens,
        gain,
        w_query,
        w_key,
        w_value,
    )
    state_shapes = [((heads, VD, FEATS), BF16), ((heads, 1, FEATS), F32)]
    state, total = call(state_body, state_shapes, keys, values, *tables)
    state = before(lax.all_gather(state, "seq"), "seq").astype(BF16)
    total = before(lax.all_gather(total, "seq"), "seq")
    mixed, inverse = call(
        attend_body,
        [((count, all_values), BF16), ((count, all_values), F32)],
        query,
        keys,
        values,
        *tables,
        state,
        total,
    )
    middle = inputs + dot(mixed, w_output)
    normed_mlp, second_back = jax.vjp(rms_norm, middle, mlp_gain.astype(F32))
    mlp_low = normed_mlp.astype(BF16)
    gate = dot(mlp_low, gate_full)
    upward = dot(mlp_low, up_full)
    hidden_val, gated_back = jax.vjp(gated, gate, upward)
    hidden = hidden_val.astype(BF16)
    layer_out = (middle + dot_nt(hidden, down_full)).astype(BF16)
    d_hidden = dot(out_grad, down_full)
    down_grad = dot_tn(out_grad, hidden).astype(BF16)
    d_gate_f, d_up_f = gated_back(d_hidden)
    d_gate = d_gate_f.astype(BF16)
    d_up = d_up_f.astype(BF16)
    gate_grad = dot_tn(mlp_low, d_gate).astype(BF16)
    up_grad = dot_tn(mlp_low, d_up).astype(BF16)
    d_normed_mlp = dot_nt(d_gate, gate_full) + dot_nt(d_up, up_full)
    d_middle_norm, mlp_gain_part = second_back(d_normed_mlp)
    d_middle = out_grad.astype(F32) + d_middle_norm
    d_branch = d_middle.astype(BF16)
    output_grad = dot_tn(mixed, d_branch).astype(BF16)
    d_mixed = dot_nt(d_branch, w_output).astype(BF16)
    d_state, d_total = call(
        back_state_body, state_shapes, query, mixed, inverse, d_mixed, *tables
    )
    d_state = before(lax.all_gather(d_state, "seq"), "seq", True).astype(BF16)
    d_total = before(lax.all_gather(d_total, "seq"), "seq", True)
    d_query, d_keys, d_values = call(
        attend_back_body,
        [
            ((count, heads * KD), BF16),
            ((count, heads * KD), BF16),
            ((count, all_values), BF16),
        ],
        query,
        keys,
        values,
        mixed,
        inverse,
        d_mixed,
        *tables,
        state,
        total,
        d_state,
        d_total,
        scratch=[
            pltpu.VMEM((count, heads * KD), F32),
            pltpu.VMEM((count, heads * KD), F32),
            pltpu.VMEM((count, LANES), F32),
        ],
    )
    d_normed = dot_nt(d_query, w_query) + dot_nt(d_keys, w_key) + dot_nt(d_values, w_value)
    query_grad = dot_tn(normed, d_query).astype(BF16)
    key_grad = dot_tn(normed, d_keys).astype(BF16)
    value_grad = dot_tn(normed, d_values).astype(BF16)
    _, first_back = jax.vjp(rms_norm, inputs, attn_gain.astype(F32))
    d_inputs_norm, attn_gain_part = first_back(d_normed)
    tokens_grad = d_middle + d_inputs_norm
    parts = [query_grad, key_grad, value_grad, output_grad, gate_grad, up_grad, down_grad]
    joined = lax.psum_scatter(
        jnp.concatenate(parts, axis=1), ("dp", "seq"), scatter_dimension=0, tiled=True
    ).astype(F32)
    edges = np.cumsum([part.shape[1] for part in parts])[:-1]
    query_grad, key_grad, value_grad, output_grad, gate_grad, up_grad, down_grad = jnp.split(
        joined, edges, axis=1
    )
    gains = lax.psum_scatter(
        jnp.stack([attn_gain_part, mlp_gain_part], axis=1),
        ("dp", "seq"),
        scatter_dimension=0,
        tiled=True,
    )
    return (
        layer_out,
        tokens_grad,
        gains[:, 0],
        query_grad,
        key_grad,
        value_grad,
        output_grad,
        gains[:, 1],
        gate_grad,
        up_grad,
        down_grad,
    )


def shards(
    tokens, attn_gain, w_query, w_key, w_value, w_output, mlp_gain, w_gate, w_up, w_down, out_grad
):
    args = (
        tokens, attn_gain, w_query, w_key, w_value, w_output, mlp_gain, w_gate, w_up, w_down, out_grad
    )
    if (lax.axis_size("dp"), lax.axis_size("seq")) != (8, 4):
        return general(*args)
    *results, gains = layer(
        tokens, attn_gain, w_query, w_key, w_value, w_output, mlp_gain, feature_tables(),
        (w_gate, w_up, w_down), out_grad,
    )
    *results, gain_grad, gain2_grad = hand_over(results, gains)
    layer_out, tok_grad, gate_grad, up_grad, down_grad, output_grad, value_grad, query_grad, key_grad = results
    return (
        layer_out,
        tok_grad,
        gain_grad.reshape(-1),
        query_grad,
        key_grad,
        value_grad,
        output_grad,
        gain2_grad.reshape(-1),
        gate_grad,
        up_grad,
        down_grad,
    )


def solution(mesh):
    rows = P(("dp", "seq"), None)
    in_specs = (rows, P(), P(), P(), P(), P(), P(), rows, rows, rows, rows)
    out_specs = (
        rows,
        rows,
        P(("dp", "seq")),
        rows,
        rows,
        rows,
        rows,
        P(("dp", "seq")),
        rows,
        rows,
        rows,
    )
    return jax.shard_map(
        shards, mesh=mesh, in_specs=in_specs, out_specs=out_specs, check_vma=False
    )
```
